128 devices in a mesh: seq: 16 (over z_hi, x, core), tensor: 2 (over z_lo), dp: 4 (over y).
Axes of the slice: x: 4, y: 4, z: 4 (z_hi: 2, z_lo: 2; z = z_hi * 2 + z_lo), core: 2. Of those that a mesh axis runs over, the one named last changes fastest.
Arguments:
- section_input: bfloat16 [4, 4096, 1280], P('dp', 'seq'), may hold values from -6 to 6
- conv_weight: bfloat16 [1280, 5, 1536], P('seq', None, 'tensor'), may hold values from -0.078125 to 0.078125
- head_weight: bfloat16 [1536, 3, 768], P('seq', None, 'tensor'), as said below
- output_weight: bfloat16 [1536, 768], P('seq', 'tensor'), may hold values from -0.21875 to 0.21875
- cotangent: bfloat16 [4, 2048, 1536], P('dp', 'seq', 'tensor'), may hold values from -6 to 6
Outputs:
- block_out: bfloat16 [4, 2048, 1536], P('dp', 'seq', 'tensor')
- conv_grad: float32 [1280, 5, 1536], P(('seq', 'dp'), None, 'tensor')
- head_grad: float32 [1536, 3, 768], P(('seq', 'dp'), None, 'tensor')
- output_grad: float32 [1536, 768], P(('seq', 'dp'), 'tensor')
The draws below stay inside these ranges and needn't reach their ends.
Inputs may be any that keep to these rules, and one draw needn't show every extreme that they name: `head_weight`: finite projection weights whose deviation lies between about 1.7 and some 25 times 1536 to the minus one half.
All inputs are finite; a program needn't handle non-finite values.
Results may differ from the reference program's by a relative error of at most 0.023.
Values may be sent and summed in bfloat16 or wider, within the bound.
A program may use at most 128 MiB of HBM per device.

```python
import jax
import jax.numpy as jnp
from jax import lax

IN_WIDTH = 1280
WIDTH = 1536
HEADS = 4
HEAD_DIM = 192
KERNEL = 5
INNER = 768
SEQS = 4
BINS = 2048
POSITIONS = 4096


def draw_head_weight(key, part):
    first = jax.random.fold_in(key, 0)
    base = jnp.clip(jax.random.normal(first, (WIDTH, 3, INNER), jnp.float32), -6.0, 6.0) * (1.7 / WIDTH ** 0.5)
    return base.astype(jnp.bfloat16)


def strengthened(result, rng, source, target, blocks, factor):
    owner, partner = [(jnp.arange(result.shape[position]) // (result.shape[position] // blocks)).reshape([-1 if axis == position else 1 for axis in range(result.ndim)]) for position in (source, target)]
    chosen = jax.random.permutation(rng, blocks)[partner]
    strong = (owner == chosen) | (owner == (partner + blocks // 2) % blocks)
    return jnp.where(strong, factor * result, result)


def steps_of(stream_key, extent, cuts, least, high):
    loudness = 1.0
    for axis_at, parts in cuts:
        heights = jax.random.uniform(jax.random.fold_in(jax.random.fold_in(stream_key, 6), axis_at), (parts,), jnp.float32, least / len(cuts), high / len(cuts))
        loudness = loudness * jnp.repeat(jnp.exp(heights), extent[axis_at] // parts).reshape((-1,) + (1,) * (len(extent) - 1 - axis_at))
    return loudness


def centred(own_key, extent, deviation, reach, cuts=(), dtype=jnp.bfloat16):
    result = jax.random.normal(own_key, extent, jnp.float32) * deviation
    if len(cuts) > 0:
        result = steps_of(own_key, extent, cuts, -0.22, 0.18) * result
    return jnp.clip(result, min=-reach, max=reach).astype(dtype)


def gaussian_with(own_key, shape, deviation, bound, shards, heavy, held_as=jnp.bfloat16):
    array = deviation * jax.random.normal(own_key, shape, jnp.float32)
    if shards:
        array = array * steps_of(own_key, shape, shards, -0.22, 0.18)
    return jnp.clip(strengthened(array, jax.random.fold_in(own_key, 3), *heavy), -bound, bound).astype(held_as)


def setup_inputs(seed: int = 0) -> dict:
    key_list = jax.random.split(jax.random.key(seed), 6)
    return {
        "section_input": centred(key_list[0], (SEQS, POSITIONS, IN_WIDTH), 1.0, 6.0, ((0, 4), (1, 16))),
        "conv_weight": centred(key_list[1], (IN_WIDTH, KERNEL, WIDTH), (IN_WIDTH * KERNEL) ** -0.5, 0.078125, ((0, 16), (2, 2))),
        "head_weight": draw_head_weight(jax.random.fold_in(key_list[5], 71), 0),
        "output_weight": centred(key_list[3], (WIDTH, INNER), INNER ** -0.5, 0.21875, ((0, 16), (1, 2))),
        "cotangent": gaussian_with(key_list[4], (SEQS, BINS, WIDTH), 1.0, 6.0, ((0, 4), (1, 16), (2, 2)), (1, 2, 16, 2.0)),
    }


def attend_one(query_rows, key_rows, value_rows, grad_rows):
    score_scale = HEAD_DIM ** (-0.5)
    scores = jnp.einsum('qhd,khd->hqk', query_rows.astype(jnp.float32), key_rows.astype(jnp.float32)) * score_scale
    weights = jax.nn.softmax(scores, axis=-1)
    rounded = weights.astype(jnp.bfloat16)
    attended = jnp.einsum('hqk,khd->qhd', rounded.astype(jnp.float32), value_rows.astype(jnp.float32)).astype(jnp.bfloat16)
    grad_prob = jnp.einsum('qhd,khd->hqk', grad_rows.astype(jnp.float32), value_rows.astype(jnp.float32))
    centre = lax.optimization_barrier(jnp.sum(weights * grad_prob, axis=-1, keepdims=True))
    grad_score = (weights * (grad_prob - centre)).astype(jnp.bfloat16)
    grad_query = (jnp.einsum('hqk,khd->qhd', grad_score.astype(jnp.float32), key_rows.astype(jnp.float32)) * score_scale).astype(jnp.bfloat16)
    grad_key = (jnp.einsum('hqk,qhd->khd', grad_score.astype(jnp.float32), query_rows.astype(jnp.float32)) * score_scale).astype(jnp.bfloat16)
    grad_value = jnp.einsum('hqk,qhd->khd', rounded.astype(jnp.float32), grad_rows.astype(jnp.float32)).astype(jnp.bfloat16)
    return (attended, grad_query, grad_key, grad_value)

def reference(section_input, conv_weight, head_weight, output_weight, cotangent):
    activity = jax.nn.gelu(section_input.astype(jnp.float32), approximate=True).astype(jnp.bfloat16)
    margin = KERNEL // 2
    padded = jnp.pad(activity, ((0, 0), (margin, margin), (0, 0)))
    length = activity.shape[1]
    conv_sum = jnp.zeros((activity.shape[0], length, WIDTH), jnp.float32)
    for offset in range(KERNEL):
        conv_sum = conv_sum + jnp.einsum('sti,io->sto', padded[:, offset:offset + length].astype(jnp.float32), conv_weight[:, offset].astype(jnp.float32))
    section = ((conv_sum[:, 0::2] + conv_sum[:, 1::2]) * 0.5).astype(jnp.bfloat16)
    section_float = section.astype(jnp.float32)
    inverse = lax.rsqrt(lax.optimization_barrier(jnp.mean(section_float * section_float, axis=-1, keepdims=True)) + 1e-06)
    normed = (section_float * inverse).astype(jnp.bfloat16)
    projected = jnp.einsum('sbc,cje->sbje', normed.astype(jnp.float32), head_weight.astype(jnp.float32)).astype(jnp.bfloat16)
    head_shape = (SEQS, BINS, HEADS, HEAD_DIM)
    query_rows = projected[:, :, 0].reshape(head_shape)
    key_rows = projected[:, :, 1].reshape(head_shape)
    value_rows = projected[:, :, 2].reshape(head_shape)
    grad_att = jnp.einsum('sbc,ce->sbe', cotangent.astype(jnp.float32), output_weight.astype(jnp.float32)).astype(jnp.bfloat16)
    attended, grad_query, grad_key, grad_value = lax.map(lambda stacked: attend_one(*stacked), (query_rows, key_rows, value_rows, grad_att.reshape(head_shape)))
    attended = attended.reshape(SEQS, BINS, INNER)
    block_out = (section_float + jnp.einsum('sbe,ce->sbc', attended.astype(jnp.float32), output_weight.astype(jnp.float32))).astype(jnp.bfloat16)
    grad_proj = jnp.stack([grad_query.reshape(SEQS, BINS, INNER), grad_key.reshape(SEQS, BINS, INNER), grad_value.reshape(SEQS, BINS, INNER)], axis=2)
    grad_normed = jnp.einsum('sbje,cje->sbc', grad_proj.astype(jnp.float32), head_weight.astype(jnp.float32))
    spread = lax.optimization_barrier(jnp.mean(grad_normed * section_float, axis=-1, keepdims=True))
    grad_section = cotangent.astype(jnp.float32) + inverse * grad_normed - inverse ** 3 * section_float * spread
    grad_pool = (0.5 * grad_section).astype(jnp.bfloat16)
    grad_conv = jnp.repeat(grad_pool, 2, axis=1).astype(jnp.float32)
    conv_grad = jnp.stack([jnp.einsum('sti,sto->io', padded[:, offset:offset + length].astype(jnp.float32), grad_conv) for offset in range(KERNEL)], axis=1)
    head_grad = jnp.einsum('sbc,sbje->cje', normed.astype(jnp.float32), grad_proj.astype(jnp.float32))
    output_grad = jnp.einsum('sbc,sbe->ce', cotangent.astype(jnp.float32), attended.astype(jnp.float32))
    return (block_out, conv_grad, head_grad, output_grad)
```

```python
import functools

import jax
import jax.numpy as jnp
from jax import lax
from jax.experimental import pallas as pl
from jax.experimental.pallas import tpu as pltpu
from jax.sharding import PartitionSpec as P

HEAD_DIM = 192
EPSILON = 1e-06
MESH = pl.DeviceIdType.MESH
BF16 = jnp.bfloat16
F32 = jnp.float32


def place():
    seq = lax.axis_index("seq")
    return seq, lax.div(seq, 2), lax.rem(seq, 2), lax.axis_index("tensor"), lax.axis_index("dp")


def device(seq, tensor, dp):
    return {"seq": seq, "tensor": tensor, "dp": dp}


def remote(src, dst, send, recv, target):
    return pltpu.make_async_remote_copy(
        src_ref=src, dst_ref=dst, send_sem=send, recv_sem=recv, device_id=target, device_id_type=MESH
    )


def greet(targets):
    barrier = pltpu.get_barrier_semaphore()
    for condition, target in targets:
        if condition is None:
            pl.semaphore_signal(barrier, inc=1, device_id=target, device_id_type=MESH)
        else:

            @pl.when(condition)
            def _(target=target):
                pl.semaphore_signal(barrier, inc=1, device_id=target, device_id_type=MESH)

    return barrier


def under(condition, action):
    if condition is None:
        action()
    else:

        @pl.when(condition)
        def _():
            action()


def communicate(kernel, collective, outputs, semaphores, *operands):
    anywhere = pl.BlockSpec(memory_space=pl.ANY)
    return pl.pallas_call(
        kernel,
        out_shape=outputs,
        in_specs=[anywhere] * len(operands),
        out_specs=tuple([anywhere] * len(outputs)),
        scratch_shapes=[pltpu.SemaphoreType.DMA((count,)) for count in semaphores],
        compiler_params=pltpu.CompilerParams(collective_id=collective, has_side_effects=True),
    )(*operands)


def half_sends(items, s, j, c, t, d, src_of, dst, send, recv, local):
    zh, m = lax.div(s, 8), lax.rem(s, 8)
    for k in range(8):
        chip = lax.rem(j + k, 8)
        target = 2 * chip + zh
        src = src_of(chip)
        copy = remote(src, dst(m), send.at[k], recv.at[m], device(target, t, d))
        if k == 0:
            items.append((c != zh, copy.start, copy.wait_send))
            own = pltpu.make_async_copy(src, dst(m), local)
            items.append((c == zh, own.start, own.wait))
        else:
            items.append((None, copy.start, copy.wait_send))
    waits = []
    for n in range(8):
        copy = remote(dst(n), dst(n), send.at[0], recv.at[n], device(s, t, d))
        waits.append((8 * c + n != s, copy.wait_recv))
    return waits


def start_kernel(at_ref, cw_ref, wp_ref, cot_ref, xt_ref, halo_ref, cwf_ref, wq_ref, cots_ref,
                 at_send, at_recv, halo_send, halo_recv, w_send, w_recv, q_send, q_recv, c_send, c_recv, local):
    s, j, c, t, d = place()
    zh = lax.div(s, 8)
    peers = [(None, device(lax.rem(s + k, 16), t, d)) for k in range(1, 16)]
    peers += [(None, device(2 * j + other, 1 - t, d)) for other in range(2)]
    barrier = greet(peers)
    items, waits = [], []
    pl.semaphore_wait(barrier, 17)

    waits += half_sends(
        items, s, j, c, t, d,
        lambda chip: at_ref.at[chip],
        lambda slot: xt_ref.at[:, :, pl.ds(pl.multiple_of(slot * 128, 128), 128)],
        at_send, at_recv, local.at[0],
    )
    edge = jnp.logical_or(s == 7, s == 8)
    for k in range(8):
        chip = lax.rem(j + k, 8)
        target = 2 * chip + 1 - zh
        copy = remote(at_ref.at[chip], halo_ref, halo_send.at[k], halo_recv.at[0], device(target, t, d))
        if k == 0:
            alone = c == 1 - zh
            own = pltpu.make_async_copy(at_ref.at[chip], halo_ref, local.at[1])
            items.append((jnp.logical_and(edge, jnp.logical_not(alone)), copy.start, copy.wait_send))
            items.append((jnp.logical_and(edge, alone), own.start, own.wait))
        else:
            items.append((edge, copy.start, copy.wait_send))
    halo_source = 8 - c
    halo_copy = remote(halo_ref, halo_ref, halo_send.at[0], halo_recv.at[0], device(s, t, d))
    waits.append((halo_source != s, halo_copy.wait_recv))
    mine = cwf_ref.at[:, pl.ds(pl.multiple_of(c * 80, 16), 80), :]
    copy = remote(cw_ref, mine, c_send.at[0], c_recv.at[0], device(2 * j + 1 - c, t, d))
    items.append((None, copy.start, copy.wait_send))
    waits.append((None, copy.wait_recv))
    own = pltpu.make_async_copy(cw_ref, mine, local.at[2])
    items.append((None, own.start, own.wait))
    for k in range(16):
        target = lax.rem(s + k, 16)
        src = wp_ref.at[lax.rem(target, 2), d]
        if k == 0:
            own = pltpu.make_async_copy(src, wq_ref.at[s], local.at[3])
            items.append((None, own.start, own.wait))
        else:
            copy = remote(src, wq_ref.at[s], w_send.at[k], w_recv.at[k], device(target, t, d))
            items.append((None, copy.start, copy.wait_send))
            waits.append((None, copy.wait_recv))
    quad_sends(items, waits, j, c, t, d, lambda cc, tt: cot_ref, cots_ref, q_send, q_recv, local.at[4])
    for condition, start, _ in items:
        under(condition, start)
    for condition, wait in waits:
        under(condition, wait)
    for condition, _, wait in items:
        under(condition, wait)


def quad_peers(j, c, t, d):
    index = 2 * c + t
    found = []
    for k in range(1, 4):
        other = lax.rem(index + k, 4)
        found.append((None, device(2 * j + lax.div(other, 2), lax.rem(other, 2), d)))
    return found


def quad_sends(items, waits, j, c, t, d, src_of, dst_ref, send, recv, local):
    index = 2 * c + t
    for k in range(4):
        other = lax.rem(index + k, 4)
        cc, tt = lax.div(other, 2), lax.rem(other, 2)
        src = src_of(cc, tt)
        if k == 0:
            own = pltpu.make_async_copy(src, dst_ref.at[c, t], local)
            items.append((None, own.start, own.wait))
        else:
            copy = remote(src, dst_ref.at[c, t], send.at[k], recv.at[k], device(2 * j + cc, tt, d))
            items.append((None, copy.start, copy.wait_send))
            waits.append((None, copy.wait_recv))


def settle(items, waits):
    for condition, start, _ in items:
        under(condition, start)
    for condition, wait in waits:
        under(condition, wait)
    for condition, _, wait in items:
        under(condition, wait)


def section_kernel(part_ref, wq_ref, rs_ref, wf_ref, send, recv, y_send, y_recv, local):
    s, j, c, t, d = place()
    zh = lax.div(s, 8)
    senders = []
    for k in range(8):
        target = device(2 * lax.rem(j + k, 8) + zh, t, d)
        senders.append((c != zh if k == 0 else None, target))
    senders += [(None, device(s, t, lax.rem(d + k, 4))) for k in range(1, 4)]
    barrier = greet(senders)
    pl.semaphore_wait(barrier, 11 - jnp.where(c == zh, 1, 0))
    items, waits = [], []
    m = lax.rem(s, 8)
    for k in range(8):
        slot = lax.rem(m + k, 8)
        target = 8 * c + slot
        copy = remote(part_ref.at[slot], rs_ref.at[j], send.at[k], recv.at[j], device(target, t, d))
        if k == 0:
            items.append((c != zh, copy.start, copy.wait_send))
            own = pltpu.make_async_copy(part_ref.at[slot], rs_ref.at[j], local.at[0])
            items.append((c == zh, own.start, own.wait))
        else:
            items.append((None, copy.start, copy.wait_send))
    for n in range(8):
        copy = remote(rs_ref.at[n], rs_ref.at[n], send.at[0], recv.at[n], device(s, t, d))
        waits.append((2 * n + zh != s, copy.wait_recv))
    own = pltpu.make_async_copy(wq_ref, wf_ref.at[:, d], local.at[1])
    items.append((None, own.start, own.wait))
    for k in range(1, 4):
        copy = remote(wq_ref, wf_ref.at[:, d], y_send.at[k], y_recv.at[k], device(s, t, lax.rem(d + k, 4)))
        items.append((None, copy.start, copy.wait_send))
        waits.append((None, copy.wait_recv))
    settle(items, waits)


def quad_kernel(count, *refs):
    s, j, c, t, d = place()
    ins, outs, sems = refs[:count], refs[count : 2 * count], refs[2 * count :]
    barrier = greet(quad_peers(j, c, t, d))
    pl.semaphore_wait(barrier, 3)
    items, waits = [], []
    for n in range(count):
        if len(ins[n].shape) == len(outs[n].shape):
            src_of = lambda cc, tt, n=n: ins[n].at[cc, tt]
        else:
            src_of = lambda cc, tt, n=n: ins[n]
        quad_sends(items, waits, j, c, t, d, src_of, outs[n], sems[3 * n], sems[3 * n + 1], sems[3 * n + 2].at[0])
    settle(items, waits)


def head_group_sends(items, waits, j, c, t, d, src_of, dst_ref, send, recv, local):
    for k in range(8):
        chip = lax.rem(j + k, 8)
        src = src_of(chip)
        if k == 0:
            own = pltpu.make_async_copy(src, dst_ref.at[j], local)
            items.append((None, own.start, own.wait))
        else:
            copy = remote(src, dst_ref.at[j], send.at[k], recv.at[k], device(2 * chip + c, t, d))
            items.append((None, copy.start, copy.wait_send))
            waits.append((None, copy.wait_recv))


def keys_kernel(kv_ref, all_ref, send, recv, local):
    s, j, c, t, d = place()
    barrier = greet([(None, device(2 * lax.rem(j + k, 8) + c, t, d)) for k in range(1, 8)])
    pl.semaphore_wait(barrier, 7)
    items, waits = [], []
    head_group_sends(items, waits, j, c, t, d, lambda chip: kv_ref, all_ref, send, recv, local.at[0])
    settle(items, waits)


def key_grads_kernel(dkv_ref, bo_ref, all_ref, bos_ref, send, recv, q_send, q_recv, local):
    s, j, c, t, d = place()
    peers = [(None, device(2 * lax.rem(j + k, 8) + c, t, d)) for k in range(1, 8)]
    barrier = greet(peers + quad_peers(j, c, t, d))
    pl.semaphore_wait(barrier, 10)
    items, waits = [], []
    head_group_sends(items, waits, j, c, t, d, lambda chip: dkv_ref.at[chip], all_ref, send, recv, local.at[0])
    quad_sends(items, waits, j, c, t, d, lambda cc, tt: bo_ref.at[cc, tt], bos_ref, q_send, q_recv, local.at[1])
    settle(items, waits)


def pool_kernel(gp_ref, hg_ref, gps_ref, hgs_ref, send, recv, y_send, y_recv, local):
    s, j, c, t, d = place()
    zh = lax.div(s, 8)
    m = lax.rem(s, 8)
    senders = []
    for k in range(8):
        n = lax.rem(m + k, 8)
        senders.append((c != zh if k == 0 else None, device(8 * c + n, t, d)))
    senders += [(None, device(s, t, lax.rem(d + k, 4))) for k in range(1, 4)]
    barrier = greet(senders)
    pl.semaphore_wait(barrier, 11 - jnp.where(c == zh, 1, 0))
    items = []
    waits = half_sends(items, s, j, c, t, d, lambda chip: gp_ref, lambda slot: gps_ref.at[slot], send, recv, local.at[0])
    own = pltpu.make_async_copy(hg_ref.at[d], hgs_ref.at[d], local.at[1])
    items.append((None, own.start, own.wait))
    for k in range(1, 4):
        other = lax.rem(d + k, 4)
        copy = remote(hg_ref.at[other], hgs_ref.at[d], y_send.at[k], y_recv.at[k], device(s, t, other))
        items.append((None, copy.start, copy.wait_send))
        waits.append((None, copy.wait_recv))
    settle(items, waits)


def last_kernel(hg_ref, cg_ref, hgs_ref, cgs_ref, send, recv, y_send, y_recv, local):
    s, j, c, t, d = place()
    peers = [(None, device(lax.rem(s + k, 16), t, d)) for k in range(1, 16)]
    index = 4 * c + d
    others = []
    for k in range(8):
        other = lax.rem(index + k, 8)
        others.append((lax.div(other, 4), lax.rem(other, 4)))
    for cc, dd in others[1:]:
        peers.append((dd != d, device(2 * j + cc, t, dd)))
    barrier = greet(peers)
    pl.semaphore_wait(barrier, 21)
    items, waits = [], []
    for k in range(16):
        target = lax.rem(s + k, 16)
        if k == 0:
            own = pltpu.make_async_copy(hg_ref.at[target], hgs_ref.at[s], local.at[0])
            items.append((None, own.start, own.wait))
        else:
            copy = remote(hg_ref.at[target], hgs_ref.at[s], send.at[k], recv.at[k], device(target, t, d))
            items.append((None, copy.start, copy.wait_send))
            waits.append((None, copy.wait_recv))
    for k in range(8):
        cc, dd = others[k]
        if k == 0:
            own = pltpu.make_async_copy(cg_ref.at[cc, dd], cgs_ref.at[c, d], local.at[1])
            items.append((None, own.start, own.wait))
        else:
            copy = remote(cg_ref.at[cc, dd], cgs_ref.at[c, d], y_send.at[k], y_recv.at[k], device(2 * j + cc, t, dd))
            items.append((None, copy.start, copy.wait_send))
            waits.append((None, copy.wait_recv))
    settle(items, waits)


def dot(a, b, dims):
    return lax.dot_general(a, b, (dims, ((), ())), preferred_element_type=F32)


def attention_kernel(q_ref, kv_ref, g_ref, att_ref, dq_ref, dkv_ref):
    scale = HEAD_DIM ** (-0.5)
    query = q_ref[...]
    grad = g_ref[...]
    keys = kv_ref[:, :HEAD_DIM]
    values = kv_ref[:, HEAD_DIM:]
    scores = dot(keys, query, ((1,), (1,))) * scale
    highest = jnp.max(scores, axis=0, keepdims=True)
    unnormed = jnp.exp(scores - highest)
    weights = unnormed / jnp.sum(unnormed, axis=0, keepdims=True)
    rounded = weights.astype(BF16)
    att_ref[...] = dot(rounded, values, ((0,), (0,))).astype(BF16)
    grad_prob = dot(values, grad, ((1,), (1,)))
    centre = jnp.sum(weights * grad_prob, axis=0, keepdims=True)
    grad_score = (weights * (grad_prob - centre)).astype(BF16)
    dq_ref[...] = (dot(grad_score, keys, ((0,), (0,))) * scale).astype(BF16)
    dkv_ref[:, :HEAD_DIM] = (dot(grad_score, query, ((1,), (0,))) * scale).astype(BF16)
    dkv_ref[:, HEAD_DIM:] = dot(rounded, grad, ((1,), (0,))).astype(BF16)


def attention(query, kv, grad):
    rows, keys = query.shape[0], kv.shape[0]
    vmem = pl.BlockSpec(memory_space=pltpu.VMEM)
    return pl.pallas_call(
        attention_kernel,
        out_shape=(
            jax.ShapeDtypeStruct((rows, HEAD_DIM), BF16),
            jax.ShapeDtypeStruct((rows, HEAD_DIM), BF16),
            jax.ShapeDtypeStruct((keys, 2 * HEAD_DIM), BF16),
        ),
        in_specs=[vmem] * 3,
        out_specs=(vmem,) * 3,
        compiler_params=pltpu.CompilerParams(vmem_limit_bytes=48 * 1024 * 1024),
    )(query, kv, grad)


def shape(*dims):
    return jax.ShapeDtypeStruct(dims, BF16)


def local(section_input, conv_weight, head_weight, output_weight, cotangent):
    s, j, c, t, d = place()
    activity = jax.nn.gelu(section_input[0].astype(F32), approximate=True).astype(BF16)
    at = activity.reshape(128, 2, 8, 160).transpose(2, 1, 3, 0)
    taps = conv_weight.transpose(1, 0, 2).astype(F32) * 0.5
    zero = jnp.zeros((1,) + taps.shape[1:], F32)
    cw = (jnp.concatenate([taps, zero]) + jnp.concatenate([zero, taps])).astype(BF16)
    wp = jnp.concatenate(
        [head_weight.reshape(96, 3, 2, 192), output_weight.reshape(96, 1, 2, 192)], axis=1
    )
    wp = wp.transpose(2, 0, 1, 3).reshape(2, 4, 24, 768)
    cot = cotangent[0]
    xt, halo, cwf, wq, cots = communicate(
        start_kernel, 1,
        (shape(2, 160, 1024), shape(2, 160, 128), shape(6, 160, 768), shape(16, 24, 768), shape(2, 2, 128, 768)),
        (8, 8, 8, 1, 16, 16, 4, 4, 1, 1, 5),
        at, cw, wp, cot,
    )
    low = jnp.where(c == 1, halo[:, :, 127:], 0)
    high = jnp.where(c == 0, halo[:, :, :1], 0)
    before = jnp.concatenate([low, xt[:, :, :-1]], axis=2)
    after = jnp.concatenate([xt[:, :, 1:], high], axis=2)
    taken = jnp.concatenate([before, xt, after], axis=0).reshape(960, 1024)
    part = dot(taken, cwf.reshape(960, 768), ((0,), (0,))).astype(BF16).reshape(8, 128, 768)
    rs, wf = communicate(
        section_kernel, 2, (shape(8, 128, 768), shape(16, 4, 24, 768)), (8, 8, 4, 4, 2), part, wq
    )
    section_local = jnp.sum(rs.astype(F32), axis=0).astype(BF16)
    (sections,) = communicate(
        functools.partial(quad_kernel, 1), 3, (shape(2, 2, 128, 768),), (4, 4, 1), section_local
    )
    weights = wf.reshape(1536, 768)
    head_full, output_full = weights[:, :576], weights[:, 576:]
    section = sections.transpose(0, 2, 1, 3).reshape(256, 1536).astype(F32)
    inverse = lax.rsqrt(jnp.mean(section * section, axis=-1, keepdims=True) + EPSILON)
    normed = (section * inverse).astype(BF16)
    projected = dot(normed, head_full, ((1,), (0,))).astype(BF16)
    cot_full = cots.transpose(0, 2, 1, 3).reshape(256, 1536)
    grad_att = dot(cot_full, output_full, ((1,), (0,))).astype(BF16)
    (kv,) = communicate(keys_kernel, 4, (shape(8, 256, 384),), (8, 8, 1), projected[:, 192:])
    attended, grad_query, dkv = attention(projected[:, :192], kv.reshape(2048, 384), grad_att)
    out_part = dot(attended, output_full, ((1,), (1,))).astype(BF16)
    out_part = out_part.reshape(2, 128, 2, 768).transpose(0, 2, 1, 3)
    dkvs, outs = communicate(
        key_grads_kernel, 5, (shape(8, 256, 384), shape(2, 2, 128, 768)), (8, 8, 4, 4, 2),
        dkv.reshape(8, 256, 384), out_part,
    )
    block_out = (
        section_local.astype(F32) + jnp.sum(outs.astype(F32), axis=(0, 1))
    ).astype(BF16)
    grad_kv = jnp.sum(dkvs.astype(F32), axis=0).astype(BF16)
    grad_proj = jnp.concatenate([grad_query, grad_kv], axis=1)
    normed_part = dot(grad_proj, head_full, ((1,), (1,)))
    spread_part = jnp.sum(normed_part * section, axis=-1) * (1.0 / 1536)
    spread_high = spread_part.astype(BF16)
    spread_low = (spread_part - spread_high.astype(F32)).astype(BF16)
    spread_pair = jnp.stack([spread_high, spread_low], axis=-1).reshape(2, 128, 2)
    spread_pair = jnp.broadcast_to(
        jnp.pad(spread_pair, ((0, 0), (0, 0), (0, 126)))[:, None], (2, 2, 128, 128)
    )
    norm_part = normed_part.astype(BF16).reshape(2, 128, 2, 768).transpose(0, 2, 1, 3)
    norms, spreads = communicate(
        functools.partial(quad_kernel, 2), 6,
        (shape(2, 2, 128, 768), shape(2, 2, 128, 128)), (4, 4, 1, 4, 4, 1), norm_part, spread_pair,
    )
    grad_normed = jnp.sum(norms.astype(F32), axis=(0, 1))
    spread = jnp.sum(spreads.astype(F32), axis=(0, 1, 3))[:, None]
    inverse_here = lax.dynamic_slice_in_dim(inverse, 128 * c, 128, 0)
    grad_section = (
        cot.astype(F32)
        + inverse_here * grad_normed
        - inverse_here**3 * section_local.astype(F32) * spread
    )
    grad_pool = (0.5 * grad_section).astype(BF16)
    head_part = dot(normed, grad_proj, ((0,), (0,)))
    output_part = dot(cot_full, attended, ((0,), (0,)))
    hg = jnp.concatenate([head_part, output_part], axis=1).astype(BF16)
    hg = hg.reshape(16, 4, 24, 768).transpose(1, 0, 2, 3)
    gps, hgs = communicate(
        pool_kernel, 7, (shape(8, 128, 768), shape(4, 16, 24, 768)), (8, 8, 4, 4, 2), grad_pool, hg
    )
    hg_sum = jnp.sum(hgs.astype(F32), axis=0).astype(BF16)
    products = dot(taken, gps.reshape(1024, 768), ((1,), (0,))).reshape(6, 160, 768)
    cg = (products[:5] + products[1:]).astype(BF16)
    cg = cg.reshape(5, 2, 4, 20, 768).transpose(1, 2, 0, 3, 4).reshape(2, 4, 100, 768)
    hgl, cgl = communicate(
        last_kernel, 8, (shape(16, 24, 768), shape(2, 4, 100, 768)), (16, 16, 8, 8, 2), hg_sum, cg
    )
    conv_grad = jnp.sum(cgl.astype(F32), axis=(0, 1)).reshape(5, 20, 768).transpose(1, 0, 2)
    both = jnp.sum(hgl.astype(F32).reshape(8, 2, 24, 4, 192), axis=0)
    both = both.transpose(1, 2, 0, 3).reshape(24, 4, 384)
    return (block_out[None], conv_grad, both[:, :3], both[:, 3])


def solution(mesh):
    placed = (
        P("dp", "seq", None),
        P("seq", None, "tensor"),
        P("seq", None, "tensor"),
        P("seq", "tensor"),
        P("dp", "seq", "tensor"),
    )
    return jax.shard_map(
        local,
        mesh=mesh,
        in_specs=placed,
        out_specs=(
            P("dp", "seq", "tensor"),
            P(("seq", "dp"), None, "tensor"),
            P(("seq", "dp"), None, "tensor"),
            P(("seq", "dp"), "tensor"),
        ),
        check_vma=False,
    )
```

```python
import functools

import jax
import jax.numpy as jnp
from jax import lax
from jax.experimental import pallas as pl
from jax.experimental.pallas import tpu as pltpu
from jax.sharding import PartitionSpec as P

HEAD_DIM = 192
EPSILON = 1e-06
MESH = pl.DeviceIdType.MESH
BF16 = jnp.bfloat16
F32 = jnp.float32


class Place:
    def __init__(self):
        self.s = lax.axis_index("seq")
        self.zh = lax.div(self.s, 8)
        self.x = lax.rem(lax.div(self.s, 2), 4)
        self.c = lax.rem(self.s, 2)
        self.t = lax.axis_index("tensor")
        self.d = lax.axis_index("dp")
        self.z = 2 * self.zh + self.t

    def at(self, x=None, zh=None, c=None, t=None, d=None):
        x = self.x if x is None else x
        zh = self.zh if zh is None else zh
        c = self.c if c is None else c
        return {
            "seq": zh * 8 + x * 2 + c,
            "tensor": self.t if t is None else t,
            "dp": self.d if d is None else d,
        }

    def along_x(self, k):
        return lax.rem(self.x + k, 4)

    def along_y(self, k):
        return lax.rem(self.d + k, 4)

    def along_z(self, k):
        return lax.rem(self.z + k, 4)

    def at_z(self, z):
        return self.at(zh=lax.div(z, 2), t=lax.rem(z, 2))

    @property
    def sibling(self):
        return self.at(c=1 - self.c)


def remote(src, dst, send, recv, target):
    return pltpu.make_async_remote_copy(
        src_ref=src, dst_ref=dst, send_sem=send, recv_sem=recv, device_id=target, device_id_type=MESH
    )


def greet(targets):
    barrier = pltpu.get_barrier_semaphore()
    for condition, target in targets:
        if condition is None:
            pl.semaphore_signal(barrier, inc=1, device_id=target, device_id_type=MESH)
        else:

            @pl.when(condition)
            def _(target=target):
                pl.semaphore_signal(barrier, inc=1, device_id=target, device_id_type=MESH)

    return barrier


def under(condition, action):
    if condition is None:
        action()
    else:

        @pl.when(condition)
        def _():
            action()


def communicate(kernel, name, collective, outputs, remotes, locals_, *operands, aliases=None, vmem=(), scratch=()):
    anywhere = pl.BlockSpec(memory_space=pl.ANY)
    inside = pl.BlockSpec(memory_space=pltpu.VMEM)
    return pl.pallas_call(
        kernel,
        name=name,
        out_shape=outputs,
        in_specs=[inside if n in vmem else anywhere for n in range(len(operands))],
        out_specs=tuple([anywhere] * len(outputs)),
        scratch_shapes=list(scratch)
        + [
            pltpu.SemaphoreType.DMA((remotes,)),
            pltpu.SemaphoreType.DMA((remotes,)),
            pltpu.SemaphoreType.DMA((locals_,)),
        ],
        input_output_aliases=aliases or {},
        compiler_params=pltpu.CompilerParams(
            collective_id=collective, has_side_effects=True, vmem_limit_bytes=16 * 1024 * 1024 if vmem else None
        ),
    )(*operands)


class Moves:
    def __init__(self, place, send, recv, local):
        self.place, self.send, self.recv, self.local = place, send, recv, local
        self.sends, self.receives, self.locals = [], [], []
        self.used = 0
        self.used_local = 0

    def slots(self, count):
        first = self.used
        self.used += count
        return first

    def push(self, src, dst, target, slot, recv_slot=None, when=None):
        recv_slot = slot if recv_slot is None else recv_slot
        copy = remote(src, dst, self.send.at[slot], self.recv.at[recv_slot], target)
        under(when, copy.start)
        self.sends.append((when, copy.wait_send))

    def keep(self, src, dst, when=None):
        copy = pltpu.make_async_copy(src, dst, self.local.at[self.used_local])
        self.used_local += 1
        under(when, copy.start)
        self.locals.append((when, copy.wait))

    def arrival(self, dst, slot, when=None):
        place = self.place
        copy = remote(dst, dst, self.send.at[0], self.recv.at[slot], place.at())
        return lambda: under(when, copy.wait_recv)

    def expect(self, dst, slot, when=None):
        self.receives.append(self.arrival(dst, slot, when))

    def settle(self):
        for wait in self.receives:
            wait()
        for when, wait in self.locals + self.sends:
            under(when, wait)


def z_gather(moves, src, dst_ref):
    p = moves.place
    first = moves.slots(4)
    moves.keep(src, dst_ref.at[p.z])
    for k in (2, 1, 3):
        moves.push(src, dst_ref.at[p.z], p.at_z(p.along_z(k)), first + k)
        moves.expect(dst_ref.at[p.along_z(4 - k)], first + k)


def z_scatter(moves, src_ref, dst_ref):
    p = moves.place
    first = moves.slots(4)
    moves.keep(src_ref.at[p.z], dst_ref.at[p.z])
    for k in (2, 1, 3):
        z = p.along_z(k)
        moves.push(src_ref.at[z], dst_ref.at[p.z], p.at_z(z), first + k)
        moves.expect(dst_ref.at[p.along_z(4 - k)], first + k)


def z_ring(p):
    return [(None, p.at_z(p.along_z(k))) for k in range(1, 4)]


def y_ring(p):
    return [(None, p.at(d=p.along_y(k))) for k in range(1, 4)]


def x_ring(p):
    return [(None, p.at(x=p.along_x(k))) for k in range(1, 4)]


def start_kernel(at_ref, edge_ref, cw_ref, wp_ref, xt_ref, low_ref, high_ref, cwf_ref, wq_ref, send, recv, local):
    p = Place()
    peers = []
    for k in range(1, 16):
        peers.append((None, {"seq": lax.rem(p.s + k, 16), "tensor": p.t, "dp": p.d}))
    barrier = greet(peers)
    pl.semaphore_wait(barrier, 15)
    moves = Moves(p, send, recv, local)

    first = moves.slots(4)
    mine = cwf_ref.at[:, 2 * p.zh + p.c]
    moves.push(cw_ref, mine, p.at(zh=1 - p.zh), first)
    moves.push(cw_ref, mine, p.sibling, first + 1)
    moves.keep(cw_ref, mine)
    from_z = cwf_ref.at[:, 2 * (1 - p.zh) + p.c]
    conv_arrival = moves.arrival(from_z, first)
    moves.expect(cwf_ref.at[:, 2 * p.zh + 1 - p.c], first + 1)

    a = moves.slots(4)
    core = lax.div(p.x, 2)
    slot = 2 * lax.rem(p.x, 2) + p.c
    spot = xt_ref.at[:, :, pl.ds(pl.multiple_of(slot * 128, 128), 128)]
    for k in (2, 1, 3, 0):
        x = p.along_x(k)
        if k == 0:
            moves.push(at_ref.at[x], spot, p.at(c=core), a, a + slot, core != p.c)
            moves.keep(at_ref.at[x], spot, core == p.c)
        else:
            moves.push(at_ref.at[x], spot, p.at(x=x, c=core), a + k, a + slot)
    for n in range(4):
        x, c = 2 * p.c + n // 2, n % 2
        here = xt_ref.at[:, :, pl.ds(n * 128, 128)]
        moves.expect(here, a + n, jnp.logical_or(x != p.x, c != p.c))
    for up, out_ref in ((True, low_ref), (False, high_ref)):
        e = moves.slots(4)
        if up:
            sends = jnp.logical_and(lax.rem(p.s, 4) == 3, p.s != 15)
            block = lax.rem(p.s + 1, 16)
        else:
            sends = jnp.logical_and(lax.rem(p.s, 4) == 0, p.s != 0)
            block = lax.rem(p.s + 15, 16)
        zh, c = lax.div(block, 8), lax.div(lax.rem(block, 8), 4)
        for k in range(4):
            x = p.along_x(k)
            src = edge_ref.at[1 if up else 0, x]
            target = p.at(x=x, zh=zh, c=c)
            if k == 0:
                alone = jnp.logical_and(zh == p.zh, c == p.c)
                moves.push(src, out_ref, target, e, e, jnp.logical_and(sends, jnp.logical_not(alone)))
                moves.keep(src, out_ref, jnp.logical_and(sends, alone))
            else:
                moves.push(src, out_ref, target, e + k, e, sends)
        base = 8 * p.zh + 4 * p.c
        if up:
            moves.expect(out_ref, e, jnp.logical_and(base != 0, base - 1 != p.s))
        else:
            moves.expect(out_ref, e, jnp.logical_and(base != 12, base + 4 != p.s))
    w = moves.slots(8)
    shard = 4 * p.zh + p.x
    for k in range(8):
        other = lax.rem(shard + k, 8)
        zh, x = lax.div(other, 4), lax.rem(other, 4)
        src = wp_ref.at[zh, p.d]
        if k == 0:
            moves.keep(src, wq_ref.at[shard])
        else:
            moves.push(src, wq_ref.at[shard], p.at(x=x, zh=zh), w + k)
            moves.expect(wq_ref.at[lax.rem(shard + 8 - k, 8)], w + k)
    conv_arrival()
    moves.push(from_z, from_z, p.sibling, first + 2)
    moves.expect(cwf_ref.at[:, 2 * (1 - p.zh) + 1 - p.c], first + 2)
    moves.settle()


def weight_rows(moves, wq_ref, wf_ref, lower, wait_now):
    p = moves.place
    y = moves.slots(8)
    src = wq_ref.at[pl.ds(lower, 4)]

    def rows(c, d):
        return wf_ref.at[lower // 4, :, c, d]

    moves.keep(src, rows(p.c, p.d))
    moves.push(src, rows(p.c, p.d), p.sibling, y)
    moves.expect(rows(1 - p.c, p.d), y)
    for k in (2, 1, 3):
        moves.push(src, rows(p.c, p.d), p.at(d=p.along_y(k)), y + k)

    def forward():
        for k in (1, 3, 2):
            d = p.along_y(4 - k)
            moves.arrival(rows(p.c, d), y + k)()
            moves.push(rows(p.c, d), rows(p.c, d), p.sibling, y + 3 + k)
            moves.expect(rows(1 - p.c, d), y + 3 + k)

    wait_now.append(forward)


def section_kernel(part_ref, cot_ref, x5_ref, wq_ref, rs_ref, cots_ref, x5s_ref, wa_ref, send, recv, local):
    p = Place()
    core = lax.div(p.x, 2)
    senders = []
    for k in range(4):
        senders.append((core != p.c if k == 0 else None, p.at(x=p.along_x(k), c=core)))
    barrier = greet(senders + [(None, p.sibling)] + z_ring(p) + y_ring(p))
    pl.semaphore_wait(barrier, 3 + jnp.where(core != p.c, 1, 0) + 1 + 3 + 3)
    moves = Moves(p, send, recv, local)
    a = moves.slots(4)
    for k in (2, 1, 3, 0):
        slot = lax.rem(2 * lax.rem(p.x, 2) + p.c + k, 4)
        x, c = 2 * p.c + lax.div(slot, 2), lax.rem(slot, 2)
        alone = jnp.logical_and(x == p.x, c == p.c)
        moves.push(part_ref.at[slot], rs_ref.at[p.x], p.at(x=x, c=c), a + k, a + p.x, jnp.logical_not(alone))
        moves.keep(part_ref.at[slot], rs_ref.at[p.x], alone)
    for x in range(4):
        moves.expect(rs_ref.at[x], a + x, jnp.logical_or(p.x != x, core != p.c))
    later = []
    weight_rows(moves, wq_ref, wa_ref, 0, later)
    z_gather(moves, cot_ref, cots_ref)
    b = moves.slots(1)
    moves.push(x5_ref, x5s_ref, p.sibling, b)
    moves.expect(x5s_ref, b)
    for action in later:
        action()
    moves.settle()


def channels_kernel(sec_ref, wq_ref, wa_ref, secs_ref, wf_ref, send, recv, local):
    p = Place()
    barrier = greet(z_ring(p) + y_ring(p) + [(None, p.sibling)])
    pl.semaphore_wait(barrier, 7)
    moves = Moves(p, send, recv, local)
    z_gather(moves, sec_ref, secs_ref)
    later = []
    weight_rows(moves, wq_ref, wf_ref, 4, later)
    for action in later:
        action()
    moves.settle()


def keys_kernel(kv_ref, all_ref, send, recv, local):
    p = Place()
    barrier = greet(x_ring(p) + [(None, p.sibling)])
    pl.semaphore_wait(barrier, 4)
    moves = Moves(p, send, recv, local)
    a = moves.slots(8)
    mine = all_ref.at[p.c, p.x]
    for k in (2, 1, 3):
        moves.push(kv_ref, mine, p.at(x=p.along_x(k)), a + k)
    moves.push(kv_ref, mine, p.sibling, a)
    moves.keep(kv_ref, mine)
    moves.expect(all_ref.at[1 - p.c, p.x], a)
    for k in (1, 3, 2):
        x = p.along_x(4 - k)
        moves.arrival(all_ref.at[p.c, x], a + k)()
        moves.push(all_ref.at[p.c, x], all_ref.at[p.c, x], p.sibling, a + 3 + k)
        moves.expect(all_ref.at[1 - p.c, x], a + 3 + k)
    moves.settle()


def key_grads_kernel(dkv_ref, bo_ref, all_ref, bos_ref, buf_ref, sum_ref, send, recv, local):
    p = Place()
    barrier = greet(x_ring(p) + [(None, p.sibling)] + z_ring(p))
    pl.semaphore_wait(barrier, 7)
    moves = Moves(p, send, recv, local)
    a = moves.slots(8)
    for k in (2, 1, 3, 0):
        x = p.along_x(k)
        moves.push(dkv_ref.at[1 - p.c, x], buf_ref.at[k], p.sibling, a + k)
    z_scatter(moves, bo_ref, bos_ref)
    for k in (2, 1, 3, 0):
        x = p.along_x(k)
        moves.arrival(buf_ref.at[k], a + k)()
        total = (dkv_ref[p.c, x].astype(F32) + buf_ref[k].astype(F32)).astype(BF16)
        if k == 0:
            sum_ref[0] = total
            moves.keep(sum_ref.at[0], all_ref.at[p.x])
        else:
            sum_ref[k] = total
            moves.push(sum_ref.at[k], all_ref.at[p.x], p.at(x=x), a + 4 + k)
            moves.expect(all_ref.at[p.along_x(4 - k)], a + 4 + k)
    moves.settle()


def norm_kernel(norm_ref, spread_ref, nh_ref, ch_ref, gpa_ref, norms_ref, spreads_ref, nhs_ref, chs_ref, gpas_ref,
                send, recv, local):
    p = Place()
    barrier = greet(z_ring(p) + [(None, p.sibling)])
    pl.semaphore_wait(barrier, 4)
    moves = Moves(p, send, recv, local)
    z_scatter(moves, norm_ref, norms_ref)
    z_scatter(moves, spread_ref, spreads_ref)
    b = moves.slots(3)
    for n, (src, dst) in enumerate(((nh_ref.at[1 - p.c], nhs_ref), (ch_ref.at[1 - p.c], chs_ref), (gpa_ref, gpas_ref))):
        moves.push(src, dst, p.sibling, b + n)
        moves.expect(dst, b + n)
    moves.settle()


def pool_kernel(gp_ref, hg_ref, gps_ref, hgs_ref, send, recv, local):
    p = Place()
    barrier = greet(
        [(None, p.at(x=p.along_x(k), c=c)) for k in range(1, 4) for c in range(2)] + [(None, p.sibling)] + y_ring(p)
    )
    pl.semaphore_wait(barrier, 10)
    moves = Moves(p, send, recv, local)
    y = moves.slots(4)
    moves.keep(hg_ref.at[p.d], hgs_ref.at[p.d])
    for k in (2, 1, 3):
        d = p.along_y(k)
        moves.push(hg_ref.at[d], hgs_ref.at[p.d], p.at(d=d), y + k)
        moves.expect(hgs_ref.at[p.along_y(4 - k)], y + k)
    a = moves.slots(8)
    block = 2 * p.x + p.c
    for k in (4, 5, 2, 3, 6, 7, 1, 0):
        other = lax.rem(block + k, 8)
        x, c = lax.div(other, 2), lax.rem(other, 2)
        if k == 0:
            moves.keep(gp_ref.at[c], gps_ref.at[block])
        else:
            moves.push(gp_ref.at[c], gps_ref.at[block], p.at(x=x, c=c), a + k)
            moves.expect(gps_ref.at[lax.rem(block + 8 - k, 8)], a + k)
    moves.settle()


def last_kernel(hg_ref, cg_ref, hgs_ref, cgs_ref, send, recv, local):
    p = Place()
    peers = []
    for zh in range(2):
        for c in range(2):
            for k in range(4):
                here = k == 0
                target = p.at(zh=zh, c=c, d=p.along_y(k))
                peers.append((jnp.logical_or(zh != p.zh, c != p.c) if here else None, target))
    for zh in range(2):
        for k in range(1, 4):
            peers.append((None, p.at(zh=zh, x=p.along_x(k), c=p.zh)))
    barrier = greet(peers)
    pl.semaphore_wait(barrier, 15 + 6)
    moves = Moves(p, send, recv, local)
    b = moves.slots(16)
    me = 8 * p.zh + 4 * p.c + p.d
    for k in (8, 12, 4, 2, 10, 14, 6, 1, 3, 9, 11, 13, 15, 5, 7, 0):
        other = lax.rem(me + k, 16)
        zh, c, d = lax.div(other, 8), lax.rem(lax.div(other, 4), 2), lax.rem(other, 4)
        src = cg_ref.at[zh, c, d]
        if k == 0:
            moves.keep(src, cgs_ref.at[me])
        else:
            moves.push(src, cgs_ref.at[me], p.at(zh=zh, c=c, d=d), b + k)
            moves.expect(cgs_ref.at[lax.rem(me + 16 - k, 16)], b + k)
    a = moves.slots(8)
    for k in range(8):
        other = lax.rem(2 * p.x + k, 8)
        x, c = lax.div(other, 2), lax.rem(other, 2)
        src, dst = hg_ref.at[x, c], hgs_ref.at[p.zh, p.x]
        alone = jnp.logical_and(jnp.logical_and(x == p.x, c == p.c), p.zh == p.c)
        if k < 2:
            moves.push(src, dst, p.at(x=x, zh=p.c, c=c), a + k, a + 4 * p.zh + p.x, jnp.logical_not(alone))
            moves.keep(src, dst, alone)
        else:
            moves.push(src, dst, p.at(x=x, zh=p.c, c=c), a + k, a + 4 * p.zh + p.x)
    for zh in range(2):
        for x in range(4):
            alone = jnp.logical_and(jnp.logical_and(x == p.x, zh == p.zh), p.zh == p.c)
            moves.expect(hgs_ref.at[zh, x], a + 4 * zh + x, jnp.logical_not(alone))
    moves.settle()

def dot(a, b, dims):
    return lax.dot_general(a, b, (dims, ((), ())), preferred_element_type=F32)


def attention_kernel(q_ref, kv_ref, g_ref, att_ref, dq_ref, dkv_ref):
    scale = HEAD_DIM ** (-0.5)
    query = q_ref[...]
    grad = g_ref[...]
    keys = kv_ref[:, :HEAD_DIM]
    values = kv_ref[:, HEAD_DIM:]
    scores = dot(keys, query, ((1,), (1,))) * scale
    highest = jnp.max(scores, axis=0, keepdims=True)
    unnormed = jnp.exp(scores - highest)
    weights = unnormed / jnp.sum(unnormed, axis=0, keepdims=True)
    rounded = weights.astype(BF16)
    att_ref[...] = dot(rounded, values, ((0,), (0,))).astype(BF16)
    grad_prob = dot(values, grad, ((1,), (1,)))
    centre = jnp.sum(weights * grad_prob, axis=0, keepdims=True)
    grad_score = (weights * (grad_prob - centre)).astype(BF16)
    dq_ref[...] = (dot(grad_score, keys, ((0,), (0,))) * scale).astype(BF16)
    dkv_ref[:, :HEAD_DIM] = (dot(grad_score, query, ((1,), (0,))) * scale).astype(BF16)
    dkv_ref[:, HEAD_DIM:] = dot(rounded, grad, ((1,), (0,))).astype(BF16)


def attention(query, kv, grad):
    rows, keys = query.shape[0], kv.shape[0]
    vmem = pl.BlockSpec(memory_space=pltpu.VMEM)
    return pl.pallas_call(
        attention_kernel,
        out_shape=(
            jax.ShapeDtypeStruct((rows, HEAD_DIM), BF16),
            jax.ShapeDtypeStruct((rows, HEAD_DIM), BF16),
            jax.ShapeDtypeStruct((keys, 2 * HEAD_DIM), BF16),
        ),
        in_specs=[vmem] * 3,
        out_specs=(vmem,) * 3,
        compiler_params=pltpu.CompilerParams(vmem_limit_bytes=48 * 1024 * 1024),
    )(query, kv, grad)


def shape(*dims):
    return jax.ShapeDtypeStruct(dims, BF16)


def local(section_input, conv_weight, head_weight, output_weight, cotangent):
    p = Place()
    activity = jax.nn.gelu(section_input[0].astype(F32), approximate=True).astype(BF16)
    bins = activity.reshape(128, 2, 2, 4, 160)
    at = bins.transpose(3, 1, 2, 4, 0).reshape(4, 2, 320, 128)
    edges = jnp.stack([bins[0], bins[127]]).transpose(0, 3, 1, 2, 4).reshape(2, 4, 2, 320)
    edges = jnp.pad(edges, ((0, 0), (0, 0), (0, 6), (0, 0)))
    cw = conv_weight.transpose(1, 0, 2)
    wp = jnp.concatenate(
        [head_weight.reshape(96, 3, 2, 192), output_weight.reshape(96, 1, 2, 192)], axis=1
    )
    wp = wp.transpose(2, 0, 1, 3).reshape(2, 4, 24, 768)
    cot = cotangent[0]
    xt, low, high, cwf, wq = communicate(
        start_kernel, "start", 1,
        (shape(2, 320, 512), shape(8, 320), shape(8, 320), shape(5, 4, 80, 768), shape(8, 24, 768)),
        24, 8, at, edges, cw, wp,
    )
    base = 8 * p.zh + 4 * p.c
    low = jnp.where(base != 0, low[:2], 0)[:, :, None]
    high = jnp.where(base != 12, high[:2], 0)[:, :, None]
    wide = jnp.concatenate([low, xt, high], axis=2).astype(F32)
    even, odd = wide[0], wide[1]
    same = (even + odd).astype(BF16)
    cross = (odd[:, :-1] + even[:, 1:]).astype(BF16)
    x5 = jnp.stack([same[:, :512], cross[:, :512], same[:, 1:513], cross[:, 1:513], same[:, 2:514]])
    x5 = x5.reshape(1600, 512)
    part = (dot(x5, cwf.reshape(1600, 768), ((0,), (0,))) * 0.5).astype(BF16).reshape(4, 128, 768)
    rs, cots, x5s, wa = communicate(
        section_kernel, "section", 2,
        (shape(4, 128, 768), shape(4, 128, 768), shape(1600, 512), shape(2, 4, 2, 4, 24, 768)),
        20, 8, part, cot, x5, wq,
    )
    section_local = jnp.sum(rs.astype(F32), axis=0).astype(BF16)
    sections, wf = communicate(
        channels_kernel, "channels", 3, (shape(4, 128, 768), shape(2, 4, 2, 4, 24, 768)), 16, 4,
        section_local, wq, wa, aliases={2: 1},
    )
    weights = wf.reshape(1536, 768)
    head_full, output_full = weights[:, :576], weights[:, 576:]

    def whole(blocks):
        return blocks.reshape(2, 2, 128, 768).transpose(0, 2, 1, 3).reshape(256, 1536)

    section = whole(sections).astype(F32)
    inverse = lax.rsqrt(jnp.mean(section * section, axis=-1, keepdims=True) + EPSILON)
    normed = (section * inverse).astype(BF16)
    projected = dot(normed, head_full, ((1,), (0,))).astype(BF16)
    cot_full = whole(cots)
    grad_att = dot(cot_full, output_full, ((1,), (0,))).astype(BF16)
    (kv,) = communicate(keys_kernel, "keys", 4, (shape(2, 4, 256, 384),), 8, 1, projected[:, 192:])
    attended, grad_query, dkv = attention(projected[:, :192], kv.reshape(2048, 384), grad_att)

    def blocks(full):
        return full.reshape(2, 128, 2, 768).transpose(0, 2, 1, 3).reshape(4, 128, 768)

    out_part = blocks(dot(attended, output_full, ((1,), (1,))).astype(BF16))
    dkvs, outs, = communicate(
        key_grads_kernel, "key_grads", 5, (shape(4, 256, 384), shape(4, 128, 768)), 12, 2,
        dkv.reshape(2, 4, 256, 384), out_part, vmem=(0,),
        scratch=(pltpu.VMEM((4, 256, 384), BF16), pltpu.VMEM((4, 256, 384), BF16)),
    )
    block_out = (section_local.astype(F32) + jnp.sum(outs.astype(F32), axis=0)).astype(BF16)
    grad_kv = jnp.sum(dkvs.astype(F32), axis=0).astype(BF16)
    grad_proj = jnp.concatenate([grad_query, grad_kv], axis=1)
    normed_part = dot(grad_proj, head_full, ((1,), (1,)))
    spread_part = jnp.sum(normed_part * section, axis=-1) * (1.0 / 1536)
    spread_high = spread_part.astype(BF16)
    spread_low = (spread_part - spread_high.astype(F32)).astype(BF16)
    spread_pair = jnp.stack([spread_high, spread_low], axis=-1).reshape(2, 128, 2)
    spread_pair = jnp.broadcast_to(
        jnp.pad(spread_pair, ((0, 0), (0, 0), (0, 126)))[:, None], (2, 2, 128, 128)
    ).reshape(4, 128, 128)
    normed_halves = normed.reshape(256, 2, 768).transpose(1, 0, 2)
    cot_halves = cot_full.reshape(256, 2, 768).transpose(1, 0, 2)
    gpa = jnp.concatenate([grad_proj, attended], axis=1)
    norms, spreads, normed_other, cot_other, gpa_other = communicate(
        norm_kernel, "norm", 6,
        (shape(4, 128, 768), shape(4, 128, 128), shape(256, 768), shape(256, 768), shape(256, 768)), 12, 2,
        blocks(normed_part.astype(BF16)), spread_pair, normed_halves, cot_halves, gpa,
    )
    grad_normed = jnp.sum(norms.astype(F32), axis=0)
    spread = jnp.sum(spreads.astype(F32), axis=(0, 2))[:, None]
    inverse_here = lax.dynamic_slice_in_dim(inverse, 128 * p.zh, 128, 0)
    grad_section = (
        cot.astype(F32)
        + inverse_here * grad_normed
        - inverse_here**3 * section_local.astype(F32) * spread
    )
    grad_pool = (0.5 * grad_section).astype(BF16)
    normed_mine = lax.dynamic_index_in_dim(normed_halves, p.c, 0, False)
    cot_mine = lax.dynamic_index_in_dim(cot_halves, p.c, 0, False)
    rows = ((0,), (0,))
    head_part = dot(normed_mine, gpa[:, :576], rows) + dot(normed_other, gpa_other[:, :576], rows)
    output_part = dot(cot_mine, gpa[:, 576:], rows) + dot(cot_other, gpa_other[:, 576:], rows)
    hg = jnp.concatenate([head_part, output_part], axis=1).astype(BF16)
    hg = hg.reshape(8, 4, 24, 768).transpose(1, 0, 2, 3)
    gps, hgs = communicate(
        pool_kernel, "pool", 7, (shape(8, 128, 384), shape(4, 8, 24, 768)), 12, 2,
        grad_pool.reshape(128, 2, 384).transpose(1, 0, 2), hg,
    )
    hg_sum = jnp.sum(hgs.astype(F32), axis=0).astype(BF16)
    pool_mine = lax.dynamic_slice_in_dim(gps, 4 * p.c, 4, 0).reshape(512, 384)
    pool_other = lax.dynamic_slice_in_dim(gps, 4 - 4 * p.c, 4, 0).reshape(512, 384)
    across = ((1,), (0,))
    cg = (dot(x5, pool_mine, across) + dot(x5s, pool_other, across)).astype(BF16)
    cg = cg.reshape(5, 2, 2, 4, 20, 384).transpose(1, 2, 3, 0, 4, 5).reshape(2, 2, 4, 100, 384)
    hgl, cgl = communicate(
        last_kernel, "last", 8, (shape(2, 4, 24, 768), shape(16, 100, 384)), 24, 4,
        hg_sum.reshape(4, 2, 24, 768), cg,
    )
    conv_grad = jnp.sum(cgl.astype(F32).reshape(2, 2, 4, 5, 20, 384), axis=(0, 2))
    conv_grad = conv_grad.transpose(2, 1, 0, 3).reshape(20, 5, 768)
    both = jnp.sum(hgl.astype(F32), axis=1).reshape(2, 24, 4, 192)
    both = both.transpose(1, 2, 0, 3).reshape(24, 4, 384)
    return (block_out[None], conv_grad, both[:, :3], both[:, 3])


def solution(mesh):
    placed = (
        P("dp", "seq", None),
        P("seq", None, "tensor"),
        P("seq", None, "tensor"),
        P("seq", "tensor"),
        P("dp", "seq", "tensor"),
    )
    return jax.shard_map(
        local,
        mesh=mesh,
        in_specs=placed,
        out_specs=(
            P("dp", "seq", "tensor"),
            P(("seq", "dp"), None, "tensor"),
            P(("seq", "dp"), None, "tensor"),
            P(("seq", "dp"), "tensor"),
        ),
        check_vma=False,
    )
```

```python
import jax
import jax.numpy as jnp
from jax import lax
from jax.experimental import pallas as pl
from jax.experimental.pallas import tpu as pltpu
from jax.sharding import PartitionSpec as P

HEAD_DIM = 192
EPSILON = 1e-06
MESH = pl.DeviceIdType.MESH
BF16 = jnp.bfloat16
F32 = jnp.float32


class Place:
    def __init__(self):
        self.s = lax.axis_index("seq")
        self.zh = lax.div(self.s, 8)
        self.x = lax.rem(lax.div(self.s, 2), 4)
        self.c = lax.rem(self.s, 2)
        self.t = lax.axis_index("tensor")
        self.d = lax.axis_index("dp")
        self.z = 2 * self.zh + self.t

    def at(self, x=None, zh=None, c=None, t=None, d=None):
        x = self.x if x is None else x
        zh = self.zh if zh is None else zh
        c = self.c if c is None else c
        return {
            "seq": zh * 8 + x * 2 + c,
            "tensor": self.t if t is None else t,
            "dp": self.d if d is None else d,
        }

    def along_x(self, k):
        return lax.rem(self.x + k, 4)

    def along_y(self, k):
        return lax.rem(self.d + k, 4)

    def along_z(self, k):
        return lax.rem(self.z + k, 4)

    def at_z(self, z):
        return self.at(zh=lax.div(z, 2), t=lax.rem(z, 2))

    @property
    def sibling(self):
        return self.at(c=1 - self.c)


def remote(src, dst, send, recv, target):
    return pltpu.make_async_remote_copy(
        src_ref=src, dst_ref=dst, send_sem=send, recv_sem=recv, device_id=target, device_id_type=MESH
    )


def greet(targets):
    barrier = pltpu.get_barrier_semaphore()
    for condition, target in targets:
        if condition is None:
            pl.semaphore_signal(barrier, inc=1, device_id=target, device_id_type=MESH)
        else:

            @pl.when(condition)
            def _(target=target):
                pl.semaphore_signal(barrier, inc=1, device_id=target, device_id_type=MESH)

    return barrier


def under(condition, action):
    if condition is None:
        action()
    else:

        @pl.when(condition)
        def _():
            action()


def communicate(kernel, name, collective, outputs, remotes, locals_, *operands, aliases=None, vmem=(), scratch=()):
    anywhere = pl.BlockSpec(memory_space=pl.ANY)
    inside = pl.BlockSpec(memory_space=pltpu.VMEM)
    return pl.pallas_call(
        kernel,
        name=name,
        out_shape=outputs,
        in_specs=[inside if n in vmem else anywhere for n in range(len(operands))],
        out_specs=tuple([anywhere] * len(outputs)),
        scratch_shapes=list(scratch)
        + [
            pltpu.SemaphoreType.DMA((remotes,)),
            pltpu.SemaphoreType.DMA((remotes,)),
            pltpu.SemaphoreType.DMA((locals_,)),
        ],
        input_output_aliases=aliases or {},
        compiler_params=pltpu.CompilerParams(
            collective_id=collective, has_side_effects=True, vmem_limit_bytes=16 * 1024 * 1024 if vmem else None
        ),
    )(*operands)


class Moves:
    def __init__(self, place, send, recv, local):
        self.place, self.send, self.recv, self.local = place, send, recv, local
        self.sends, self.receives, self.locals = [], [], []
        self.used = 0
        self.used_local = 0

    def slots(self, count):
        first = self.used
        self.used += count
        return first

    def push(self, src, dst, target, slot, recv_slot=None, when=None):
        recv_slot = slot if recv_slot is None else recv_slot
        copy = remote(src, dst, self.send.at[slot], self.recv.at[recv_slot], target)
        under(when, copy.start)
        self.sends.append((when, copy.wait_send))

    def keep(self, src, dst, when=None):
        copy = pltpu.make_async_copy(src, dst, self.local.at[self.used_local])
        self.used_local += 1
        under(when, copy.start)
        self.locals.append((when, copy.wait))

    def arrival(self, dst, slot, when=None):
        place = self.place
        copy = remote(dst, dst, self.send.at[0], self.recv.at[slot], place.at())
        return lambda: under(when, copy.wait_recv)

    def expect(self, dst, slot, when=None):
        self.receives.append(self.arrival(dst, slot, when))

    def settle(self):
        for wait in self.receives:
            wait()
        for when, wait in self.locals + self.sends:
            under(when, wait)


def z_ring(p):
    return [(None, p.at_z(p.along_z(k))) for k in range(1, 4)]


def y_ring(p):
    return [(None, p.at(d=p.along_y(k))) for k in range(1, 4)]


def last_kernel(hg_ref, cg_ref, hgs_ref, cgs_ref, send, recv, local):
    p = Place()
    peers = []
    for zh in range(2):
        for c in range(2):
            for k in range(4):
                here = k == 0
                target = p.at(zh=zh, c=c, d=p.along_y(k))
                peers.append((jnp.logical_or(zh != p.zh, c != p.c) if here else None, target))
    for zh in range(2):
        for k in range(1, 4):
            peers.append((None, p.at(zh=zh, x=p.along_x(k), c=p.zh)))
    barrier = greet(peers)
    pl.semaphore_wait(barrier, 15 + 6)
    moves = Moves(p, send, recv, local)
    b = moves.slots(16)
    me = 8 * p.zh + 4 * p.c + p.d
    for k in (8, 12, 4, 2, 10, 14, 6, 1, 3, 9, 11, 13, 15, 5, 7, 0):
        other = lax.rem(me + k, 16)
        zh, c, d = lax.div(other, 8), lax.rem(lax.div(other, 4), 2), lax.rem(other, 4)
        src = cg_ref.at[zh, c, d]
        if k == 0:
            moves.keep(src, cgs_ref.at[me])
        else:
            moves.push(src, cgs_ref.at[me], p.at(zh=zh, c=c, d=d), b + k)
            moves.expect(cgs_ref.at[lax.rem(me + 16 - k, 16)], b + k)
    a = moves.slots(8)
    for k in range(8):
        other = lax.rem(2 * p.x + k, 8)
        x, c = lax.div(other, 2), lax.rem(other, 2)
        src, dst = hg_ref.at[x, c], hgs_ref.at[p.zh, p.x]
        alone = jnp.logical_and(jnp.logical_and(x == p.x, c == p.c), p.zh == p.c)
        if k < 2:
            moves.push(src, dst, p.at(x=x, zh=p.c, c=c), a + k, a + 4 * p.zh + p.x, jnp.logical_not(alone))
            moves.keep(src, dst, alone)
        else:
            moves.push(src, dst, p.at(x=x, zh=p.c, c=c), a + k, a + 4 * p.zh + p.x)
    for zh in range(2):
        for x in range(4):
            alone = jnp.logical_and(jnp.logical_and(x == p.x, zh == p.zh), p.zh == p.c)
            moves.expect(hgs_ref.at[zh, x], a + 4 * zh + x, jnp.logical_not(alone))
    moves.settle()

def dot(a, b, dims):
    return lax.dot_general(a, b, (dims, ((), ())), preferred_element_type=F32)


NN = ((1,), (0,))
NT = ((1,), (1,))
TN = ((0,), (0,))


def main_kernel(
    at_ref, edge_ref, cw_ref, wp_ref, cot_ref,
    out_ref, hgo_ref, cg_ref,
    xt_ref, low_ref, high_ref, cwf_ref, wf_ref, cots_ref, x5_ref, x5s_ref, part_ref, rs_ref, sec_ref, secs_ref,
    inv_ref, nb_ref, nl_ref, cl_ref, kv_ref, st_ref, dp_ref, p16_ref, ds_ref, dkv_ref, buf_ref, sum_ref, dkvs_ref,
    bo_ref, bos_ref, gpa_ref, gpas_ref, norm_ref, norms_ref, spread_ref, spreads_ref, hg_ref, hgs_ref, gp_ref, gps_ref,
    send, recv, local,
):
    p = Place()
    scale = HEAD_DIM ** (-0.5)
    peers = [(None, {"seq": lax.rem(p.s + k, 16), "tensor": p.t, "dp": p.d}) for k in range(1, 16)]
    peers += [(None, p.at(t=1 - p.t)), (None, p.at(zh=1 - p.zh, t=1 - p.t))] + y_ring(p)
    barrier = greet(peers)
    pl.semaphore_wait(barrier, 20)
    moves = Moves(p, send, recv, local)
    arrival = moves.arrival

    first = moves.slots(4)
    mine = cwf_ref.at[:, 2 * p.zh + p.c]
    moves.push(cw_ref, mine, p.at(zh=1 - p.zh), first)
    moves.push(cw_ref, mine, p.sibling, first + 1)
    moves.keep(cw_ref, mine)
    from_z = cwf_ref.at[:, 2 * (1 - p.zh) + p.c]

    a = moves.slots(4)
    core = lax.div(p.x, 2)
    slot = 2 * lax.rem(p.x, 2) + p.c
    spot = xt_ref.at[slot]
    for k in (2, 1, 3, 0):
        x = p.along_x(k)
        if k == 0:
            moves.push(at_ref.at[x], spot, p.at(c=core), a, a + slot, core != p.c)
            moves.keep(at_ref.at[x], spot, core == p.c)
        else:
            moves.push(at_ref.at[x], spot, p.at(x=x, c=core), a + k, a + slot)
    base = 8 * p.zh + 4 * p.c
    halo = []
    for up, end_ref in ((True, low_ref), (False, high_ref)):
        e = moves.slots(4)
        if up:
            sends = jnp.logical_and(lax.rem(p.s, 4) == 3, p.s != 15)
            block = lax.rem(p.s + 1, 16)
        else:
            sends = jnp.logical_and(lax.rem(p.s, 4) == 0, p.s != 0)
            block = lax.rem(p.s + 15, 16)
        zh, c = lax.div(block, 8), lax.div(lax.rem(block, 8), 4)
        for k in range(4):
            x = p.along_x(k)
            src = edge_ref.at[1 if up else 0, x]
            target = p.at(x=x, zh=zh, c=c)
            if k == 0:
                alone = jnp.logical_and(zh == p.zh, c == p.c)
                moves.push(src, end_ref, target, e, e, jnp.logical_and(sends, jnp.logical_not(alone)))
                moves.keep(src, end_ref, jnp.logical_and(sends, alone))
            else:
                moves.push(src, end_ref, target, e + k, e, sends)
        if up:
            halo.append(arrival(end_ref, e, jnp.logical_and(base != 0, base - 1 != p.s)))
        else:
            halo.append(arrival(end_ref, e, jnp.logical_and(base != 12, base + 4 != p.s)))

    def quarter(zh, x, c, d):
        rows = pl.ds(pl.multiple_of(48 * lax.div(d, 2), 16), 48)
        columns = pl.ds(pl.multiple_of(384 * lax.rem(d, 2), 128), 384)
        return wf_ref.at[zh, x, c, rows, columns]

    def quarters(c, d):
        rows = pl.ds(pl.multiple_of(48 * lax.div(d, 2), 16), 48)
        columns = pl.ds(pl.multiple_of(384 * lax.rem(d, 2), 128), 384)
        return wf_ref.at[:, :, c, rows, columns]

    w = moves.slots(8)
    shard = 4 * p.zh + p.x
    own_quarter = quarter(p.zh, p.x, p.c, p.d)
    quarter_arrivals = []
    for k in range(8):
        other = lax.rem(shard + k, 8)
        zh, x = lax.div(other, 4), lax.rem(other, 4)
        src = wp_ref.at[zh, p.d]
        if k == 0:
            copy = pltpu.make_async_copy(src, own_quarter, local.at[moves.used_local])
            moves.used_local += 1
            copy.start()
            quarter_arrivals.append(copy.wait)
        else:
            moves.push(src, own_quarter, p.at(x=x, zh=zh), w + k)
            other = lax.rem(shard + 8 - k, 8)
            quarter_arrivals.append(arrival(quarter(lax.div(other, 4), lax.rem(other, 4), p.c, p.d), w + k))

    cot_first = moves.slots(4)
    cot_own = pltpu.make_async_copy(cot_ref, cots_ref.at[p.z], local.at[moves.used_local])
    moves.used_local += 1
    cot_own.start()
    cot_arrivals = [cot_own.wait]
    for k in (2, 1, 3):
        moves.push(cot_ref, cots_ref.at[p.z], p.at_z(p.along_z(k)), cot_first + k)
        cot_arrivals.append(arrival(cots_ref.at[p.along_z(4 - k)], cot_first + k))

    arrival(from_z, first)()
    moves.push(from_z, from_z, p.sibling, first + 2)
    for wait in quarter_arrivals:
        wait()
    y = moves.slots(8)
    moves.push(quarters(p.c, p.d), quarters(p.c, p.d), p.sibling, y)
    for k in (2, 1, 3):
        moves.push(quarters(p.c, p.d), quarters(p.c, p.d), p.at(d=p.along_y(k)), y + k)

    for n in range(4):
        x, c = 2 * p.c + n // 2, n % 2
        arrival(xt_ref.at[n], a + n, jnp.logical_or(x != p.x, c != p.c))()
    for wait in halo:
        wait()
    for when, wait in moves.locals:
        under(when, wait)
    moves.locals = []
    pick = (lax.broadcasted_iota(jnp.int32, (16, 128), 0) == lax.broadcasted_iota(jnp.int32, (16, 128), 1)).astype(BF16)
    zero_rows = jnp.zeros((16, 384), BF16)
    low = dot(jnp.where(base != 0, low_ref[...], zero_rows), pick, TN)[:320]
    high = dot(jnp.where(base != 12, high_ref[...], zero_rows), pick, TN)[:320]
    even = jnp.concatenate([xt_ref[n, 0] for n in range(4)], axis=1).astype(F32)
    odd = jnp.concatenate([xt_ref[n, 1] for n in range(4)], axis=1).astype(F32)
    lane = lax.broadcasted_iota(jnp.int32, (320, 512), 1)
    both = even + odd
    x5_ref[pl.ds(640, 320), :] = both.astype(BF16)
    x5_ref[pl.ds(0, 320), :] = jnp.where(lane == 0, low[:, 0:1] + low[:, 1:2], pltpu.roll(both, 1, 1)).astype(BF16)
    x5_ref[pl.ds(1280, 320), :] = jnp.where(
        lane == 511, high[:, 0:1] + high[:, 1:2], pltpu.roll(both, 511, 1)
    ).astype(BF16)
    x5_ref[pl.ds(320, 320), :] = (even + jnp.where(lane == 0, low[:, 1:2], pltpu.roll(odd, 1, 1))).astype(BF16)
    x5_ref[pl.ds(960, 320), :] = (odd + jnp.where(lane == 511, high[:, 0:1], pltpu.roll(even, 511, 1))).astype(BF16)
    arrival(cwf_ref.at[:, 2 * p.zh + 1 - p.c], first + 1)()
    arrival(cwf_ref.at[:, 2 * (1 - p.zh) + 1 - p.c], first + 2)()
    b = moves.slots(4)
    for half in range(2):
        conv = dot(x5_ref[:, 256 * half : 256 * half + 256], cwf_ref[...].reshape(1600, 768), TN) * 0.5
        for n in range(2):
            slot = 2 * half + n
            part_ref[slot] = conv[128 * n : 128 * n + 128].astype(BF16)
            x = 2 * p.c + half
            alone = jnp.logical_and(x == p.x, n == p.c)
            moves.push(part_ref.at[slot], rs_ref.at[p.x], p.at(x=x, c=n), b + slot, b + p.x, jnp.logical_not(alone))
            moves.keep(part_ref.at[slot], rs_ref.at[p.x], alone)
    other_x5 = moves.slots(1)
    moves.push(x5_ref, x5s_ref, p.sibling, other_x5)
    for x in range(4):
        arrival(rs_ref.at[x], b + x, jnp.logical_or(p.x != x, core != p.c))()
    for when, wait in moves.locals:
        under(when, wait)
    moves.locals = []
    total = rs_ref[0].astype(F32)
    for x in range(1, 4):
        total = total + rs_ref[x].astype(F32)
    sec_ref[...] = total.astype(BF16)
    secs_ref[p.z] = total.astype(BF16)
    g = moves.slots(4)
    for k in (2, 1, 3):
        moves.push(sec_ref, secs_ref.at[p.z], p.at_z(p.along_z(k)), g + k)

    for k in (1, 3, 2):
        d = p.along_y(4 - k)
        arrival(quarters(p.c, d), y + k)()
        moves.push(quarters(p.c, d), quarters(p.c, d), p.sibling, y + 3 + k)
    for wait in cot_arrivals:
        wait()
    o = moves.slots(4)
    for zh in range(2):
        cl_ref[zh] = cots_ref[2 * zh + p.c]
        moves.push(cots_ref.at[2 * zh + 1 - p.c], cl_ref.at[2 + zh], p.sibling, o + zh)
    arrival(quarters(1 - p.c, p.d), y)()
    for k in (1, 3, 2):
        arrival(quarters(1 - p.c, p.along_y(4 - k)), y + 3 + k)()

    def kv_rows(zh):
        return wf_ref[zh, :, :, :, :640].reshape(768, 640)

    def output_rows(zh):
        return wf_ref[zh, :, :, :, 512:].reshape(768, 256)

    def channels(ref, t):
        return jnp.concatenate([ref[t], ref[2 + t]], axis=0)

    wide_lane = lax.broadcasted_iota(jnp.int32, (256, 256), 1)
    grad_att = dot(channels(cots_ref, 0), output_rows(0), NN) + dot(channels(cots_ref, 1), output_rows(1), NN)
    grad_att = jnp.where(wide_lane < 64, 0.0, grad_att).astype(BF16)

    for k in (2, 1, 3):
        arrival(secs_ref.at[p.along_z(4 - k)], g + k)()
    for zh in range(2):
        left, right = secs_ref[2 * zh].astype(F32), secs_ref[2 * zh + 1].astype(F32)
        squares = jnp.sum(left * left, axis=1, keepdims=True) + jnp.sum(right * right, axis=1, keepdims=True)
        inverse = lax.rsqrt(squares * (1.0 / 1536) + EPSILON)
        inv_ref[zh] = jnp.broadcast_to(inverse, (128, 128))
        nb_ref[2 * zh] = (left * inverse).astype(BF16)
        nb_ref[2 * zh + 1] = (right * inverse).astype(BF16)
    projected = dot(channels(nb_ref, 0), kv_rows(0), NN) + dot(channels(nb_ref, 1), kv_rows(1), NN)
    kv_ref[p.c, p.x] = projected[:, :384].astype(BF16)
    query = jnp.where(wide_lane < 192, projected[:, 384:], 0.0).astype(BF16)
    q = moves.slots(8)
    mine = kv_ref.at[p.c, p.x]
    for k in (2, 1, 3):
        moves.push(mine, mine, p.at(x=p.along_x(k)), q + k)
    moves.push(mine, mine, p.sibling, q)
    for zh in range(2):
        nl_ref[zh] = nb_ref[2 * zh + p.c]
        moves.push(nb_ref.at[2 * zh + 1 - p.c], nl_ref.at[2 + zh], p.sibling, o + 2 + zh)
    for k in (1, 3, 2):
        spot = kv_ref.at[p.c, p.along_x(4 - k)]
        arrival(spot, q + k)()
        moves.push(spot, spot, p.sibling, q + 3 + k)
    arrival(kv_ref.at[1 - p.c, p.x], q)()
    for k in (1, 3, 2):
        arrival(kv_ref.at[1 - p.c, p.along_x(4 - k)], q + 3 + k)()

    highest = None
    for n in range(8):
        scores = dot(kv_ref[n // 4, n % 4, :, :256], query, NT) * scale
        st_ref[n] = scores
        top = jnp.max(scores, axis=0, keepdims=True)
        highest = top if highest is None else jnp.maximum(highest, top)
    sums = jnp.zeros((1, 256), F32)
    for n in range(8):
        unnormed = jnp.exp(st_ref[n] - highest)
        st_ref[n] = unnormed
        sums = sums + jnp.sum(unnormed, axis=0, keepdims=True)
    share = 1.0 / sums
    centre = jnp.zeros((1, 256), F32)
    for n in range(8):
        weights = st_ref[n] * share
        grad_prob = dot(kv_ref[n // 4, n % 4, :, 128:], grad_att, NT)
        centre = centre + jnp.sum(weights * grad_prob, axis=0, keepdims=True)
        st_ref[n] = weights
        dp_ref[n] = grad_prob
        p16_ref[n] = weights.astype(BF16)
    r = moves.slots(8)

    def key_grads(c, x):
        n = 4 * c + x
        grad_score = (st_ref[n] * (dp_ref[n] - centre)).astype(BF16)
        ds_ref[n] = grad_score
        keys = dot(grad_score, query, NN) * scale
        values = dot(p16_ref[n], grad_att, NN)
        return jnp.concatenate([keys[:, :128], keys[:, 128:] + values[:, :128], values[:, 128:]], axis=1)

    for k in (2, 1, 3, 0):
        dkv_ref[k] = key_grads(1 - p.c, p.along_x(k)).astype(BF16)
        moves.push(dkv_ref.at[k], buf_ref.at[k], p.sibling, r + k)
    for k in (2, 1, 3, 0):
        x = p.along_x(k)
        here = key_grads(p.c, x)
        arrival(buf_ref.at[k], r + k)()
        sum_ref[k] = (here + buf_ref[k].astype(F32)).astype(BF16)
        if k:
            moves.push(sum_ref.at[k], dkvs_ref.at[p.x], p.at(x=x), r + 4 + k)
    dkvs_ref[p.x] = sum_ref[0]

    def rows8(ref, first, last):
        return ref[:, :, :, first:last].reshape(2048, last - first)

    attended = dot(p16_ref[...].reshape(2048, 256), rows8(kv_ref, 128, 384), TN)
    attended = jnp.where(wide_lane < 64, 0.0, attended).astype(BF16)
    grad_query = dot(ds_ref[...].reshape(2048, 256), rows8(kv_ref, 0, 256), TN) * scale
    grad_query = jnp.where(wide_lane < 192, grad_query, 0.0).astype(BF16)
    gpa_ref[:, 384:512] = grad_query[:, :128]
    gpa_ref[:, 512:640] = grad_query[:, 128:] + attended[:, :128]
    gpa_ref[:, 640:] = attended[:, 128:]
    u = moves.slots(4)
    for t in range(2):
        block = dot(attended, output_rows(t), NT).astype(BF16)
        bo_ref[t] = block[:128]
        bo_ref[2 + t] = block[128:]
    for k in (2, 1, 3):
        z = p.along_z(k)
        moves.push(bo_ref.at[z], bos_ref.at[p.z], p.at_z(z), u + k)
    bos_ref[p.z] = bo_ref[p.z]

    for k in (1, 3, 2):
        arrival(dkvs_ref.at[p.along_x(4 - k)], r + 4 + k)()
    total = dkvs_ref[0].astype(F32)
    for x in range(1, 4):
        total = total + dkvs_ref[x].astype(F32)
    grad_kv = total.astype(BF16)
    gpa_ref[:, :384] = grad_kv
    h = moves.slots(5)
    moves.push(gpa_ref, gpas_ref, p.sibling, h)
    grad_proj = jnp.concatenate([grad_kv, grad_query], axis=1)
    spread = jnp.zeros((256, 1), F32)
    for t in range(2):
        block = dot(grad_proj, kv_rows(t), NT)
        spread = spread + jnp.sum(block * channels(secs_ref, t).astype(F32), axis=1, keepdims=True)
        rounded = block.astype(BF16)
        norm_ref[t] = rounded[:128]
        norm_ref[2 + t] = rounded[128:]
    spread = spread * (1.0 / 1536)
    for zh in range(2):
        spread_ref[zh] = jnp.broadcast_to(spread[128 * zh : 128 * zh + 128], (128, 128))
    m = moves.slots(8)
    for k in (2, 1, 3):
        z = p.along_z(k)
        moves.push(norm_ref.at[z], norms_ref.at[p.z], p.at_z(z), m + k)
        moves.push(spread_ref.at[lax.div(z, 2)], spreads_ref.at[p.z], p.at_z(z), m + 4 + k)
    norms_ref[p.z] = norm_ref[p.z]
    spreads_ref[p.z] = spread_ref[p.zh]

    for n in range(4):
        arrival((cl_ref if n < 2 else nl_ref).at[2 + n % 2], o + n)()
    arrival(gpas_ref, h)()
    grads = jnp.concatenate([gpa_ref[...], gpas_ref[...]], axis=0)
    head_part = dot(nl_ref[...].reshape(512, 768), grads[:, :640], TN)
    output_part = dot(cl_ref[...].reshape(512, 768), grads[:, 512:], TN)
    tile_lane = lax.broadcasted_iota(jnp.int32, (768, 128), 1)
    middle = jnp.where(tile_lane < 64, head_part[:, 512:], output_part[:, :128])
    parts = jnp.concatenate([head_part[:, :512], middle, output_part[:, 128:]], axis=1)
    for n in range(8):
        for d in range(4):
            row = 96 * n + 24 * d
            hg_ref[d, n] = parts[row : row + 24].astype(BF16)
    for k in (2, 1, 3):
        d = p.along_y(k)
        moves.push(hg_ref.at[d], hgs_ref.at[p.d], p.at(d=d), h + 1 + k)
    hgs_ref[p.d] = hg_ref[p.d]

    for k in (1, 3, 2):
        arrival(bos_ref.at[p.along_z(4 - k)], u + k)()
    total = sec_ref[...].astype(F32)
    projected_out = bos_ref[0].astype(F32)
    for z in range(1, 4):
        projected_out = projected_out + bos_ref[z].astype(F32)
    out_ref[...] = (total + projected_out).astype(BF16)

    for k in (1, 3, 2):
        arrival(norms_ref.at[p.along_z(4 - k)], m + k)()
        arrival(spreads_ref.at[p.along_z(4 - k)], m + 4 + k)()
    grad_normed = norms_ref[0].astype(F32)
    mean = spreads_ref[0]
    for z in range(1, 4):
        grad_normed = grad_normed + norms_ref[z].astype(F32)
        mean = mean + spreads_ref[z]
    inverse = inv_ref[p.zh][:, :1]
    grad_section = cots_ref[p.z].astype(F32) + inverse * grad_normed - inverse * inverse * inverse * total * mean[:, :1]
    grad_pool = (0.5 * grad_section).astype(BF16)
    gp_ref[0] = grad_pool[:, :384]
    gp_ref[1] = grad_pool[:, 384:]
    j = moves.slots(8)
    block = 2 * p.x + p.c
    for k in (4, 5, 2, 3, 6, 7, 1):
        other = lax.rem(block + k, 8)
        x, c = lax.div(other, 2), lax.rem(other, 2)
        moves.push(gp_ref.at[c], gps_ref.at[block], p.at(x=x, c=c), j + k)
    gps_ref[block] = gp_ref[p.c]
    for k in (1, 3, 2):
        arrival(hgs_ref.at[p.along_y(4 - k)], h + 1 + k)()
    rows = hgs_ref[0].astype(F32)
    for d in range(1, 4):
        rows = rows + hgs_ref[d].astype(F32)
    hgo_ref[...] = rows.astype(BF16)

    arrival(x5s_ref, other_x5)()
    for k in (1, 7, 6, 2, 3, 4, 5):
        arrival(gps_ref.at[lax.rem(block + 8 - k, 8)], j + k)()
    here = gps_ref[pl.ds(4 * p.c, 4)].reshape(512, 384)
    there = gps_ref[pl.ds(4 - 4 * p.c, 4)].reshape(512, 384)
    cg_ref[...] = (dot(x5_ref[...], here, NN) + dot(x5s_ref[...], there, NN)).astype(BF16)
    moves.settle()


def main_call(at, edges, cw, wp, cot):
    anywhere = pl.BlockSpec(memory_space=pl.ANY)
    inside = pl.BlockSpec(memory_space=pltpu.VMEM)

    def vmem(*dims, dtype=BF16):
        return pltpu.VMEM(dims, dtype)

    scratch = [
        vmem(4, 2, 320, 128), vmem(16, 384), vmem(16, 384), vmem(5, 4, 80, 768), vmem(2, 4, 2, 96, 768),
        vmem(4, 128, 768), vmem(1600, 512), vmem(1600, 512), vmem(4, 128, 768), vmem(4, 128, 768),
        vmem(128, 768), vmem(4, 128, 768),
        vmem(2, 128, 128, dtype=F32), vmem(4, 128, 768), vmem(4, 128, 768), vmem(4, 128, 768),
        vmem(2, 4, 256, 384), vmem(8, 256, 256, dtype=F32), vmem(8, 256, 256, dtype=F32),
        vmem(8, 256, 256), vmem(8, 256, 256), vmem(4, 256, 384), vmem(4, 256, 384), vmem(4, 256, 384),
        vmem(4, 256, 384),
        vmem(4, 128, 768), vmem(4, 128, 768), vmem(256, 768), vmem(256, 768), vmem(4, 128, 768), vmem(4, 128, 768),
        vmem(2, 128, 128, dtype=F32), vmem(4, 128, 128, dtype=F32),
        vmem(4, 8, 24, 768), vmem(4, 8, 24, 768), vmem(2, 128, 384), vmem(8, 128, 384),
        pltpu.SemaphoreType.DMA((112,)), pltpu.SemaphoreType.DMA((112,)), pltpu.SemaphoreType.DMA((12,)),
    ]
    return pl.pallas_call(
        main_kernel,
        name="main",
        out_shape=(shape(128, 768), shape(8, 24, 768), shape(1600, 384)),
        in_specs=[anywhere] * 5,
        out_specs=(inside,) * 3,
        scratch_shapes=scratch,
        compiler_params=pltpu.CompilerParams(
            collective_id=1, has_side_effects=True, vmem_limit_bytes=60 * 1024 * 1024
        ),
    )(at, edges, cw, wp, cot)


def shape(*dims):
    return jax.ShapeDtypeStruct(dims, BF16)


def local(section_input, conv_weight, head_weight, output_weight, cotangent):
    activity = jax.nn.gelu(section_input[0].astype(F32), approximate=True).astype(BF16)
    bins = activity.reshape(128, 2, 2, 4, 160)
    at = bins.transpose(3, 1, 2, 4, 0).reshape(4, 2, 320, 128)
    edges = jnp.stack([bins[0], bins[127]]).transpose(0, 3, 1, 2, 4).reshape(2, 4, 2, 320)
    edges = jnp.pad(edges, ((0, 0), (0, 0), (0, 14), (0, 64)))
    cw = conv_weight.transpose(1, 0, 2)
    heads = head_weight.reshape(96, 3, 2, 192)
    wp = jnp.stack([heads[:, 1], heads[:, 2], heads[:, 0], output_weight.reshape(96, 2, 192)], axis=2)
    wp = wp.reshape(2, 48, 2, 2, 384).transpose(2, 0, 3, 1, 4).reshape(2, 4, 48, 384)
    block_out, hg_sum, cg = main_call(at, edges, cw, wp, cotangent[0])
    cg = cg.reshape(5, 2, 2, 4, 20, 384).transpose(1, 2, 3, 0, 4, 5).reshape(2, 2, 4, 100, 384)
    hgl, cgl = communicate(
        last_kernel, "last", 8, (shape(2, 4, 24, 768), shape(16, 100, 384)), 24, 4,
        hg_sum.reshape(4, 2, 24, 768), cg,
    )
    conv_grad = jnp.sum(cgl.astype(F32).reshape(2, 2, 4, 5, 20, 384), axis=(0, 2))
    conv_grad = conv_grad.transpose(2, 1, 0, 3).reshape(20, 5, 768)
    both = jnp.sum(hgl.astype(F32), axis=1).reshape(2, 24, 4, 192)
    both = both.transpose(1, 2, 0, 3).reshape(24, 4, 384)
    head_grad = jnp.stack([both[:, 2], both[:, 0], both[:, 1]], axis=1)
    return (block_out[None], conv_grad, head_grad, both[:, 3])


def solution(mesh):
    placed = (
        P("dp", "seq", None),
        P("seq", None, "tensor"),
        P("seq", None, "tensor"),
        P("seq", "tensor"),
        P("dp", "seq", "tensor"),
    )
    return jax.shard_map(
        local,
        mesh=mesh,
        in_specs=placed,
        out_specs=(
            P("dp", "seq", "tensor"),
            P(("seq", "dp"), None, "tensor"),
            P(("seq", "dp"), None, "tensor"),
            P(("seq", "dp"), "tensor"),
        ),
        check_vma=False,
    )
```

```python
import jax
import jax.numpy as jnp
from jax import lax
from jax.experimental import pallas as pl
from jax.experimental.pallas import tpu as pltpu
from jax.sharding import PartitionSpec as P

HEAD_DIM = 192
EPSILON = 1e-06
MESH = pl.DeviceIdType.MESH
BF16 = jnp.bfloat16
F32 = jnp.float32


class Place:
    def __init__(self):
        self.s = lax.axis_index("seq")
        self.zh = lax.div(self.s, 8)
        self.x = lax.rem(lax.div(self.s, 2), 4)
        self.c = lax.rem(self.s, 2)
        self.t = lax.axis_index("tensor")
        self.d = lax.axis_index("dp")
        self.z = 2 * self.zh + self.t

    def at(self, x=None, zh=None, c=None, t=None, d=None):
        x = self.x if x is None else x
        zh = self.zh if zh is None else zh
        c = self.c if c is None else c
        return {
            "seq": zh * 8 + x * 2 + c,
            "tensor": self.t if t is None else t,
            "dp": self.d if d is None else d,
        }

    def along_x(self, k):
        return lax.rem(self.x + k, 4)

    def along_y(self, k):
        return lax.rem(self.d + k, 4)

    def along_z(self, k):
        return lax.rem(self.z + k, 4)

    def at_z(self, z):
        return self.at(zh=lax.div(z, 2), t=lax.rem(z, 2))

    @property
    def sibling(self):
        return self.at(c=1 - self.c)


def remote(src, dst, send, recv, target):
    return pltpu.make_async_remote_copy(
        src_ref=src, dst_ref=dst, send_sem=send, recv_sem=recv, device_id=target, device_id_type=MESH
    )


def greet(targets):
    barrier = pltpu.get_barrier_semaphore()
    for condition, target in targets:
        if condition is None:
            pl.semaphore_signal(barrier, inc=1, device_id=target, device_id_type=MESH)
        else:

            @pl.when(condition)
            def _(target=target):
                pl.semaphore_signal(barrier, inc=1, device_id=target, device_id_type=MESH)

    return barrier


def under(condition, action):
    if condition is None:
        action()
    else:

        @pl.when(condition)
        def _():
            action()


class Moves:
    def __init__(self, place, send, recv, local):
        self.place, self.send, self.recv, self.local = place, send, recv, local
        self.sends, self.receives, self.locals = [], [], []
        self.used = 0
        self.used_local = 0

    def slots(self, count):
        first = self.used
        self.used += count
        return first

    def push(self, src, dst, target, slot, recv_slot=None, when=None):
        recv_slot = slot if recv_slot is None else recv_slot
        copy = remote(src, dst, self.send.at[slot], self.recv.at[recv_slot], target)
        under(when, copy.start)
        self.sends.append((when, copy.wait_send))

    def keep(self, src, dst, when=None):
        copy = pltpu.make_async_copy(src, dst, self.local.at[self.used_local])
        self.used_local += 1
        under(when, copy.start)
        self.locals.append((when, copy.wait))

    def arrival(self, dst, slot, when=None):
        place = self.place
        copy = remote(dst, dst, self.send.at[0], self.recv.at[slot], place.at())
        return lambda: under(when, copy.wait_recv)

    def expect(self, dst, slot, when=None):
        self.receives.append(self.arrival(dst, slot, when))

    def settle(self):
        for wait in self.receives:
            wait()
        for when, wait in self.locals + self.sends:
            under(when, wait)


def z_ring(p):
    return [(None, p.at_z(p.along_z(k))) for k in range(1, 4)]


def y_ring(p):
    return [(None, p.at(d=p.along_y(k))) for k in range(1, 4)]


def dot(a, b, dims):
    return lax.dot_general(a, b, (dims, ((), ())), preferred_element_type=F32)


NN = ((1,), (0,))
NT = ((1,), (1,))
TN = ((0,), (0,))


def main_kernel(
    at_ref, edge_ref, cw_ref, wp_ref, cot_ref,
    out_ref, conv_ref, head_ref, output_ref,
    xt_ref, low_ref, high_ref, cwf_ref, wf_ref, cots_ref, x5_ref, x5s_ref, part_ref, rs_ref, sec_ref, secs_ref,
    inv_ref, nb_ref, nl_ref, cl_ref, kv_ref, st_ref, dp_ref, p16_ref, ds_ref, dkv_ref, buf_ref, sum_ref, dkvs_ref,
    bo_ref, bos_ref, gpa_ref, gpas_ref, norm_ref, norms_ref, spread_ref, spreads_ref, hg_ref, hgs_ref, gp_ref, gps_ref,
    hgo_ref, hgl_ref, cgf_ref, cgm_ref, cg_ref, cgs_ref, send, recv, local,
):
    p = Place()
    scale = HEAD_DIM ** (-0.5)
    peers = [(None, {"seq": lax.rem(p.s + k, 16), "tensor": p.t, "dp": p.d}) for k in range(1, 16)]
    peers += [(None, p.at(t=1 - p.t)), (None, p.at(zh=1 - p.zh, t=1 - p.t))]
    for zh in range(2):
        for c in range(2):
            peers += [(None, p.at(zh=zh, c=c, d=p.along_y(k))) for k in range(1, 4)]
    barrier = greet(peers)
    pl.semaphore_wait(barrier, 29)
    moves = Moves(p, send, recv, local)
    arrival = moves.arrival

    first = moves.slots(4)
    mine = cwf_ref.at[:, 2 * p.zh + p.c]
    moves.push(cw_ref, mine, p.at(zh=1 - p.zh), first)
    moves.push(cw_ref, mine, p.sibling, first + 1)
    moves.keep(cw_ref, mine)
    from_z = cwf_ref.at[:, 2 * (1 - p.zh) + p.c]

    a = moves.slots(4)
    core = lax.div(p.x, 2)
    slot = 2 * lax.rem(p.x, 2) + p.c
    spot = xt_ref.at[slot]
    for k in (2, 1, 3, 0):
        x = p.along_x(k)
        if k == 0:
            moves.push(at_ref.at[x], spot, p.at(c=core), a, a + slot, core != p.c)
            moves.keep(at_ref.at[x], spot, core == p.c)
        else:
            moves.push(at_ref.at[x], spot, p.at(x=x, c=core), a + k, a + slot)
    base = 8 * p.zh + 4 * p.c
    halo = []
    for up, end_ref in ((True, low_ref), (False, high_ref)):
        e = moves.slots(4)
        if up:
            sends = jnp.logical_and(lax.rem(p.s, 4) == 3, p.s != 15)
            block = lax.rem(p.s + 1, 16)
        else:
            sends = jnp.logical_and(lax.rem(p.s, 4) == 0, p.s != 0)
            block = lax.rem(p.s + 15, 16)
        zh, c = lax.div(block, 8), lax.div(lax.rem(block, 8), 4)
        for k in range(4):
            x = p.along_x(k)
            src = edge_ref.at[1 if up else 0, x]
            target = p.at(x=x, zh=zh, c=c)
            if k == 0:
                alone = jnp.logical_and(zh == p.zh, c == p.c)
                moves.push(src, end_ref, target, e, e, jnp.logical_and(sends, jnp.logical_not(alone)))
                moves.keep(src, end_ref, jnp.logical_and(sends, alone))
            else:
                moves.push(src, end_ref, target, e + k, e, sends)
        if up:
            halo.append(arrival(end_ref, e, jnp.logical_and(base != 0, base - 1 != p.s)))
        else:
            halo.append(arrival(end_ref, e, jnp.logical_and(base != 12, base + 4 != p.s)))

    def quarter(zh, x, c, d):
        rows = pl.ds(pl.multiple_of(48 * lax.div(d, 2), 16), 48)
        columns = pl.ds(pl.multiple_of(384 * lax.rem(d, 2), 128), 384)
        return wf_ref.at[zh, x, c, rows, columns]

    def quarters(c, d):
        rows = pl.ds(pl.multiple_of(48 * lax.div(d, 2), 16), 48)
        columns = pl.ds(pl.multiple_of(384 * lax.rem(d, 2), 128), 384)
        return wf_ref.at[:, :, c, rows, columns]

    w = moves.slots(8)
    shard = 4 * p.zh + p.x
    own_quarter = quarter(p.zh, p.x, p.c, p.d)
    quarter_arrivals = []
    for k in range(8):
        other = lax.rem(shard + k, 8)
        zh, x = lax.div(other, 4), lax.rem(other, 4)
        src = wp_ref.at[zh, p.d]
        if k == 0:
            copy = pltpu.make_async_copy(src, own_quarter, local.at[moves.used_local])
            moves.used_local += 1
            copy.start()
            quarter_arrivals.append(copy.wait)
        else:
            moves.push(src, own_quarter, p.at(x=x, zh=zh), w + k)
            other = lax.rem(shard + 8 - k, 8)
            quarter_arrivals.append(arrival(quarter(lax.div(other, 4), lax.rem(other, 4), p.c, p.d), w + k))


    arrival(from_z, first)()
    moves.push(from_z, from_z, p.sibling, first + 2)
    for wait in quarter_arrivals:
        wait()
    y = moves.slots(8)
    moves.push(quarters(p.c, p.d), quarters(p.c, p.d), p.sibling, y)
    for k in (2, 1, 3):
        moves.push(quarters(p.c, p.d), quarters(p.c, p.d), p.at(d=p.along_y(k)), y + k)

    for n in range(4):
        x, c = 2 * p.c + n // 2, n % 2
        arrival(xt_ref.at[n], a + n, jnp.logical_or(x != p.x, c != p.c))()
    for wait in halo:
        wait()
    for when, wait in moves.locals:
        under(when, wait)
    moves.locals = []
    pick = (lax.broadcasted_iota(jnp.int32, (16, 128), 0) == lax.broadcasted_iota(jnp.int32, (16, 128), 1)).astype(BF16)
    zero_rows = jnp.zeros((16, 384), BF16)
    low = dot(jnp.where(base != 0, low_ref[...], zero_rows), pick, TN)[:320]
    high = dot(jnp.where(base != 12, high_ref[...], zero_rows), pick, TN)[:320]
    even = jnp.concatenate([xt_ref[n, 0] for n in range(4)], axis=1).astype(F32)
    odd = jnp.concatenate([xt_ref[n, 1] for n in range(4)], axis=1).astype(F32)
    lane = lax.broadcasted_iota(jnp.int32, (320, 512), 1)
    both = even + odd
    x5_ref[pl.ds(640, 320), :] = both.astype(BF16)
    x5_ref[pl.ds(0, 320), :] = jnp.where(lane == 0, low[:, 0:1] + low[:, 1:2], pltpu.roll(both, 1, 1)).astype(BF16)
    x5_ref[pl.ds(1280, 320), :] = jnp.where(
        lane == 511, high[:, 0:1] + high[:, 1:2], pltpu.roll(both, 511, 1)
    ).astype(BF16)
    x5_ref[pl.ds(320, 320), :] = (even + jnp.where(lane == 0, low[:, 1:2], pltpu.roll(odd, 1, 1))).astype(BF16)
    x5_ref[pl.ds(960, 320), :] = (odd + jnp.where(lane == 511, high[:, 0:1], pltpu.roll(even, 511, 1))).astype(BF16)
    arrival(cwf_ref.at[:, 2 * p.zh + 1 - p.c], first + 1)()
    arrival(cwf_ref.at[:, 2 * (1 - p.zh) + 1 - p.c], first + 2)()
    b = moves.slots(4)
    for half in range(2):
        conv = dot(x5_ref[:, 256 * half : 256 * half + 256], cwf_ref[...].reshape(1600, 768), TN) * 0.5
        for n in range(2):
            slot = 2 * half + n
            part_ref[slot] = conv[128 * n : 128 * n + 128].astype(BF16)
            x = 2 * p.c + half
            alone = jnp.logical_and(x == p.x, n == p.c)
            moves.push(part_ref.at[slot], rs_ref.at[p.x], p.at(x=x, c=n), b + slot, b + p.x, jnp.logical_not(alone))
            moves.keep(part_ref.at[slot], rs_ref.at[p.x], alone)
    other_x5 = moves.slots(1)
    moves.push(x5_ref, x5s_ref, p.sibling, other_x5)
    for x in range(4):
        arrival(rs_ref.at[x], b + x, jnp.logical_or(p.x != x, core != p.c))()
    for when, wait in moves.locals:
        under(when, wait)
    moves.locals = []
    total = rs_ref[0].astype(F32)
    for x in range(1, 4):
        total = total + rs_ref[x].astype(F32)
    sec_ref[...] = total.astype(BF16)
    secs_ref[p.z] = total.astype(BF16)
    g = moves.slots(4)
    for k in (2, 1, 3):
        moves.push(sec_ref, secs_ref.at[p.z], p.at_z(p.along_z(k)), g + k)

    for k in (1, 3, 2):
        d = p.along_y(4 - k)
        arrival(quarters(p.c, d), y + k)()
        moves.push(quarters(p.c, d), quarters(p.c, d), p.sibling, y + 3 + k)
    arrival(quarters(1 - p.c, p.d), y)()
    for k in (1, 3, 2):
        arrival(quarters(1 - p.c, p.along_y(4 - k)), y + 3 + k)()

    def kv_rows(zh):
        return wf_ref[zh, :, :, :, :640].reshape(768, 640)

    def output_rows(zh):
        return wf_ref[zh, :, :, :, 512:].reshape(768, 256)

    def channels(ref, t):
        return jnp.concatenate([ref[t], ref[2 + t]], axis=0)

    wide_lane = lax.broadcasted_iota(jnp.int32, (256, 256), 1)

    for k in (2, 1, 3):
        arrival(secs_ref.at[p.along_z(4 - k)], g + k)()
    cot_first = moves.slots(4)
    cot_own = pltpu.make_async_copy(cot_ref, cots_ref.at[p.z], local.at[moves.used_local])
    moves.used_local += 1
    cot_own.start()
    cot_arrivals = [cot_own.wait]
    for k in (2, 1, 3):
        moves.push(cot_ref, cots_ref.at[p.z], p.at_z(p.along_z(k)), cot_first + k)
        cot_arrivals.append(arrival(cots_ref.at[p.along_z(4 - k)], cot_first + k))
    o = moves.slots(4)
    for zh in range(2):
        left, right = secs_ref[2 * zh].astype(F32), secs_ref[2 * zh + 1].astype(F32)
        squares = jnp.sum(left * left, axis=1, keepdims=True) + jnp.sum(right * right, axis=1, keepdims=True)
        inverse = lax.rsqrt(squares * (1.0 / 1536) + EPSILON)
        inv_ref[zh] = jnp.broadcast_to(inverse, (128, 128))
        nb_ref[2 * zh] = (left * inverse).astype(BF16)
        nb_ref[2 * zh + 1] = (right * inverse).astype(BF16)
    projected = dot(channels(nb_ref, 0), kv_rows(0), NN) + dot(channels(nb_ref, 1), kv_rows(1), NN)
    kv_ref[p.c, p.x] = projected[:, :384].astype(BF16)
    query = jnp.where(wide_lane < 192, projected[:, 384:], 0.0).astype(BF16)
    q = moves.slots(8)
    mine = kv_ref.at[p.c, p.x]
    for k in (2, 1, 3):
        moves.push(mine, mine, p.at(x=p.along_x(k)), q + k)
    moves.push(mine, mine, p.sibling, q)
    for zh in range(2):
        nl_ref[zh] = nb_ref[2 * zh + p.c]
        moves.push(nb_ref.at[2 * zh + 1 - p.c], nl_ref.at[2 + zh], p.sibling, o + 2 + zh)
    for k in (1, 3, 2):
        spot = kv_ref.at[p.c, p.along_x(4 - k)]
        arrival(spot, q + k)()
        moves.push(spot, spot, p.sibling, q + 3 + k)
    arrival(kv_ref.at[1 - p.c, p.x], q)()
    for k in (1, 3, 2):
        arrival(kv_ref.at[1 - p.c, p.along_x(4 - k)], q + 3 + k)()

    highest = None
    for n in range(8):
        scores = dot(kv_ref[n // 4, n % 4, :, :256], query, NT) * scale
        st_ref[n] = scores
        top = jnp.max(scores, axis=0, keepdims=True)
        highest = top if highest is None else jnp.maximum(highest, top)
    sums = jnp.zeros((1, 256), F32)
    for n in range(8):
        unnormed = jnp.exp(st_ref[n] - highest)
        st_ref[n] = unnormed
        sums = sums + jnp.sum(unnormed, axis=0, keepdims=True)
    share = 1.0 / sums
    for wait in cot_arrivals:
        wait()
    for zh in range(2):
        cl_ref[zh] = cots_ref[2 * zh + p.c]
        moves.push(cots_ref.at[2 * zh + 1 - p.c], cl_ref.at[2 + zh], p.sibling, o + zh)
    grad_att = dot(channels(cots_ref, 0), output_rows(0), NN) + dot(channels(cots_ref, 1), output_rows(1), NN)
    grad_att = jnp.where(wide_lane < 64, 0.0, grad_att).astype(BF16)
    centre = jnp.zeros((1, 256), F32)
    for n in range(8):
        weights = st_ref[n] * share
        grad_prob = dot(kv_ref[n // 4, n % 4, :, 128:], grad_att, NT)
        centre = centre + jnp.sum(weights * grad_prob, axis=0, keepdims=True)
        st_ref[n] = weights
        dp_ref[n] = grad_prob
        p16_ref[n] = weights.astype(BF16)
    r = moves.slots(8)

    def key_grads(c, x):
        n = 4 * c + x
        grad_score = (st_ref[n] * (dp_ref[n] - centre)).astype(BF16)
        ds_ref[n] = grad_score
        keys = dot(grad_score, query, NN) * scale
        values = dot(p16_ref[n], grad_att, NN)
        return jnp.concatenate([keys[:, :128], keys[:, 128:] + values[:, :128], values[:, 128:]], axis=1)

    for k in (2, 1, 3, 0):
        dkv_ref[k] = key_grads(1 - p.c, p.along_x(k)).astype(BF16)
        moves.push(dkv_ref.at[k], buf_ref.at[k], p.sibling, r + k)
    for k in (2, 1, 3, 0):
        x = p.along_x(k)
        here = key_grads(p.c, x)
        arrival(buf_ref.at[k], r + k)()
        sum_ref[k] = (here + buf_ref[k].astype(F32)).astype(BF16)
        if k:
            moves.push(sum_ref.at[k], dkvs_ref.at[p.x], p.at(x=x), r + 4 + k)
    dkvs_ref[p.x] = sum_ref[0]

    def rows8(ref, first, last):
        return ref[:, :, :, first:last].reshape(2048, last - first)

    attended = dot(p16_ref[...].reshape(2048, 256), rows8(kv_ref, 128, 384), TN)
    attended = jnp.where(wide_lane < 64, 0.0, attended).astype(BF16)
    grad_query = dot(ds_ref[...].reshape(2048, 256), rows8(kv_ref, 0, 256), TN) * scale
    grad_query = jnp.where(wide_lane < 192, grad_query, 0.0).astype(BF16)
    gpa_ref[:, 384:512] = grad_query[:, :128]
    gpa_ref[:, 512:640] = grad_query[:, 128:] + attended[:, :128]
    gpa_ref[:, 640:] = attended[:, 128:]
    u = moves.slots(4)
    for t in range(2):
        block = dot(attended, output_rows(t), NT).astype(BF16)
        bo_ref[t] = block[:128]
        bo_ref[2 + t] = block[128:]
    for k in (2, 1, 3):
        z = p.along_z(k)
        moves.push(bo_ref.at[z], bos_ref.at[p.z], p.at_z(z), u + k)
    bos_ref[p.z] = bo_ref[p.z]

    for k in (1, 3, 2):
        arrival(dkvs_ref.at[p.along_x(4 - k)], r + 4 + k)()
    total = dkvs_ref[0].astype(F32)
    for x in range(1, 4):
        total = total + dkvs_ref[x].astype(F32)
    grad_kv = total.astype(BF16)
    gpa_ref[:, :384] = grad_kv
    h = moves.slots(5)
    moves.push(gpa_ref, gpas_ref, p.sibling, h)
    grad_proj = jnp.concatenate([grad_kv, grad_query], axis=1)
    spread = jnp.zeros((256, 1), F32)
    for t in range(2):
        block = dot(grad_proj, kv_rows(t), NT)
        spread = spread + jnp.sum(block * channels(secs_ref, t).astype(F32), axis=1, keepdims=True)
        rounded = block.astype(BF16)
        norm_ref[t] = rounded[:128]
        norm_ref[2 + t] = rounded[128:]
    spread = spread * (1.0 / 1536)
    for zh in range(2):
        spread_ref[zh] = jnp.broadcast_to(spread[128 * zh : 128 * zh + 128], (128, 128)).T[:8]
    m = moves.slots(8)
    for k in (2, 1, 3):
        z = p.along_z(k)
        moves.push(norm_ref.at[z], norms_ref.at[p.z], p.at_z(z), m + k)
        moves.push(spread_ref.at[lax.div(z, 2)], spreads_ref.at[p.z], p.at_z(z), m + 4 + k)
    norms_ref[p.z] = norm_ref[p.z]
    spreads_ref[p.z] = spread_ref[p.zh]

    for n in range(4):
        arrival((cl_ref if n < 2 else nl_ref).at[2 + n % 2], o + n)()
    arrival(gpas_ref, h)()
    grads = jnp.concatenate([gpa_ref[...], gpas_ref[...]], axis=0)
    head_part = dot(nl_ref[...].reshape(512, 768), grads[:, :640], TN)
    output_part = dot(cl_ref[...].reshape(512, 768), grads[:, 512:], TN)
    tile_lane = lax.broadcasted_iota(jnp.int32, (768, 128), 1)
    middle = jnp.where(tile_lane < 64, head_part[:, 512:], output_part[:, :128])
    parts = jnp.concatenate([head_part[:, :512], middle, output_part[:, 128:]], axis=1)
    for n in range(8):
        for d in range(4):
            row = 96 * n + 24 * d
            hg_ref[d, n] = parts[row : row + 24].astype(BF16)
    for k in (2, 1, 3):
        d = p.along_y(k)
        moves.push(hg_ref.at[d], hgs_ref.at[p.d], p.at(d=d), h + 1 + k)
    hgs_ref[p.d] = hg_ref[p.d]

    for k in (1, 3, 2):
        arrival(bos_ref.at[p.along_z(4 - k)], u + k)()
    total = sec_ref[...].astype(F32)
    projected_out = bos_ref[0].astype(F32)
    for z in range(1, 4):
        projected_out = projected_out + bos_ref[z].astype(F32)
    out_ref[...] = (total + projected_out).astype(BF16)

    for k in (1, 3, 2):
        arrival(norms_ref.at[p.along_z(4 - k)], m + k)()
        arrival(spreads_ref.at[p.along_z(4 - k)], m + 4 + k)()
    grad_normed = norms_ref[0].astype(F32)
    mean = spreads_ref[0]
    for z in range(1, 4):
        grad_normed = grad_normed + norms_ref[z].astype(F32)
        mean = mean + spreads_ref[z]
    mean = jnp.concatenate([mean] * 16, axis=0).T[:, :1]
    inverse = inv_ref[p.zh][:, :1]
    grad_section = cots_ref[p.z].astype(F32) + inverse * grad_normed - inverse * inverse * inverse * total * mean
    grad_pool = (0.5 * grad_section).astype(BF16)
    gp_ref[0] = grad_pool[:, :384]
    gp_ref[1] = grad_pool[:, 384:]
    j = moves.slots(8)
    block = 2 * p.x + p.c
    for k in (4, 5, 2, 3, 6, 7, 1):
        other = lax.rem(block + k, 8)
        x, c = lax.div(other, 2), lax.rem(other, 2)
        moves.push(gp_ref.at[c], gps_ref.at[block], p.at(x=x, c=c), j + k)
    gps_ref[block] = gp_ref[p.c]
    for k in (1, 3, 2):
        arrival(hgs_ref.at[p.along_y(4 - k)], h + 1 + k)()
    rows = hgs_ref[0].astype(F32)
    for d in range(1, 4):
        rows = rows + hgs_ref[d].astype(F32)
    rows = rows.astype(BF16)
    f = moves.slots(8)
    for n in range(8):
        hgo_ref[n // 2, n % 2] = rows[n]
    alone = []
    for k in (2, 3, 4, 5, 6, 7, 0, 1):
        other = lax.rem(2 * p.x + k, 8)
        x, c = lax.div(other, 2), lax.rem(other, 2)
        src, dst = hgo_ref.at[x, c], hgl_ref.at[p.zh, p.x]
        if k < 2:
            alone = jnp.logical_and(jnp.logical_and(x == p.x, c == p.c), p.zh == p.c)
            moves.push(src, dst, p.at(x=x, zh=p.c, c=c), f + k, f + 4 * p.zh + p.x, jnp.logical_not(alone))
            moves.keep(src, dst, alone)
        else:
            moves.push(src, dst, p.at(x=x, zh=p.c, c=c), f + k, f + 4 * p.zh + p.x)

    arrival(x5s_ref, other_x5)()
    for k in (1, 7, 6, 2, 3, 4, 5):
        arrival(gps_ref.at[lax.rem(block + 8 - k, 8)], j + k)()
    here = gps_ref[pl.ds(4 * p.c, 4)].reshape(512, 384)
    there = gps_ref[pl.ds(4 - 4 * p.c, 4)].reshape(512, 384)
    cgf_ref[...] = dot(x5_ref[...], here, NN) + dot(x5s_ref[...], there, NN)
    for n in range(16):
        for tap in range(5):
            cgm_ref[n % 2, pl.ds(20 * tap, 20), :] = cgf_ref[pl.ds(320 * tap + 20 * n, 20), :]
        cg_ref[n] = cgm_ref[n % 2].astype(BF16)
    e = moves.slots(16)
    me = 8 * p.zh + 4 * p.c + p.d
    for k in (10, 14, 2, 6, 8, 12, 4, 9, 11, 13, 15, 1, 3, 5, 7):
        other = lax.rem(me + k, 16)
        zh, c, d = lax.div(other, 8), lax.rem(lax.div(other, 4), 2), lax.rem(other, 4)
        moves.push(cg_ref.at[other], cgs_ref.at[me], p.at(zh=zh, c=c, d=d), e + k)
    cgs_ref[me] = cg_ref[me]
    for zh in range(2):
        for x in range(4):
            alone = jnp.logical_and(jnp.logical_and(x == p.x, zh == p.zh), p.zh == p.c)
            arrival(hgl_ref.at[zh, x], f + 4 * zh + x, jnp.logical_not(alone))()
    for when, wait in moves.locals:
        under(when, wait)
    moves.locals = []
    heads = []
    for zh in range(2):
        rows = hgl_ref[zh, 0].astype(F32)
        for x in range(1, 4):
            rows = rows + hgl_ref[zh, x].astype(F32)
        heads.append(rows)
    for n, first in enumerate((384, 0, 192, 576)):
        piece = jnp.concatenate([rows[:, first : first + 192] for rows in heads], axis=1)
        if n < 3:
            head_ref[:, n, :] = piece
        else:
            output_ref[...] = piece
    for k in (1, 2, 3, 4, 5, 6, 7, 8, 9, 10, 11, 12, 13, 14, 15):
        arrival(cgs_ref.at[lax.rem(me + 16 - k, 16)], e + k)()
    for c in range(2):
        total = None
        for zh in range(2):
            for d in range(4):
                part = cgs_ref[8 * zh + 4 * c + d].astype(F32)
                total = part if total is None else total + part
        cgm_ref[c] = total
        for tap in range(5):
            conv_ref[:, tap, 384 * c : 384 * c + 384] = cgm_ref[c, pl.ds(20 * tap, 20), :]
    moves.settle()


def main_call(at, edges, cw, wp, cot):
    anywhere = pl.BlockSpec(memory_space=pl.ANY)
    inside = pl.BlockSpec(memory_space=pltpu.VMEM)

    def vmem(*dims, dtype=BF16):
        return pltpu.VMEM(dims, dtype)

    scratch = [
        vmem(4, 2, 320, 128), vmem(16, 384), vmem(16, 384), vmem(5, 4, 80, 768), vmem(2, 4, 2, 96, 768),
        vmem(4, 128, 768), vmem(1600, 512), vmem(1600, 512), vmem(4, 128, 768), vmem(4, 128, 768),
        vmem(128, 768), vmem(4, 128, 768),
        vmem(2, 128, 128, dtype=F32), vmem(4, 128, 768), vmem(4, 128, 768), vmem(4, 128, 768),
        vmem(2, 4, 256, 384), vmem(8, 256, 256, dtype=F32), vmem(8, 256, 256, dtype=F32),
        vmem(8, 256, 256), vmem(8, 256, 256), vmem(4, 256, 384), vmem(4, 256, 384), vmem(4, 256, 384),
        vmem(4, 256, 384),
        vmem(4, 128, 768), vmem(4, 128, 768), vmem(256, 768), vmem(256, 768), vmem(4, 128, 768), vmem(4, 128, 768),
        vmem(2, 8, 128, dtype=F32), vmem(4, 8, 128, dtype=F32),
        vmem(4, 8, 24, 768), vmem(4, 8, 24, 768), vmem(2, 128, 384), vmem(8, 128, 384),
        vmem(4, 2, 24, 768), vmem(2, 4, 24, 768), vmem(1600, 384, dtype=F32), vmem(2, 104, 384, dtype=F32),
        vmem(16, 104, 384), vmem(16, 104, 384),
        pltpu.SemaphoreType.DMA((136,)), pltpu.SemaphoreType.DMA((136,)), pltpu.SemaphoreType.DMA((16,)),
    ]
    return pl.pallas_call(
        main_kernel,
        name="main",
        out_shape=(
            shape(128, 768),
            jax.ShapeDtypeStruct((20, 5, 768), F32),
            jax.ShapeDtypeStruct((24, 3, 384), F32),
            jax.ShapeDtypeStruct((24, 384), F32),
        ),
        in_specs=[anywhere] * 5,
        out_specs=(inside,) * 4,
        scratch_shapes=scratch,
        compiler_params=pltpu.CompilerParams(
            collective_id=1, has_side_effects=True, vmem_limit_bytes=60 * 1024 * 1024
        ),
    )(at, edges, cw, wp, cot)


def shape(*dims):
    return jax.ShapeDtypeStruct(dims, BF16)


def local(section_input, conv_weight, head_weight, output_weight, cotangent):
    activity = jax.nn.gelu(section_input[0].astype(F32), approximate=True).astype(BF16)
    bins = activity.reshape(128, 2, 2, 4, 160)
    at = bins.transpose(3, 1, 2, 4, 0).reshape(4, 2, 320, 128)
    edges = jnp.stack([bins[0], bins[127]]).transpose(0, 3, 1, 2, 4).reshape(2, 4, 2, 320)
    edges = jnp.pad(edges, ((0, 0), (0, 0), (0, 14), (0, 64)))
    cw = conv_weight.transpose(1, 0, 2)
    heads = head_weight.reshape(96, 3, 2, 192)
    wp = jnp.stack([heads[:, 1], heads[:, 2], heads[:, 0], output_weight.reshape(96, 2, 192)], axis=2)
    wp = wp.reshape(2, 48, 2, 2, 384).transpose(2, 0, 3, 1, 4).reshape(2, 4, 48, 384)
    block_out, conv_grad, head_grad, output_grad = main_call(at, edges, cw, wp, cotangent[0])
    return (block_out[None], conv_grad, head_grad, output_grad)


def solution(mesh):
    placed = (
        P("dp", "seq", None),
        P("seq", None, "tensor"),
        P("seq", None, "tensor"),
        P("seq", "tensor"),
        P("dp", "seq", "tensor"),
    )
    return jax.shard_map(
        local,
        mesh=mesh,
        in_specs=placed,
        out_specs=(
            P("dp", "seq", "tensor"),
            P(("seq", "dp"), None, "tensor"),
            P(("seq", "dp"), None, "tensor"),
            P(("seq", "dp"), "tensor"),
        ),
        check_vma=False,
    )
```

```python
import jax
import jax.numpy as jnp
from jax import lax
from jax.experimental import pallas as pl
from jax.experimental.pallas import tpu as pltpu
from jax.sharding import PartitionSpec as P

HEAD_DIM = 192
EPSILON = 1e-06
MESH = pl.DeviceIdType.MESH
BF16 = jnp.bfloat16
F32 = jnp.float32


class Place:
    def __init__(self):
        self.s = lax.axis_index("seq")
        self.zh = lax.div(self.s, 8)
        self.x = lax.rem(lax.div(self.s, 2), 4)
        self.c = lax.rem(self.s, 2)
        self.t = lax.axis_index("tensor")
        self.d = lax.axis_index("dp")
        self.z = 2 * self.zh + self.t

    def at(self, x=None, zh=None, c=None, t=None, d=None):
        x = self.x if x is None else x
        zh = self.zh if zh is None else zh
        c = self.c if c is None else c
        return {
            "seq": zh * 8 + x * 2 + c,
            "tensor": self.t if t is None else t,
            "dp": self.d if d is None else d,
        }

    def along_x(self, k):
        return lax.rem(self.x + k, 4)

    def along_y(self, k):
        return lax.rem(self.d + k, 4)

    def along_z(self, k):
        return lax.rem(self.z + k, 4)

    def at_z(self, z):
        return self.at(zh=lax.div(z, 2), t=lax.rem(z, 2))

    @property
    def sibling(self):
        return self.at(c=1 - self.c)


def remote(src, dst, send, recv, target):
    return pltpu.make_async_remote_copy(
        src_ref=src, dst_ref=dst, send_sem=send, recv_sem=recv, device_id=target, device_id_type=MESH
    )


def greet(targets):
    barrier = pltpu.get_barrier_semaphore()
    for condition, target in targets:
        if condition is None:
            pl.semaphore_signal(barrier, inc=1, device_id=target, device_id_type=MESH)
        else:

            @pl.when(condition)
            def _(target=target):
                pl.semaphore_signal(barrier, inc=1, device_id=target, device_id_type=MESH)

    return barrier


def under(condition, action):
    if condition is None:
        action()
    else:

        @pl.when(condition)
        def _():
            action()


class Moves:
    def __init__(self, place, send, recv, local):
        self.place, self.send, self.recv, self.local = place, send, recv, local
        self.sends, self.receives, self.locals = [], [], []
        self.used = 0
        self.used_local = 0

    def slots(self, count):
        first = self.used
        self.used += count
        return first

    def push(self, src, dst, target, slot, recv_slot=None, when=None):
        recv_slot = slot if recv_slot is None else recv_slot
        copy = remote(src, dst, self.send.at[slot], self.recv.at[recv_slot], target)
        under(when, copy.start)
        self.sends.append((when, copy.wait_send))

    def keep(self, src, dst, when=None):
        copy = pltpu.make_async_copy(src, dst, self.local.at[self.used_local])
        self.used_local += 1
        under(when, copy.start)
        self.locals.append((when, copy.wait))

    def arrival(self, dst, slot, when=None):
        place = self.place
        copy = remote(dst, dst, self.send.at[0], self.recv.at[slot], place.at())
        return lambda: under(when, copy.wait_recv)

    def expect(self, dst, slot, when=None):
        self.receives.append(self.arrival(dst, slot, when))

    def settle(self):
        for wait in self.receives:
            wait()
        for when, wait in self.locals + self.sends:
            under(when, wait)


def z_ring(p):
    return [(None, p.at_z(p.along_z(k))) for k in range(1, 4)]


def y_ring(p):
    return [(None, p.at(d=p.along_y(k))) for k in range(1, 4)]


def dot(a, b, dims):
    return lax.dot_general(a, b, (dims, ((), ())), preferred_element_type=F32)


NN = ((1,), (0,))
NT = ((1,), (1,))
TN = ((0,), (0,))


def main_kernel(
    input_ref, cw_ref, hw_ref, ow_ref, cot_ref,
    out_ref, conv_ref, head_ref, output_ref,
    act_ref, at_ref, edge_ref, wp_ref, end_ref, xt_ref, low_ref, high_ref, cwf_ref, wf_ref, cots_ref, x5_ref, x5s_ref, part_ref, rs_ref, sec_ref, secs_ref,
    inv_ref, nb_ref, nl_ref, cl_ref, kv_ref, st_ref, dp_ref, p16_ref, ds_ref, dkv_ref, buf_ref, sum_ref, dkvs_ref,
    bo_ref, bos_ref, gpa_ref, gpas_ref, norm_ref, norms_ref, spread_ref, spreads_ref, hg_ref, hgs_ref, gp_ref, gps_ref,
    hgo_ref, hgl_ref, cgf_ref, cgm_ref, cg_ref, cgs_ref, send, recv, local,
):
    p = Place()
    scale = HEAD_DIM ** (-0.5)
    peers = [(None, {"seq": lax.rem(p.s + k, 16), "tensor": p.t, "dp": p.d}) for k in range(1, 16)]
    peers += [(None, p.at(t=1 - p.t)), (None, p.at(zh=1 - p.zh, t=1 - p.t))]
    for zh in range(2):
        for c in range(2):
            peers += [(None, p.at(zh=zh, c=c, d=p.along_y(k))) for k in range(1, 4)]
    barrier = greet(peers)
    pl.semaphore_wait(barrier, 29)
    moves = Moves(p, send, recv, local)
    arrival = moves.arrival

    first = moves.slots(12)

    def fifth(zh, c, n):
        return cwf_ref.at[:, 2 * zh + c, pl.ds(pl.multiple_of(16 * n, 16), 16), :]

    other_half = 1 - p.zh
    moves.push(cw_ref.at[:, pl.ds(pl.multiple_of(16 * p.d, 16), 16), :], fifth(p.zh, p.c, p.d), p.at(zh=other_half), first)
    moves.push(cw_ref.at[:, pl.ds(64, 16), :], fifth(p.zh, p.c, 4), p.at(zh=other_half), first + 1)
    mine = cwf_ref.at[:, 2 * p.zh + p.c]
    moves.push(cw_ref, mine, p.sibling, first + 2)
    moves.keep(cw_ref, mine)

    for head in range(2):
        lanes = slice(192 * head, 192 * head + 192)
        keys, values, queries = (hw_ref[n, :, lanes].astype(F32) for n in (1, 2, 0))
        pairs = (jnp.concatenate([keys, values], axis=1), jnp.concatenate([queries, ow_ref[:, lanes].astype(F32)], axis=1))
        for column in range(2):
            for row in range(2):
                wp_ref[head, 2 * row + column] = pairs[column][48 * row : 48 * row + 48].astype(BF16)

    def quarter(zh, x, c, d):
        rows = pl.ds(pl.multiple_of(48 * lax.div(d, 2), 16), 48)
        columns = pl.ds(pl.multiple_of(384 * lax.rem(d, 2), 128), 384)
        return wf_ref.at[zh, x, c, rows, columns]

    def quarters(c, d):
        rows = pl.ds(pl.multiple_of(48 * lax.div(d, 2), 16), 48)
        columns = pl.ds(pl.multiple_of(384 * lax.rem(d, 2), 128), 384)
        return wf_ref.at[:, :, c, rows, columns]

    w = moves.slots(8)
    shard = 4 * p.zh + p.x
    own_quarter = quarter(p.zh, p.x, p.c, p.d)
    quarter_arrivals = []
    for k in range(8):
        other = lax.rem(shard + k, 8)
        zh, x = lax.div(other, 4), lax.rem(other, 4)
        src = wp_ref.at[zh, p.d]
        if k == 0:
            copy = pltpu.make_async_copy(src, own_quarter, local.at[moves.used_local])
            moves.used_local += 1
            copy.start()
            quarter_arrivals.append(copy.wait)
        else:
            moves.push(src, own_quarter, p.at(x=x, zh=zh), w + k)
            other = lax.rem(shard + 8 - k, 8)
            quarter_arrivals.append(arrival(quarter(lax.div(other, 4), lax.rem(other, 4), p.c, p.d), w + k))

    for n in range(10):
        lanes = slice(128 * n, 128 * n + 128)
        rows = jax.nn.gelu(input_ref[:, lanes].astype(F32), approximate=True).astype(BF16)
        edge_ref[0, :, lanes] = rows[:16]
        edge_ref[1, :, lanes] = rows[240:]
        act_ref[n] = rows.astype(F32)
        for parity in range(2):
            turned = act_ref[n, pl.ds(parity, 128, stride=2), :].T.astype(BF16)
            begin = 128 * n
            while begin < 128 * n + 128:
                end = min(128 * n + 128, (begin // 160 + 1) * 160)
                zh, x = divmod(begin // 160, 4)
                spot = 160 * zh + begin % 160
                at_ref[x, parity, spot : spot + end - begin] = turned[begin - 128 * n : end - 128 * n]
                begin = end
    a = moves.slots(4)
    core = lax.div(p.x, 2)
    slot = 2 * lax.rem(p.x, 2) + p.c
    spot = xt_ref.at[slot]
    for k in (2, 1, 3, 0):
        x = p.along_x(k)
        if k == 0:
            moves.push(at_ref.at[x], spot, p.at(c=core), a, a + slot, core != p.c)
            moves.keep(at_ref.at[x], spot, core == p.c)
        else:
            moves.push(at_ref.at[x], spot, p.at(x=x, c=core), a + k, a + slot)
    base = 8 * p.zh + 4 * p.c
    halo = []
    for up, bound_ref in ((True, low_ref), (False, high_ref)):
        e = moves.slots(4)
        if up:
            sends = jnp.logical_and(lax.rem(p.s, 4) == 3, p.s != 15)
            block = lax.rem(p.s + 1, 16)
        else:
            sends = jnp.logical_and(lax.rem(p.s, 4) == 0, p.s != 0)
            block = lax.rem(p.s + 15, 16)
        zh, c = lax.div(block, 8), lax.div(lax.rem(block, 8), 4)
        for k in range(4):
            x = p.along_x(k)
            src = edge_ref.at[1 if up else 0]
            target = p.at(x=x, zh=zh, c=c)
            if k == 0:
                alone = jnp.logical_and(zh == p.zh, c == p.c)
                moves.push(src, bound_ref, target, e, e, jnp.logical_and(sends, jnp.logical_not(alone)))
                moves.keep(src, bound_ref, jnp.logical_and(sends, alone))
            else:
                moves.push(src, bound_ref, target, e + k, e, sends)
        if up:
            halo.append(arrival(bound_ref, e, jnp.logical_and(base != 0, base - 1 != p.s)))
        else:
            halo.append(arrival(bound_ref, e, jnp.logical_and(base != 12, base + 4 != p.s)))

    moves.arrival(fifth(other_half, p.c, p.d), first)()
    got = fifth(other_half, p.c, p.d)
    for k in (2, 1, 3):
        moves.push(got, got, p.at(d=p.along_y(k)), first + 3 + k)
    moves.push(got, got, p.sibling, first + 3)
    got = fifth(other_half, p.c, 4)
    moves.arrival(got, first + 1)()
    moves.push(got, got, p.sibling, first + 7)
    for k in (1, 3, 2):
        got = fifth(other_half, p.c, p.along_y(4 - k))
        moves.arrival(got, first + 3 + k)()
        moves.push(got, got, p.sibling, first + 7 + k)
    for wait in quarter_arrivals:
        wait()
    y = moves.slots(8)
    moves.push(quarters(p.c, p.d), quarters(p.c, p.d), p.sibling, y)
    for k in (2, 1, 3):
        moves.push(quarters(p.c, p.d), quarters(p.c, p.d), p.at(d=p.along_y(k)), y + k)

    for n in range(4):
        x, c = 2 * p.c + n // 2, n % 2
        arrival(xt_ref.at[n], a + n, jnp.logical_or(x != p.x, c != p.c))()
    for wait in halo:
        wait()
    for when, wait in moves.locals:
        under(when, wait)
    moves.locals = []
    row = lax.broadcasted_iota(jnp.int32, (16, 128), 0)
    column = lax.broadcasted_iota(jnp.int32, (16, 128), 1)
    zero_rows = jnp.zeros((16, 1280), BF16)
    ends = []
    for there, bound_ref, shift in ((base != 0, low_ref, 14), (base != 12, high_ref, 0)):
        pick = (row == column + shift).astype(BF16)
        end_ref[...] = dot(jnp.where(there, bound_ref[...], zero_rows), pick, TN)
        lower = pl.multiple_of(160 * p.x, 32)
        ends.append(jnp.concatenate([end_ref[pl.ds(lower, 160)], end_ref[pl.ds(640 + lower, 160)]], axis=0))
    low, high = ends
    even = jnp.concatenate([xt_ref[n, 0] for n in range(4)], axis=1).astype(F32)
    odd = jnp.concatenate([xt_ref[n, 1] for n in range(4)], axis=1).astype(F32)
    lane = lax.broadcasted_iota(jnp.int32, (320, 512), 1)
    both = even + odd
    x5_ref[pl.ds(640, 320), :] = both.astype(BF16)
    x5_ref[pl.ds(0, 320), :] = jnp.where(lane == 0, low[:, 0:1] + low[:, 1:2], pltpu.roll(both, 1, 1)).astype(BF16)
    x5_ref[pl.ds(1280, 320), :] = jnp.where(
        lane == 511, high[:, 0:1] + high[:, 1:2], pltpu.roll(both, 511, 1)
    ).astype(BF16)
    x5_ref[pl.ds(320, 320), :] = (even + jnp.where(lane == 0, low[:, 1:2], pltpu.roll(odd, 1, 1))).astype(BF16)
    x5_ref[pl.ds(960, 320), :] = (odd + jnp.where(lane == 511, high[:, 0:1], pltpu.roll(even, 511, 1))).astype(BF16)
    arrival(cwf_ref.at[:, 2 * p.zh + 1 - p.c], first + 2)()
    arrival(fifth(other_half, 1 - p.c, p.d), first + 3)()
    arrival(fifth(other_half, 1 - p.c, 4), first + 7)()
    for k in (1, 3, 2):
        arrival(fifth(other_half, 1 - p.c, p.along_y(4 - k)), first + 7 + k)()
    b = moves.slots(4)
    for half in range(2):
        conv = dot(x5_ref[:, 256 * half : 256 * half + 256], cwf_ref[...].reshape(1600, 768), TN) * 0.5
        for n in range(2):
            slot = 2 * half + n
            part_ref[slot] = conv[128 * n : 128 * n + 128].astype(BF16)
            x = 2 * p.c + half
            alone = jnp.logical_and(x == p.x, n == p.c)
            moves.push(part_ref.at[slot], rs_ref.at[p.x], p.at(x=x, c=n), b + slot, b + p.x, jnp.logical_not(alone))
            moves.keep(part_ref.at[slot], rs_ref.at[p.x], alone)
    other_x5 = moves.slots(1)
    moves.push(x5_ref, x5s_ref, p.sibling, other_x5)
    for x in range(4):
        arrival(rs_ref.at[x], b + x, jnp.logical_or(p.x != x, core != p.c))()
    for when, wait in moves.locals:
        under(when, wait)
    moves.locals = []
    total = rs_ref[0].astype(F32)
    for x in range(1, 4):
        total = total + rs_ref[x].astype(F32)
    sec_ref[...] = total.astype(BF16)
    secs_ref[p.z] = total.astype(BF16)
    g = moves.slots(4)
    for k in (2, 1, 3):
        moves.push(sec_ref, secs_ref.at[p.z], p.at_z(p.along_z(k)), g + k)

    for k in (1, 3, 2):
        d = p.along_y(4 - k)
        arrival(quarters(p.c, d), y + k)()
        moves.push(quarters(p.c, d), quarters(p.c, d), p.sibling, y + 3 + k)
    arrival(quarters(1 - p.c, p.d), y)()
    for k in (1, 3, 2):
        arrival(quarters(1 - p.c, p.along_y(4 - k)), y + 3 + k)()

    def kv_rows(zh):
        return wf_ref[zh, :, :, :, :640].reshape(768, 640)

    def output_rows(zh):
        return wf_ref[zh, :, :, :, 512:].reshape(768, 256)

    def channels(ref, t):
        return jnp.concatenate([ref[t], ref[2 + t]], axis=0)

    wide_lane = lax.broadcasted_iota(jnp.int32, (256, 256), 1)

    for k in (2, 1, 3):
        arrival(secs_ref.at[p.along_z(4 - k)], g + k)()
    cot_first = moves.slots(4)
    cot_own = pltpu.make_async_copy(cot_ref, cots_ref.at[p.z], local.at[moves.used_local])
    moves.used_local += 1
    cot_own.start()
    cot_arrivals = [cot_own.wait]
    for k in (2, 1, 3):
        moves.push(cot_ref, cots_ref.at[p.z], p.at_z(p.along_z(k)), cot_first + k)
        cot_arrivals.append(arrival(cots_ref.at[p.along_z(4 - k)], cot_first + k))
    o = moves.slots(4)
    for zh in range(2):
        left, right = secs_ref[2 * zh].astype(F32), secs_ref[2 * zh + 1].astype(F32)
        squares = jnp.sum(left * left, axis=1, keepdims=True) + jnp.sum(right * right, axis=1, keepdims=True)
        inverse = lax.rsqrt(squares * (1.0 / 1536) + EPSILON)
        inv_ref[zh] = jnp.broadcast_to(inverse, (128, 128))
        nb_ref[2 * zh] = (left * inverse).astype(BF16)
        nb_ref[2 * zh + 1] = (right * inverse).astype(BF16)
    projected = dot(channels(nb_ref, 0), kv_rows(0), NN) + dot(channels(nb_ref, 1), kv_rows(1), NN)
    kv_ref[p.c, p.x] = projected[:, :384].astype(BF16)
    query = jnp.where(wide_lane < 192, projected[:, 384:], 0.0).astype(BF16)
    q = moves.slots(8)
    mine = kv_ref.at[p.c, p.x]
    for k in (2, 1, 3):
        moves.push(mine, mine, p.at(x=p.along_x(k)), q + k)
    moves.push(mine, mine, p.sibling, q)
    for zh in range(2):
        nl_ref[zh] = nb_ref[2 * zh + p.c]
        moves.push(nb_ref.at[2 * zh + 1 - p.c], nl_ref.at[2 + zh], p.sibling, o + 2 + zh)
    for k in (1, 3, 2):
        spot = kv_ref.at[p.c, p.along_x(4 - k)]
        arrival(spot, q + k)()
        moves.push(spot, spot, p.sibling, q + 3 + k)
    arrival(kv_ref.at[1 - p.c, p.x], q)()
    for k in (1, 3, 2):
        arrival(kv_ref.at[1 - p.c, p.along_x(4 - k)], q + 3 + k)()

    highest = None
    for n in range(8):
        scores = dot(kv_ref[n // 4, n % 4, :, :256], query, NT) * scale
        st_ref[n] = scores
        top = jnp.max(scores, axis=0, keepdims=True)
        highest = top if highest is None else jnp.maximum(highest, top)
    sums = jnp.zeros((1, 256), F32)
    for n in range(8):
        unnormed = jnp.exp(st_ref[n] - highest)
        st_ref[n] = unnormed
        sums = sums + jnp.sum(unnormed, axis=0, keepdims=True)
    share = 1.0 / sums
    for wait in cot_arrivals:
        wait()
    for zh in range(2):
        cl_ref[zh] = cots_ref[2 * zh + p.c]
        moves.push(cots_ref.at[2 * zh + 1 - p.c], cl_ref.at[2 + zh], p.sibling, o + zh)
    grad_att = dot(channels(cots_ref, 0), output_rows(0), NN) + dot(channels(cots_ref, 1), output_rows(1), NN)
    grad_att = jnp.where(wide_lane < 64, 0.0, grad_att).astype(BF16)
    centre = jnp.zeros((1, 256), F32)
    for n in range(8):
        weights = st_ref[n] * share
        grad_prob = dot(kv_ref[n // 4, n % 4, :, 128:], grad_att, NT)
        centre = centre + jnp.sum(weights * grad_prob, axis=0, keepdims=True)
        st_ref[n] = weights
        dp_ref[n] = grad_prob
        p16_ref[n] = weights.astype(BF16)
    r = moves.slots(8)

    def key_grads(c, x):
        n = 4 * c + x
        grad_score = (st_ref[n] * (dp_ref[n] - centre)).astype(BF16)
        ds_ref[n] = grad_score
        keys = dot(grad_score, query, NN) * scale
        values = dot(p16_ref[n], grad_att, NN)
        return jnp.concatenate([keys[:, :128], keys[:, 128:] + values[:, :128], values[:, 128:]], axis=1)

    for k in (2, 1, 3, 0):
        dkv_ref[k] = key_grads(1 - p.c, p.along_x(k)).astype(BF16)
        moves.push(dkv_ref.at[k], buf_ref.at[k], p.sibling, r + k)
    for k in (2, 1, 3, 0):
        x = p.along_x(k)
        here = key_grads(p.c, x)
        arrival(buf_ref.at[k], r + k)()
        sum_ref[k] = (here + buf_ref[k].astype(F32)).astype(BF16)
        if k:
            moves.push(sum_ref.at[k], dkvs_ref.at[p.x], p.at(x=x), r + 4 + k)
    dkvs_ref[p.x] = sum_ref[0]

    def rows8(ref, first, last):
        return ref[:, :, :, first:last].reshape(2048, last - first)

    attended = dot(p16_ref[...].reshape(2048, 256), rows8(kv_ref, 128, 384), TN)
    attended = jnp.where(wide_lane < 64, 0.0, attended).astype(BF16)
    grad_query = dot(ds_ref[...].reshape(2048, 256), rows8(kv_ref, 0, 256), TN) * scale
    grad_query = jnp.where(wide_lane < 192, grad_query, 0.0).astype(BF16)
    gpa_ref[:, 384:512] = grad_query[:, :128]
    gpa_ref[:, 512:640] = grad_query[:, 128:] + attended[:, :128]
    gpa_ref[:, 640:] = attended[:, 128:]
    u = moves.slots(4)
    for t in range(2):
        block = dot(attended, output_rows(t), NT).astype(BF16)
        bo_ref[t] = block[:128]
        bo_ref[2 + t] = block[128:]
    for k in (2, 1, 3):
        z = p.along_z(k)
        moves.push(bo_ref.at[z], bos_ref.at[p.z], p.at_z(z), u + k)
    bos_ref[p.z] = bo_ref[p.z]

    for k in (1, 3, 2):
        arrival(dkvs_ref.at[p.along_x(4 - k)], r + 4 + k)()
    total = dkvs_ref[0].astype(F32)
    for x in range(1, 4):
        total = total + dkvs_ref[x].astype(F32)
    grad_kv = total.astype(BF16)
    gpa_ref[:, :384] = grad_kv
    h = moves.slots(5)
    moves.push(gpa_ref, gpas_ref, p.sibling, h)
    grad_proj = jnp.concatenate([grad_kv, grad_query], axis=1)
    spread = jnp.zeros((256, 1), F32)
    for t in range(2):
        block = dot(grad_proj, kv_rows(t), NT)
        spread = spread + jnp.sum(block * channels(secs_ref, t).astype(F32), axis=1, keepdims=True)
        rounded = block.astype(BF16)
        norm_ref[t] = rounded[:128]
        norm_ref[2 + t] = rounded[128:]
    spread = spread * (1.0 / 1536)
    for zh in range(2):
        spread_ref[zh] = jnp.broadcast_to(spread[128 * zh : 128 * zh + 128], (128, 128)).T[:8]
    m = moves.slots(8)
    for k in (2, 1, 3):
        z = p.along_z(k)
        moves.push(norm_ref.at[z], norms_ref.at[p.z], p.at_z(z), m + k)
        moves.push(spread_ref.at[lax.div(z, 2)], spreads_ref.at[p.z], p.at_z(z), m + 4 + k)
    norms_ref[p.z] = norm_ref[p.z]
    spreads_ref[p.z] = spread_ref[p.zh]

    for n in range(4):
        arrival((cl_ref if n < 2 else nl_ref).at[2 + n % 2], o + n)()
    arrival(gpas_ref, h)()
    grads = jnp.concatenate([gpa_ref[...], gpas_ref[...]], axis=0)
    head_part = dot(nl_ref[...].reshape(512, 768), grads[:, :640], TN)
    output_part = dot(cl_ref[...].reshape(512, 768), grads[:, 512:], TN)
    tile_lane = lax.broadcasted_iota(jnp.int32, (768, 128), 1)
    middle = jnp.where(tile_lane < 64, head_part[:, 512:], output_part[:, :128])
    parts = jnp.concatenate([head_part[:, :512], middle, output_part[:, 128:]], axis=1)
    for n in range(8):
        for d in range(4):
            row = 96 * n + 24 * d
            hg_ref[d, n] = parts[row : row + 24].astype(BF16)
    for k in (2, 1, 3):
        d = p.along_y(k)
        moves.push(hg_ref.at[d], hgs_ref.at[p.d], p.at(d=d), h + 1 + k)
    hgs_ref[p.d] = hg_ref[p.d]

    for k in (1, 3, 2):
        arrival(bos_ref.at[p.along_z(4 - k)], u + k)()
    total = sec_ref[...].astype(F32)
    projected_out = bos_ref[0].astype(F32)
    for z in range(1, 4):
        projected_out = projected_out + bos_ref[z].astype(F32)
    out_ref[...] = (total + projected_out).astype(BF16)

    for k in (1, 3, 2):
        arrival(norms_ref.at[p.along_z(4 - k)], m + k)()
        arrival(spreads_ref.at[p.along_z(4 - k)], m + 4 + k)()
    grad_normed = norms_ref[0].astype(F32)
    mean = spreads_ref[0]
    for z in range(1, 4):
        grad_normed = grad_normed + norms_ref[z].astype(F32)
        mean = mean + spreads_ref[z]
    mean = jnp.concatenate([mean] * 16, axis=0).T[:, :1]
    inverse = inv_ref[p.zh][:, :1]
    grad_section = cots_ref[p.z].astype(F32) + inverse * grad_normed - inverse * inverse * inverse * total * mean
    grad_pool = (0.5 * grad_section).astype(BF16)
    gp_ref[0] = grad_pool[:, :384]
    gp_ref[1] = grad_pool[:, 384:]
    j = moves.slots(8)
    block = 2 * p.x + p.c
    for k in (4, 5, 2, 3, 6, 7, 1):
        other = lax.rem(block + k, 8)
        x, c = lax.div(other, 2), lax.rem(other, 2)
        moves.push(gp_ref.at[c], gps_ref.at[block], p.at(x=x, c=c), j + k)
    gps_ref[block] = gp_ref[p.c]
    for k in (1, 3, 2):
        arrival(hgs_ref.at[p.along_y(4 - k)], h + 1 + k)()
    rows = hgs_ref[0].astype(F32)
    for d in range(1, 4):
        rows = rows + hgs_ref[d].astype(F32)
    rows = rows.astype(BF16)
    f = moves.slots(8)
    for n in range(8):
        hgo_ref[n // 2, n % 2] = rows[n]
    alone = []
    for k in (2, 3, 4, 5, 6, 7, 0, 1):
        other = lax.rem(2 * p.x + k, 8)
        x, c = lax.div(other, 2), lax.rem(other, 2)
        src, dst = hgo_ref.at[x, c], hgl_ref.at[p.zh, p.x]
        if k < 2:
            alone = jnp.logical_and(jnp.logical_and(x == p.x, c == p.c), p.zh == p.c)
            moves.push(src, dst, p.at(x=x, zh=p.c, c=c), f + k, f + 4 * p.zh + p.x, jnp.logical_not(alone))
            moves.keep(src, dst, alone)
        else:
            moves.push(src, dst, p.at(x=x, zh=p.c, c=c), f + k, f + 4 * p.zh + p.x)

    arrival(x5s_ref, other_x5)()
    for k in (1, 7, 6, 2, 3, 4, 5):
        arrival(gps_ref.at[lax.rem(block + 8 - k, 8)], j + k)()
    here = gps_ref[pl.ds(4 * p.c, 4)].reshape(512, 384)
    there = gps_ref[pl.ds(4 - 4 * p.c, 4)].reshape(512, 384)
    cgf_ref[...] = dot(x5_ref[...], here, NN) + dot(x5s_ref[...], there, NN)
    for n in range(16):
        for tap in range(5):
            cgm_ref[n % 2, pl.ds(20 * tap, 20), :] = cgf_ref[pl.ds(320 * tap + 20 * n, 20), :]
        cg_ref[n] = cgm_ref[n % 2].astype(BF16)
    e = moves.slots(16)
    me = 8 * p.zh + 4 * p.c + p.d
    for k in (10, 14, 2, 6, 8, 12, 4, 9, 11, 13, 15, 1, 3, 5, 7):
        other = lax.rem(me + k, 16)
        zh, c, d = lax.div(other, 8), lax.rem(lax.div(other, 4), 2), lax.rem(other, 4)
        moves.push(cg_ref.at[other], cgs_ref.at[me], p.at(zh=zh, c=c, d=d), e + k)
    cgs_ref[me] = cg_ref[me]
    for zh in range(2):
        for x in range(4):
            alone = jnp.logical_and(jnp.logical_and(x == p.x, zh == p.zh), p.zh == p.c)
            arrival(hgl_ref.at[zh, x], f + 4 * zh + x, jnp.logical_not(alone))()
    for when, wait in moves.locals:
        under(when, wait)
    moves.locals = []
    heads = []
    for zh in range(2):
        rows = hgl_ref[zh, 0].astype(F32)
        for x in range(1, 4):
            rows = rows + hgl_ref[zh, x].astype(F32)
        heads.append(rows)
    for n, first in enumerate((384, 0, 192, 576)):
        piece = jnp.concatenate([rows[:, first : first + 192] for rows in heads], axis=1)
        if n < 3:
            head_ref[n] = piece
        else:
            output_ref[...] = piece
    for k in (1, 2, 3, 4, 5, 6, 7, 8, 9, 10, 11, 12, 13, 14, 15):
        arrival(cgs_ref.at[lax.rem(me + 16 - k, 16)], e + k)()
    for c in range(2):
        total = None
        for zh in range(2):
            for d in range(4):
                part = cgs_ref[8 * zh + 4 * c + d].astype(F32)
                total = part if total is None else total + part
        cgm_ref[c] = total
        for tap in range(5):
            conv_ref[tap, :, 384 * c : 384 * c + 384] = cgm_ref[c, pl.ds(20 * tap, 20), :]
    moves.settle()


def main_call(section_input, cw, hw, ow, cot):
    anywhere = pl.BlockSpec(memory_space=pl.ANY)
    inside = pl.BlockSpec(memory_space=pltpu.VMEM)

    def vmem(*dims, dtype=BF16):
        return pltpu.VMEM(dims, dtype)

    scratch = [
        vmem(10, 256, 128, dtype=F32), vmem(4, 2, 320, 128), vmem(2, 16, 1280), vmem(2, 4, 48, 384),
        vmem(1280, 128, dtype=F32), vmem(4, 2, 320, 128), vmem(16, 1280), vmem(16, 1280), vmem(5, 4, 80, 768), vmem(2, 4, 2, 96, 768),
        vmem(4, 128, 768), vmem(1600, 512), vmem(1600, 512), vmem(4, 128, 768), vmem(4, 128, 768),
        vmem(128, 768), vmem(4, 128, 768),
        vmem(2, 128, 128, dtype=F32), vmem(4, 128, 768), vmem(4, 128, 768), vmem(4, 128, 768),
        vmem(2, 4, 256, 384), vmem(8, 256, 256, dtype=F32), vmem(8, 256, 256, dtype=F32),
        vmem(8, 256, 256), vmem(8, 256, 256), vmem(4, 256, 384), vmem(4, 256, 384), vmem(4, 256, 384),
        vmem(4, 256, 384),
        vmem(4, 128, 768), vmem(4, 128, 768), vmem(256, 768), vmem(256, 768), vmem(4, 128, 768), vmem(4, 128, 768),
        vmem(2, 8, 128, dtype=F32), vmem(4, 8, 128, dtype=F32),
        vmem(4, 8, 24, 768), vmem(4, 8, 24, 768), vmem(2, 128, 384), vmem(8, 128, 384),
        vmem(4, 2, 24, 768), vmem(2, 4, 24, 768), vmem(1600, 384, dtype=F32), vmem(2, 104, 384, dtype=F32),
        vmem(16, 104, 384), vmem(16, 104, 384),
        pltpu.SemaphoreType.DMA((144,)), pltpu.SemaphoreType.DMA((144,)), pltpu.SemaphoreType.DMA((16,)),
    ]
    return pl.pallas_call(
        main_kernel,
        name="main",
        out_shape=(
            shape(128, 768),
            jax.ShapeDtypeStruct((5, 20, 768), F32),
            jax.ShapeDtypeStruct((3, 24, 384), F32),
            jax.ShapeDtypeStruct((24, 384), F32),
        ),
        in_specs=[inside, anywhere, inside, inside, anywhere],
        out_specs=(inside,) * 4,
        scratch_shapes=scratch,
        compiler_params=pltpu.CompilerParams(
            collective_id=1, has_side_effects=True, vmem_limit_bytes=60 * 1024 * 1024
        ),
    )(section_input, cw, hw, ow, cot)


def shape(*dims):
    return jax.ShapeDtypeStruct(dims, BF16)


def finish_kernel(*refs):
    for source, target in zip(refs[:4], refs[4:]):
        target[...] = source[...]


def finish(*arrays):
    inside = pl.BlockSpec(memory_space=pltpu.VMEM)
    return pl.pallas_call(
        finish_kernel,
        name="finish",
        out_shape=tuple(jax.ShapeDtypeStruct(array.shape, array.dtype) for array in arrays),
        in_specs=[inside] * 4,
        out_specs=(inside,) * 4,
    )(*arrays)


def local(section_input, conv_weight, head_weight, output_weight, cotangent):
    block_out, conv_grad, head_grad, output_grad = finish(
        *main_call(
            section_input[0], conv_weight.transpose(1, 0, 2), head_weight.transpose(1, 0, 2), output_weight, cotangent[0]
        )
    )
    return (block_out[None], conv_grad.transpose(1, 0, 2), head_grad.transpose(1, 0, 2), output_grad)


def solution(mesh):
    placed = (
        P("dp", "seq", None),
        P("seq", None, "tensor"),
        P("seq", None, "tensor"),
        P("seq", "tensor"),
        P("dp", "seq", "tensor"),
    )
    return jax.shard_map(
        local,
        mesh=mesh,
        in_specs=placed,
        out_specs=(
            P("dp", "seq", "tensor"),
            P(("seq", "dp"), None, "tensor"),
            P(("seq", "dp"), None, "tensor"),
            P(("seq", "dp"), "tensor"),
        ),
        check_vma=False,
    )
```

```python
import jax
import jax.numpy as jnp
from jax import lax
from jax.experimental import pallas as pl
from jax.experimental.pallas import tpu as pltpu
from jax.sharding import PartitionSpec as P

HEAD_DIM = 192
EPSILON = 1e-06
MESH = pl.DeviceIdType.MESH
BF16 = jnp.bfloat16
F32 = jnp.float32


class Place:
    def __init__(self):
        self.s = lax.axis_index("seq")
        self.zh = lax.div(self.s, 8)
        self.x = lax.rem(lax.div(self.s, 2), 4)
        self.c = lax.rem(self.s, 2)
        self.t = lax.axis_index("tensor")
        self.d = lax.axis_index("dp")
        self.z = 2 * self.zh + self.t

    def at(self, x=None, zh=None, c=None, t=None, d=None):
        x = self.x if x is None else x
        zh = self.zh if zh is None else zh
        c = self.c if c is None else c
        return {
            "seq": zh * 8 + x * 2 + c,
            "tensor": self.t if t is None else t,
            "dp": self.d if d is None else d,
        }

    def along_x(self, k):
        return lax.rem(self.x + k, 4)

    def along_y(self, k):
        return lax.rem(self.d + k, 4)

    def along_z(self, k):
        return lax.rem(self.z + k, 4)

    def at_z(self, z):
        return self.at(zh=lax.div(z, 2), t=lax.rem(z, 2))

    @property
    def sibling(self):
        return self.at(c=1 - self.c)


def remote(src, dst, send, recv, target):
    return pltpu.make_async_remote_copy(
        src_ref=src, dst_ref=dst, send_sem=send, recv_sem=recv, device_id=target, device_id_type=MESH
    )


def greet(targets):
    barrier = pltpu.get_barrier_semaphore()
    for condition, target in targets:
        if condition is None:
            pl.semaphore_signal(barrier, inc=1, device_id=target, device_id_type=MESH)
        else:

            @pl.when(condition)
            def _(target=target):
                pl.semaphore_signal(barrier, inc=1, device_id=target, device_id_type=MESH)

    return barrier


def under(condition, action):
    if condition is None:
        action()
    else:

        @pl.when(condition)
        def _():
            action()


class Moves:
    def __init__(self, place, send, recv, local):
        self.place, self.send, self.recv, self.local = place, send, recv, local
        self.sends, self.receives, self.locals = [], [], []
        self.used = 0
        self.used_local = 0

    def slots(self, count):
        first = self.used
        self.used += count
        return first

    def push(self, src, dst, target, slot, recv_slot=None, when=None):
        recv_slot = slot if recv_slot is None else recv_slot
        copy = remote(src, dst, self.send.at[slot], self.recv.at[recv_slot], target)
        under(when, copy.start)
        self.sends.append((when, copy.wait_send))

    def keep(self, src, dst, when=None):
        copy = pltpu.make_async_copy(src, dst, self.local.at[self.used_local])
        self.used_local += 1
        under(when, copy.start)
        self.locals.append((when, copy.wait))

    def arrival(self, dst, slot, when=None):
        place = self.place
        copy = remote(dst, dst, self.send.at[0], self.recv.at[slot], place.at())
        return lambda: under(when, copy.wait_recv)

    def expect(self, dst, slot, when=None):
        self.receives.append(self.arrival(dst, slot, when))

    def settle(self):
        for wait in self.receives:
            wait()
        for when, wait in self.locals + self.sends:
            under(when, wait)


def z_ring(p):
    return [(None, p.at_z(p.along_z(k))) for k in range(1, 4)]


def y_ring(p):
    return [(None, p.at(d=p.along_y(k))) for k in range(1, 4)]


def dot(a, b, dims):
    return lax.dot_general(a, b, (dims, ((), ())), preferred_element_type=F32)


NN = ((1,), (0,))
NT = ((1,), (1,))
TN = ((0,), (0,))


def main_kernel(
    input_ref, cw_ref, hw_ref, ow_ref, cot_ref,
    out_ref, conv_ref, head_ref, output_ref,
    act_ref, at_ref, edge_ref, wp_ref, end_ref, xt_ref, low_ref, high_ref, cwf_ref, wf_ref, cots_ref,
    x5_ref, x5t_ref, x5s_ref, part_ref, rs_ref, sec_ref, secs_ref, inv_ref, nb_ref, nl_ref, cl_ref,
    kv_ref, st_ref, dp_ref, p16_ref, ds_ref, dkv_ref, buf_ref, sum_ref, dkvs_ref, bo_ref, bos_ref,
    grads_ref, others_ref, norma_ref, normb_ref, normsa_ref, normsb_ref, spread_ref, spreads_ref,
    hg_ref, hgs_ref, gpa_ref, gpb_ref, gpsa_ref, gpsb_ref, hgo_ref, hgl_ref, cgf_ref, cgm_ref,
    cga_ref, cgb_ref, cgsa_ref, cgsb_ref, send, recv, local,
):
    p = Place()
    scale = HEAD_DIM ** (-0.5)
    peers = [(None, {"seq": lax.rem(p.s + k, 16), "tensor": p.t, "dp": p.d}) for k in range(1, 16)]
    peers += [(None, p.at(t=1 - p.t)), (None, p.at(zh=1 - p.zh, t=1 - p.t))]
    for zh in range(2):
        for c in range(2):
            peers += [(None, p.at(zh=zh, c=c, d=p.along_y(k))) for k in range(1, 4)]
    barrier = greet(peers)
    pl.semaphore_wait(barrier, 29)
    moves = Moves(p, send, recv, local)
    arrival = moves.arrival

    first = moves.slots(12)

    def fifth(zh, c, n):
        return cwf_ref.at[:, 2 * zh + c, pl.ds(pl.multiple_of(16 * n, 16), 16), :]

    other_half = 1 - p.zh
    moves.push(cw_ref.at[:, pl.ds(pl.multiple_of(16 * p.d, 16), 16), :], fifth(p.zh, p.c, p.d), p.at(zh=other_half), first)
    moves.push(cw_ref.at[:, pl.ds(64, 16), :], fifth(p.zh, p.c, 4), p.at(zh=other_half), first + 1)
    mine = cwf_ref.at[:, 2 * p.zh + p.c]
    moves.push(cw_ref, mine, p.sibling, first + 2)
    moves.keep(cw_ref, mine)

    a = moves.slots(8)
    core = lax.div(p.x, 2)
    slot = 2 * lax.rem(p.x, 2) + p.c

    def half_rows(ref, index, half):
        return ref.at[index, :, pl.ds(160 * half, 160), :]

    for n in range(10):
        lanes = slice(128 * n, 128 * n + 128)
        rows = jax.nn.gelu(input_ref[:, lanes].astype(F32), approximate=True).astype(BF16)
        edge_ref[0, :, lanes] = rows[:16]
        edge_ref[1, :, lanes] = rows[240:]
        act_ref[n] = rows.astype(F32)
        for parity in range(2):
            turned = act_ref[n, pl.ds(parity, 128, stride=2), :].T.astype(BF16)
            begin = 128 * n
            while begin < 128 * n + 128:
                end = min(128 * n + 128, (begin // 160 + 1) * 160)
                zh, x = divmod(begin // 160, 4)
                spot = 160 * zh + begin % 160
                at_ref[x, parity, spot : spot + end - begin] = turned[begin - 128 * n : end - 128 * n]
                begin = end
        if n % 5 == 4:
            half = n // 5
            spot = half_rows(xt_ref, slot, half)
            for k in (2, 1, 3, 0):
                x = p.along_x(k)
                src = half_rows(at_ref, x, half)
                if k == 0:
                    moves.push(src, spot, p.at(c=core), a + 4 * half, a + 4 * half + slot, core != p.c)
                    moves.keep(src, spot, core == p.c)
                else:
                    moves.push(src, spot, p.at(x=x, c=core), a + 4 * half + k, a + 4 * half + slot)
    base = 8 * p.zh + 4 * p.c
    halo = []
    for up, bound_ref in ((True, low_ref), (False, high_ref)):
        e = moves.slots(4)
        if up:
            sends = jnp.logical_and(lax.rem(p.s, 4) == 3, p.s != 15)
            block = lax.rem(p.s + 1, 16)
        else:
            sends = jnp.logical_and(lax.rem(p.s, 4) == 0, p.s != 0)
            block = lax.rem(p.s + 15, 16)
        zh, c = lax.div(block, 8), lax.div(lax.rem(block, 8), 4)
        for k in range(4):
            x = p.along_x(k)
            src = edge_ref.at[1 if up else 0]
            target = p.at(x=x, zh=zh, c=c)
            if k == 0:
                alone = jnp.logical_and(zh == p.zh, c == p.c)
                moves.push(src, bound_ref, target, e, e, jnp.logical_and(sends, jnp.logical_not(alone)))
                moves.keep(src, bound_ref, jnp.logical_and(sends, alone))
            else:
                moves.push(src, bound_ref, target, e + k, e, sends)
        if up:
            halo.append(arrival(bound_ref, e, jnp.logical_and(base != 0, base - 1 != p.s)))
        else:
            halo.append(arrival(bound_ref, e, jnp.logical_and(base != 12, base + 4 != p.s)))

    for head in range(2):
        lanes = slice(192 * head, 192 * head + 192)
        keys, values, queries = (hw_ref[n, :, lanes].astype(F32) for n in (1, 2, 0))
        pairs = (jnp.concatenate([keys, values], axis=1), jnp.concatenate([queries, ow_ref[:, lanes].astype(F32)], axis=1))
        for column in range(2):
            for row in range(2):
                wp_ref[head, 2 * row + column] = pairs[column][48 * row : 48 * row + 48].astype(BF16)

    def quarter(zh, x, c, d):
        rows = pl.ds(pl.multiple_of(48 * lax.div(d, 2), 16), 48)
        columns = pl.ds(pl.multiple_of(384 * lax.rem(d, 2), 128), 384)
        return wf_ref.at[zh, x, c, rows, columns]

    def quarters(c, d):
        rows = pl.ds(pl.multiple_of(48 * lax.div(d, 2), 16), 48)
        columns = pl.ds(pl.multiple_of(384 * lax.rem(d, 2), 128), 384)
        return wf_ref.at[:, :, c, rows, columns]

    w = moves.slots(8)
    shard = 4 * p.zh + p.x
    own_quarter = quarter(p.zh, p.x, p.c, p.d)
    quarter_arrivals = []
    for k in range(8):
        other = lax.rem(shard + k, 8)
        zh, x = lax.div(other, 4), lax.rem(other, 4)
        src = wp_ref.at[zh, p.d]
        if k == 0:
            copy = pltpu.make_async_copy(src, own_quarter, local.at[moves.used_local])
            moves.used_local += 1
            copy.start()
            quarter_arrivals.append(copy.wait)
        else:
            moves.push(src, own_quarter, p.at(x=x, zh=zh), w + k)
            other = lax.rem(shard + 8 - k, 8)
            quarter_arrivals.append(arrival(quarter(lax.div(other, 4), lax.rem(other, 4), p.c, p.d), w + k))

    moves.arrival(fifth(other_half, p.c, p.d), first)()
    got = fifth(other_half, p.c, p.d)
    for k in (2, 1, 3):
        moves.push(got, got, p.at(d=p.along_y(k)), first + 3 + k)
    moves.push(got, got, p.sibling, first + 3)
    got = fifth(other_half, p.c, 4)
    moves.arrival(got, first + 1)()
    moves.push(got, got, p.sibling, first + 7)
    for k in (1, 3, 2):
        got = fifth(other_half, p.c, p.along_y(4 - k))
        moves.arrival(got, first + 3 + k)()
        moves.push(got, got, p.sibling, first + 7 + k)
    for wait in quarter_arrivals:
        wait()
    y = moves.slots(8)
    moves.push(quarters(p.c, p.d), quarters(p.c, p.d), p.sibling, y)
    for k in (2, 1, 3):
        moves.push(quarters(p.c, p.d), quarters(p.c, p.d), p.at(d=p.along_y(k)), y + k)

    for n in range(4):
        x, c = 2 * p.c + n // 2, n % 2
        for half in range(2):
            arrival(half_rows(xt_ref, n, half), a + 4 * half + n, jnp.logical_or(x != p.x, c != p.c))()
    for wait in halo:
        wait()
    for when, wait in moves.locals:
        under(when, wait)
    moves.locals = []
    row = lax.broadcasted_iota(jnp.int32, (16, 128), 0)
    column = lax.broadcasted_iota(jnp.int32, (16, 128), 1)
    zero_rows = jnp.zeros((16, 1280), BF16)
    ends = []
    for there, bound_ref, shift in ((base != 0, low_ref, 14), (base != 12, high_ref, 0)):
        pick = (row == column + shift).astype(BF16)
        end_ref[...] = dot(jnp.where(there, bound_ref[...], zero_rows), pick, TN)
        lower = pl.multiple_of(160 * p.x, 32)
        ends.append(jnp.concatenate([end_ref[pl.ds(lower, 160)], end_ref[pl.ds(640 + lower, 160)]], axis=0))
    low, high = ends
    even = jnp.concatenate([xt_ref[n, 0] for n in range(4)], axis=1).astype(F32)
    odd = jnp.concatenate([xt_ref[n, 1] for n in range(4)], axis=1).astype(F32)
    lane = lax.broadcasted_iota(jnp.int32, (320, 512), 1)
    both = even + odd
    x5_ref[pl.ds(640, 320), :] = both.astype(BF16)
    x5_ref[pl.ds(0, 320), :] = jnp.where(lane == 0, low[:, 0:1] + low[:, 1:2], pltpu.roll(both, 1, 1)).astype(BF16)
    x5_ref[pl.ds(1280, 320), :] = jnp.where(
        lane == 511, high[:, 0:1] + high[:, 1:2], pltpu.roll(both, 511, 1)
    ).astype(BF16)
    x5_ref[pl.ds(320, 320), :] = (even + jnp.where(lane == 0, low[:, 1:2], pltpu.roll(odd, 1, 1))).astype(BF16)
    x5_ref[pl.ds(960, 320), :] = (odd + jnp.where(lane == 511, high[:, 0:1], pltpu.roll(even, 511, 1))).astype(BF16)
    arrival(cwf_ref.at[:, 2 * p.zh + 1 - p.c], first + 2)()
    arrival(fifth(other_half, 1 - p.c, p.d), first + 3)()
    arrival(fifth(other_half, 1 - p.c, 4), first + 7)()
    for k in (1, 3, 2):
        arrival(fifth(other_half, 1 - p.c, p.along_y(4 - k)), first + 7 + k)()
    x5t_ref[...] = x5_ref[...].T
    b = moves.slots(8)
    pieces = ((0, 512), (512, 256))
    for piece, (lower, width) in enumerate(pieces):
        lanes = pl.ds(lower, width)
        conv = dot(x5t_ref[...], cwf_ref[:, :, :, lanes].reshape(1600, width), NN) * 0.5
        for slot in range(4):
            part_ref[slot, :, lanes] = conv[128 * slot : 128 * slot + 128].astype(BF16)
            x, c = 2 * p.c + slot // 2, slot % 2
            alone = jnp.logical_and(x == p.x, c == p.c)
            src, dst = part_ref.at[slot, :, lanes], rs_ref.at[p.x, :, lanes]
            moves.push(src, dst, p.at(x=x, c=c), b + 4 * piece + slot, b + 4 * piece + p.x, jnp.logical_not(alone))
            moves.keep(src, dst, alone)
    other_x5 = moves.slots(1)
    moves.push(x5_ref, x5s_ref, p.sibling, other_x5)
    for when, wait in moves.locals:
        under(when, wait)
    moves.locals = []
    g = moves.slots(8)
    for piece, (lower, width) in enumerate(pieces):
        lanes = pl.ds(lower, width)
        for x in range(4):
            arrival(rs_ref.at[x, :, lanes], b + 4 * piece + x, jnp.logical_or(p.x != x, core != p.c))()
        total = rs_ref[0, :, lanes].astype(F32)
        for x in range(1, 4):
            total = total + rs_ref[x, :, lanes].astype(F32)
        sec_ref[:, lanes] = total.astype(BF16)
        secs_ref[p.z, :, lanes] = total.astype(BF16)
        for k in (2, 1, 3):
            moves.push(sec_ref.at[:, lanes], secs_ref.at[p.z, :, lanes], p.at_z(p.along_z(k)), g + 4 * piece + k)

    for k in (1, 3, 2):
        d = p.along_y(4 - k)
        arrival(quarters(p.c, d), y + k)()
        moves.push(quarters(p.c, d), quarters(p.c, d), p.sibling, y + 3 + k)
    arrival(quarters(1 - p.c, p.d), y)()
    for k in (1, 3, 2):
        arrival(quarters(1 - p.c, p.along_y(4 - k)), y + 3 + k)()

    def kv_rows(zh):
        return wf_ref[zh, :, :, :, :640].reshape(768, 640)

    def output_rows(zh):
        return wf_ref[zh, :, :, :, 512:].reshape(768, 256)

    def channels(ref, t):
        return jnp.concatenate([ref[t], ref[2 + t]], axis=0)

    wide_lane = lax.broadcasted_iota(jnp.int32, (256, 256), 1)

    for k in (2, 1, 3):
        for piece, (lower, width) in enumerate(pieces):
            arrival(secs_ref.at[p.along_z(4 - k), :, pl.ds(lower, width)], g + 4 * piece + k)()
    cot_first = moves.slots(4)
    cot_own = pltpu.make_async_copy(cot_ref, cots_ref.at[p.z], local.at[moves.used_local])
    moves.used_local += 1
    cot_own.start()
    cot_arrivals = [cot_own.wait]
    for k in (2, 1, 3):
        moves.push(cot_ref, cots_ref.at[p.z], p.at_z(p.along_z(k)), cot_first + k)
        cot_arrivals.append(arrival(cots_ref.at[p.along_z(4 - k)], cot_first + k))
    o = moves.slots(4)
    for zh in range(2):
        left, right = secs_ref[2 * zh].astype(F32), secs_ref[2 * zh + 1].astype(F32)
        squares = jnp.sum(left * left, axis=1, keepdims=True) + jnp.sum(right * right, axis=1, keepdims=True)
        inverse = lax.rsqrt(squares * (1.0 / 1536) + EPSILON)
        inv_ref[zh] = jnp.broadcast_to(inverse, (128, 128))
        nb_ref[2 * zh] = (left * inverse).astype(BF16)
        nb_ref[2 * zh + 1] = (right * inverse).astype(BF16)
    projected = dot(channels(nb_ref, 0), kv_rows(0), NN) + dot(channels(nb_ref, 1), kv_rows(1), NN)
    kv_ref[p.c, p.x] = projected[:, :384].astype(BF16)
    query = jnp.where(wide_lane < 192, projected[:, 384:], 0.0).astype(BF16)
    q = moves.slots(8)
    mine = kv_ref.at[p.c, p.x]
    for k in (2, 1, 3):
        moves.push(mine, mine, p.at(x=p.along_x(k)), q + k)
    moves.push(mine, mine, p.sibling, q)
    for zh in range(2):
        nl_ref[zh] = nb_ref[2 * zh + p.c]
        moves.push(nb_ref.at[2 * zh + 1 - p.c], nl_ref.at[2 + zh], p.sibling, o + 2 + zh)
    for k in (1, 3, 2):
        spot = kv_ref.at[p.c, p.along_x(4 - k)]
        arrival(spot, q + k)()
        moves.push(spot, spot, p.sibling, q + 3 + k)
    arrival(kv_ref.at[1 - p.c, p.x], q)()
    for k in (1, 3, 2):
        arrival(kv_ref.at[1 - p.c, p.along_x(4 - k)], q + 3 + k)()

    highest = None
    for n in range(8):
        scores = dot(kv_ref[n // 4, n % 4, :, :256], query, NT) * scale
        st_ref[n] = scores
        top = jnp.max(scores, axis=0, keepdims=True)
        highest = top if highest is None else jnp.maximum(highest, top)
    sums = jnp.zeros((1, 256), F32)
    for n in range(8):
        unnormed = jnp.exp(st_ref[n] - highest)
        st_ref[n] = unnormed
        sums = sums + jnp.sum(unnormed, axis=0, keepdims=True)
    share = 1.0 / sums
    for wait in cot_arrivals:
        wait()
    for zh in range(2):
        cl_ref[zh] = cots_ref[2 * zh + p.c]
        moves.push(cots_ref.at[2 * zh + 1 - p.c], cl_ref.at[2 + zh], p.sibling, o + zh)
    grad_att = dot(channels(cots_ref, 0), output_rows(0), NN) + dot(channels(cots_ref, 1), output_rows(1), NN)
    grad_att = jnp.where(wide_lane < 64, 0.0, grad_att).astype(BF16)
    centre = jnp.zeros((1, 256), F32)
    for n in range(8):
        weights = st_ref[n] * share
        grad_prob = dot(kv_ref[n // 4, n % 4, :, 128:], grad_att, NT)
        centre = centre + jnp.sum(weights * grad_prob, axis=0, keepdims=True)
        st_ref[n] = weights
        dp_ref[n] = grad_prob
        p16_ref[n] = weights.astype(BF16)
    r = moves.slots(8)

    def key_grads(c, x):
        n = 4 * c + x
        grad_score = (st_ref[n] * (dp_ref[n] - centre)).astype(BF16)
        ds_ref[n] = grad_score
        keys = dot(grad_score, query, NN) * scale
        values = dot(p16_ref[n], grad_att, NN)
        return jnp.concatenate([keys[:, :128], keys[:, 128:] + values[:, :128], values[:, 128:]], axis=1)

    for k in (2, 1, 3, 0):
        dkv_ref[k] = key_grads(1 - p.c, p.along_x(k)).astype(BF16)
        moves.push(dkv_ref.at[k], buf_ref.at[k], p.sibling, r + k)
    for k in (2, 1, 3, 0):
        x = p.along_x(k)
        here = key_grads(p.c, x)
        arrival(buf_ref.at[k], r + k)()
        sum_ref[k] = (here + buf_ref[k].astype(F32)).astype(BF16)
        if k:
            moves.push(sum_ref.at[k], dkvs_ref.at[p.x], p.at(x=x), r + 4 + k)
    dkvs_ref[p.x] = sum_ref[0]

    def rows8(ref, first, last):
        return ref[:, :, :, first:last].reshape(2048, last - first)

    attended = dot(p16_ref[...].reshape(2048, 256), rows8(kv_ref, 128, 384), TN)
    attended = jnp.where(wide_lane < 64, 0.0, attended).astype(BF16)
    grad_query = dot(ds_ref[...].reshape(2048, 256), rows8(kv_ref, 0, 256), TN) * scale
    grad_query = jnp.where(wide_lane < 192, grad_query, 0.0).astype(BF16)
    grads_ref[0, :, :128] = grad_query[:, :128]
    grads_ref[0, :, 128:256] = grad_query[:, 128:] + attended[:, :128]
    grads_ref[0, :, 256:] = attended[:, 128:]
    h = moves.slots(12)
    moves.push(grads_ref.at[0], others_ref.at[0], p.sibling, h)
    u = moves.slots(4)
    for t in range(2):
        block = dot(attended, output_rows(t), NT).astype(BF16)
        bo_ref[t] = block[:128]
        bo_ref[2 + t] = block[128:]
    for k in (2, 1, 3):
        z = p.along_z(k)
        moves.push(bo_ref.at[z], bos_ref.at[p.z], p.at_z(z), u + k)
    bos_ref[p.z] = bo_ref[p.z]

    def share_rows(part, values):
        for n in range(8):
            for d in range(4):
                row = 96 * n + 24 * d
                hg_ref[part, d, n] = values[row : row + 24].astype(BF16)
        for k in (2, 1, 3):
            d = p.along_y(k)
            moves.push(hg_ref.at[part, d], hgs_ref.at[part, p.d], p.at(d=d), h + 4 + 4 * part + k)
        hgs_ref[part, p.d] = hg_ref[part, p.d]

    def all_bins(part):
        return jnp.concatenate([grads_ref[part], others_ref[part]], axis=0)

    for n in range(4):
        arrival((cl_ref if n < 2 else nl_ref).at[2 + n % 2], o + n)()
    arrival(others_ref.at[0], h)()
    grads = all_bins(0)
    head_part = dot(nl_ref[...].reshape(512, 768), grads[:, :256], TN)
    output_part = dot(cl_ref[...].reshape(512, 768), grads[:, 128:], TN)
    tile_lane = lax.broadcasted_iota(jnp.int32, (768, 128), 1)
    middle = jnp.where(tile_lane < 64, head_part[:, 128:], output_part[:, :128])
    share_rows(0, jnp.concatenate([head_part[:, :128], middle, output_part[:, 128:]], axis=1))

    for k in (1, 3, 2):
        arrival(dkvs_ref.at[p.along_x(4 - k)], r + 4 + k)()
    total = dkvs_ref[0].astype(F32)
    for x in range(1, 4):
        total = total + dkvs_ref[x].astype(F32)
    grad_kv = total.astype(BF16)
    grads_ref[1] = grad_kv
    moves.push(grads_ref.at[1], others_ref.at[1], p.sibling, h + 1)
    grad_proj = jnp.concatenate([grad_kv, grad_query], axis=1)
    spread = jnp.zeros((256, 1), F32)
    for t in range(2):
        block = dot(grad_proj, kv_rows(t), NT)
        spread = spread + jnp.sum(block * channels(secs_ref, t).astype(F32), axis=1, keepdims=True)
        rounded = block.astype(BF16)
        for zh in range(2):
            rows = slice(128 * zh, 128 * zh + 128)
            for c in range(2):
                norma_ref[2 * zh + t, :, 128 * c : 128 * c + 128] = rounded[rows, 384 * c : 384 * c + 128]
                normb_ref[2 * zh + t, :, 256 * c : 256 * c + 256] = rounded[rows, 384 * c + 128 : 384 * c + 384]
    spread = spread * (1.0 / 1536)
    for zh in range(2):
        spread_ref[zh] = jnp.broadcast_to(spread[128 * zh : 128 * zh + 128], (128, 128)).T[:8]
    m = moves.slots(12)
    for k in (2, 1, 3):
        z = p.along_z(k)
        moves.push(spread_ref.at[lax.div(z, 2)], spreads_ref.at[p.z], p.at_z(z), m + 8 + k)
        moves.push(norma_ref.at[z], normsa_ref.at[p.z], p.at_z(z), m + k)
    normsa_ref[p.z] = norma_ref[p.z]
    normsb_ref[p.z] = normb_ref[p.z]
    spreads_ref[p.z] = spread_ref[p.zh]
    for k in (1, 3, 2):
        arrival(normsa_ref.at[p.along_z(4 - k)], m + k)()
        arrival(spreads_ref.at[p.along_z(4 - k)], m + 8 + k)()
    for k in (2, 1, 3):
        z = p.along_z(k)
        moves.push(normb_ref.at[z], normsb_ref.at[p.z], p.at_z(z), m + 4 + k)

    mean = spreads_ref[0]
    for z in range(1, 4):
        mean = mean + spreads_ref[z]
    mean = jnp.concatenate([mean] * 16, axis=0).T[:, :1]
    inverse = inv_ref[p.zh][:, :1]
    factor = inverse * inverse * inverse * mean
    block = 2 * p.x + p.c
    j = moves.slots(16)

    def pool(norms, gp, gps, lower, width):
        for c in range(2):
            lanes = pl.ds(384 * c + lower, width)
            here = pl.ds(width * c, width)
            grad_normed = norms[0, :, here].astype(F32)
            for z in range(1, 4):
                grad_normed = grad_normed + norms[z, :, here].astype(F32)
            grad_section = cots_ref[p.z, :, lanes].astype(F32) + inverse * grad_normed
            grad_section = grad_section - factor * sec_ref[:, lanes].astype(F32)
            gp[c] = (0.5 * grad_section).astype(BF16)
        gps[block] = gp[p.c]

    def pool_sends(gp, gps, first):
        for k in (4, 5, 2, 3, 6, 7, 1):
            other = lax.rem(block + k, 8)
            x, c = lax.div(other, 2), lax.rem(other, 2)
            moves.push(gp.at[c], gps.at[block], p.at(x=x, c=c), first + k)

    def pool_arrivals(gps, first):
        for k in (1, 7, 6, 2, 3, 4, 5):
            arrival(gps.at[lax.rem(block + 8 - k, 8)], first + k)()

    pool(normsa_ref, gpa_ref, gpsa_ref, 0, 128)
    pool_sends(gpa_ref, gpsa_ref, j)
    arrival(others_ref.at[1], h + 1)()
    share_rows(1, dot(nl_ref[...].reshape(512, 768), all_bins(1), TN))
    for k in (1, 3, 2):
        arrival(normsb_ref.at[p.along_z(4 - k)], m + 4 + k)()
    pool(normsb_ref, gpb_ref, gpsb_ref, 128, 256)
    pool_arrivals(gpsa_ref, j)
    pool_sends(gpb_ref, gpsb_ref, j + 8)

    arrival(x5s_ref, other_x5)()
    e = moves.slots(32)
    me = 8 * p.zh + 4 * p.c + p.d

    def conv_grad(gps, cg, cgs, lower, width, first):
        here = gps[pl.ds(4 * p.c, 4)].reshape(512, width)
        there = gps[pl.ds(4 - 4 * p.c, 4)].reshape(512, width)
        cgf_ref[:, lower : lower + width] = dot(x5_ref[...], here, NN) + dot(x5s_ref[...], there, NN)
        for n in range(16):
            for tap in range(5):
                cgm_ref[n % 2, pl.ds(20 * tap, 20), lower : lower + width] = cgf_ref[
                    pl.ds(320 * tap + 20 * n, 20), lower : lower + width
                ]
            cg[n] = cgm_ref[n % 2, :, lower : lower + width].astype(BF16)
        for k in (10, 14, 2, 6, 8, 12, 4, 9, 11, 13, 15, 1, 3, 5, 7):
            other = lax.rem(me + k, 16)
            zh, c, d = lax.div(other, 8), lax.rem(lax.div(other, 4), 2), lax.rem(other, 4)
            moves.push(cg.at[other], cgs.at[me], p.at(zh=zh, c=c, d=d), first + k)
        cgs[me] = cg[me]

    conv_grad(gpsa_ref, cga_ref, cgsa_ref, 0, 128, e)
    pool_arrivals(gpsb_ref, j + 8)
    conv_grad(gpsb_ref, cgb_ref, cgsb_ref, 128, 256, e + 16)

    for k in (1, 3, 2):
        arrival(bos_ref.at[p.along_z(4 - k)], u + k)()
    total = sec_ref[...].astype(F32)
    projected_out = bos_ref[0].astype(F32)
    for z in range(1, 4):
        projected_out = projected_out + bos_ref[z].astype(F32)
    out_ref[...] = (total + projected_out).astype(BF16)

    f = moves.slots(8)
    for part in range(2):
        for k in (1, 3, 2):
            arrival(hgs_ref.at[part, p.along_y(4 - k)], h + 4 + 4 * part + k)()
        rows = hgs_ref[part, 0].astype(F32)
        for d in range(1, 4):
            rows = rows + hgs_ref[part, d].astype(F32)
        rows = rows.astype(BF16)
        lanes = pl.ds(384 - 384 * part, 384)
        for n in range(8):
            hgo_ref[n // 2, n % 2, :, lanes] = rows[n]
    for k in (2, 3, 4, 5, 6, 7, 0, 1):
        other = lax.rem(2 * p.x + k, 8)
        x, c = lax.div(other, 2), lax.rem(other, 2)
        src, dst = hgo_ref.at[x, c], hgl_ref.at[p.zh, p.x]
        if k < 2:
            alone = jnp.logical_and(jnp.logical_and(x == p.x, c == p.c), p.zh == p.c)
            moves.push(src, dst, p.at(x=x, zh=p.c, c=c), f + k, f + 4 * p.zh + p.x, jnp.logical_not(alone))
            moves.keep(src, dst, alone)
        else:
            moves.push(src, dst, p.at(x=x, zh=p.c, c=c), f + k, f + 4 * p.zh + p.x)
    for zh in range(2):
        for x in range(4):
            alone = jnp.logical_and(jnp.logical_and(x == p.x, zh == p.zh), p.zh == p.c)
            arrival(hgl_ref.at[zh, x], f + 4 * zh + x, jnp.logical_not(alone))()
    for when, wait in moves.locals:
        under(when, wait)
    moves.locals = []
    heads = []
    for zh in range(2):
        rows = hgl_ref[zh, 0].astype(F32)
        for x in range(1, 4):
            rows = rows + hgl_ref[zh, x].astype(F32)
        heads.append(rows)
    for n, first in enumerate((384, 0, 192, 576)):
        piece = jnp.concatenate([rows[:, first : first + 192] for rows in heads], axis=1)
        if n < 3:
            head_ref[n] = piece
        else:
            output_ref[...] = piece
    for cgs, lower, width, first in ((cgsa_ref, 0, 128, e), (cgsb_ref, 128, 256, e + 16)):
        for k in range(1, 16):
            arrival(cgs.at[lax.rem(me + 16 - k, 16)], first + k)()
        for c in range(2):
            total = None
            for zh in range(2):
                for d in range(4):
                    part = cgs[8 * zh + 4 * c + d].astype(F32)
                    total = part if total is None else total + part
            lanes = slice(lower, lower + width)
            cgm_ref[c, :, lanes] = total
            for tap in range(5):
                conv_ref[tap, :, 384 * c + lower : 384 * c + lower + width] = cgm_ref[c, pl.ds(20 * tap, 20), lanes]
    moves.settle()


def main_call(section_input, cw, hw, ow, cot):
    anywhere = pl.BlockSpec(memory_space=pl.ANY)
    inside = pl.BlockSpec(memory_space=pltpu.VMEM)

    def vmem(*dims, dtype=BF16):
        return pltpu.VMEM(dims, dtype)

    scratch = [
        vmem(10, 256, 128, dtype=F32), vmem(4, 2, 320, 128), vmem(2, 16, 1280), vmem(2, 4, 48, 384),
        vmem(1280, 128, dtype=F32), vmem(4, 2, 320, 128), vmem(16, 1280), vmem(16, 1280),
        vmem(5, 4, 80, 768), vmem(2, 4, 2, 96, 768), vmem(4, 128, 768),
        vmem(1600, 512), vmem(512, 1600), vmem(1600, 512), vmem(4, 128, 768), vmem(4, 128, 768),
        vmem(128, 768), vmem(4, 128, 768), vmem(2, 128, 128, dtype=F32),
        vmem(4, 128, 768), vmem(4, 128, 768), vmem(4, 128, 768),
        vmem(2, 4, 256, 384), vmem(8, 256, 256, dtype=F32), vmem(8, 256, 256, dtype=F32),
        vmem(8, 256, 256), vmem(8, 256, 256), vmem(4, 256, 384), vmem(4, 256, 384), vmem(4, 256, 384),
        vmem(4, 256, 384), vmem(4, 128, 768), vmem(4, 128, 768),
        vmem(2, 256, 384), vmem(2, 256, 384),
        vmem(4, 128, 256), vmem(4, 128, 512), vmem(4, 128, 256), vmem(4, 128, 512),
        vmem(2, 8, 128, dtype=F32), vmem(4, 8, 128, dtype=F32),
        vmem(2, 4, 8, 24, 384), vmem(2, 4, 8, 24, 384),
        vmem(2, 128, 128), vmem(2, 128, 256), vmem(8, 128, 128), vmem(8, 128, 256),
        vmem(4, 2, 24, 768), vmem(2, 4, 24, 768), vmem(1600, 384, dtype=F32), vmem(2, 104, 384, dtype=F32),
        vmem(16, 104, 128), vmem(16, 104, 256), vmem(16, 104, 128), vmem(16, 104, 256),
        pltpu.SemaphoreType.DMA((192,)), pltpu.SemaphoreType.DMA((192,)), pltpu.SemaphoreType.DMA((24,)),
    ]
    return pl.pallas_call(
        main_kernel,
        name="main",
        out_shape=(
            shape(128, 768),
            jax.ShapeDtypeStruct((5, 20, 768), F32),
            jax.ShapeDtypeStruct((3, 24, 384), F32),
            jax.ShapeDtypeStruct((24, 384), F32),
        ),
        in_specs=[inside, anywhere, inside, inside, anywhere],
        out_specs=(inside,) * 4,
        scratch_shapes=scratch,
        compiler_params=pltpu.CompilerParams(
            collective_id=1, has_side_effects=True, vmem_limit_bytes=60 * 1024 * 1024
        ),
    )(section_input, cw, hw, ow, cot)


def shape(*dims):
    return jax.ShapeDtypeStruct(dims, BF16)


def finish_kernel(*refs):
    for source, target in zip(refs[:4], refs[4:]):
        target[...] = source[...]


def finish(*arrays):
    inside = pl.BlockSpec(memory_space=pltpu.VMEM)
    return pl.pallas_call(
        finish_kernel,
        name="finish",
        out_shape=tuple(jax.ShapeDtypeStruct(array.shape, array.dtype) for array in arrays),
        in_specs=[inside] * 4,
        out_specs=(inside,) * 4,
    )(*arrays)


def local(section_input, conv_weight, head_weight, output_weight, cotangent):
    block_out, conv_grad, head_grad, output_grad = finish(
        *main_call(
            section_input[0], conv_weight.transpose(1, 0, 2), head_weight.transpose(1, 0, 2), output_weight, cotangent[0]
        )
    )
    return (block_out[None], conv_grad.transpose(1, 0, 2), head_grad.transpose(1, 0, 2), output_grad)


def solution(mesh):
    placed = (
        P("dp", "seq", None),
        P("seq", None, "tensor"),
        P("seq", None, "tensor"),
        P("seq", "tensor"),
        P("dp", "seq", "tensor"),
    )
    return jax.shard_map(
        local,
        mesh=mesh,
        in_specs=placed,
        out_specs=(
            P("dp", "seq", "tensor"),
            P(("seq", "dp"), None, "tensor"),
            P(("seq", "dp"), None, "tensor"),
            P(("seq", "dp"), "tensor"),
        ),
        check_vma=False,
    )
```

```python
import jax
import jax.numpy as jnp
from jax import lax
from jax.experimental import pallas as pl
from jax.experimental.pallas import tpu as pltpu
from jax.sharding import PartitionSpec as P

HEAD_DIM = 192
EPSILON = 1e-06
MESH = pl.DeviceIdType.MESH
BF16 = jnp.bfloat16
F32 = jnp.float32


class Place:
    def __init__(self):
        self.s = lax.axis_index("seq")
        self.zh = lax.div(self.s, 8)
        self.x = lax.rem(lax.div(self.s, 2), 4)
        self.c = lax.rem(self.s, 2)
        self.t = lax.axis_index("tensor")
        self.d = lax.axis_index("dp")
        self.z = 2 * self.zh + self.t

    def at(self, x=None, zh=None, c=None, t=None, d=None):
        x = self.x if x is None else x
        zh = self.zh if zh is None else zh
        c = self.c if c is None else c
        return {
            "seq": zh * 8 + x * 2 + c,
            "tensor": self.t if t is None else t,
            "dp": self.d if d is None else d,
        }

    def along_x(self, k):
        return lax.rem(self.x + k, 4)

    def along_y(self, k):
        return lax.rem(self.d + k, 4)

    def along_z(self, k):
        return lax.rem(self.z + k, 4)

    def at_z(self, z):
        return self.at(zh=lax.div(z, 2), t=lax.rem(z, 2))

    @property
    def sibling(self):
        return self.at(c=1 - self.c)


def remote(src, dst, send, recv, target):
    return pltpu.make_async_remote_copy(
        src_ref=src, dst_ref=dst, send_sem=send, recv_sem=recv, device_id=target, device_id_type=MESH
    )


def greet(targets):
    barrier = pltpu.get_barrier_semaphore()
    for condition, target in targets:
        if condition is None:
            pl.semaphore_signal(barrier, inc=1, device_id=target, device_id_type=MESH)
        else:

            @pl.when(condition)
            def _(target=target):
                pl.semaphore_signal(barrier, inc=1, device_id=target, device_id_type=MESH)

    return barrier


def under(condition, action):
    if condition is None:
        action()
    else:

        @pl.when(condition)
        def _():
            action()


class Moves:
    def __init__(self, place, send, recv, local):
        self.place, self.send, self.recv, self.local = place, send, recv, local
        self.sends, self.receives, self.locals = [], [], []
        self.used = 0
        self.used_local = 0

    def slots(self, count):
        first = self.used
        self.used += count
        return first

    def push(self, src, dst, target, slot, recv_slot=None, when=None):
        recv_slot = slot if recv_slot is None else recv_slot
        copy = remote(src, dst, self.send.at[slot], self.recv.at[recv_slot], target)
        under(when, copy.start)
        self.sends.append((when, copy.wait_send))

    def keep(self, src, dst, when=None):
        copy = pltpu.make_async_copy(src, dst, self.local.at[self.used_local])
        self.used_local += 1
        under(when, copy.start)
        self.locals.append((when, copy.wait))

    def arrival(self, dst, slot, when=None):
        place = self.place
        copy = remote(dst, dst, self.send.at[0], self.recv.at[slot], place.at())
        return lambda: under(when, copy.wait_recv)

    def expect(self, dst, slot, when=None):
        self.receives.append(self.arrival(dst, slot, when))

    def settle(self):
        for wait in self.receives:
            wait()
        for when, wait in self.locals + self.sends:
            under(when, wait)


def z_ring(p):
    return [(None, p.at_z(p.along_z(k))) for k in range(1, 4)]


def y_ring(p):
    return [(None, p.at(d=p.along_y(k))) for k in range(1, 4)]


def dot(a, b, dims):
    return lax.dot_general(a, b, (dims, ((), ())), preferred_element_type=F32)


NN = ((1,), (0,))
NT = ((1,), (1,))
TN = ((0,), (0,))


def main_kernel(
    input_ref, cw_ref, hw_ref, ow_ref, cot_ref,
    out_ref, conv_ref, head_ref, output_ref,
    act_ref, at_ref, edge_ref, wp_ref, end_ref, xt_ref, low_ref, high_ref, cwf_ref, wf_ref, cots_ref,
    x5_ref, x5t_ref, x5s_ref, part_ref, rs_ref, sec_ref, secs_ref, inv_ref, nb_ref, nl_ref, nlt_ref, cl_ref,
    kv_ref, st_ref, dp_ref, p16_ref, ds_ref, dkv_ref, buf_ref, sum_ref, dkvs_ref, bo_ref, bos_ref,
    grads_ref, others_ref, norma_ref, normb_ref, normsa_ref, normsb_ref, spread_ref, spreads_ref,
    hg_ref, hgs_ref, gpa_ref, gpb_ref, gpc_ref, gpsa_ref, gpsb_ref, gpsc_ref, hgo_ref, hgl_ref, cgf_ref, cgm_ref,
    cga_ref, cgb_ref, cgc_ref, cgsa_ref, cgsb_ref, cgsc_ref, send, recv, local,
):
    p = Place()
    scale = HEAD_DIM ** (-0.5)
    peers = [(None, {"seq": lax.rem(p.s + k, 16), "tensor": p.t, "dp": p.d}) for k in range(1, 16)]
    peers += [(None, p.at(t=1 - p.t)), (None, p.at(zh=1 - p.zh, t=1 - p.t))]
    for zh in range(2):
        for c in range(2):
            peers += [(None, p.at(zh=zh, c=c, d=p.along_y(k))) for k in range(1, 4)]
    barrier = greet(peers)
    pl.semaphore_wait(barrier, 29)
    moves = Moves(p, send, recv, local)
    arrival = moves.arrival

    first = moves.slots(12)

    def fifth(zh, c, n):
        return cwf_ref.at[:, 2 * zh + c, pl.ds(pl.multiple_of(16 * n, 16), 16), :]

    other_half = 1 - p.zh
    moves.push(cw_ref.at[:, pl.ds(pl.multiple_of(16 * p.d, 16), 16), :], fifth(p.zh, p.c, p.d), p.at(zh=other_half), first)
    moves.push(cw_ref.at[:, pl.ds(64, 16), :], fifth(p.zh, p.c, 4), p.at(zh=other_half), first + 1)
    mine = cwf_ref.at[:, 2 * p.zh + p.c]
    moves.push(cw_ref, mine, p.sibling, first + 2)
    moves.keep(cw_ref, mine)

    a = moves.slots(8)
    core = lax.div(p.x, 2)
    slot = 2 * lax.rem(p.x, 2) + p.c

    def half_rows(ref, index, half):
        return ref.at[index, :, pl.ds(160 * half, 160), :]

    for n in range(10):
        lanes = slice(128 * n, 128 * n + 128)
        rows = jax.nn.gelu(input_ref[:, lanes].astype(F32), approximate=True).astype(BF16)
        edge_ref[0, :, lanes] = rows[:16]
        edge_ref[1, :, lanes] = rows[240:]
        act_ref[n] = rows.astype(F32)
        for parity in range(2):
            turned = act_ref[n, pl.ds(parity, 128, stride=2), :].T.astype(BF16)
            begin = 128 * n
            while begin < 128 * n + 128:
                end = min(128 * n + 128, (begin // 160 + 1) * 160)
                zh, x = divmod(begin // 160, 4)
                spot = 160 * zh + begin % 160
                at_ref[x, parity, spot : spot + end - begin] = turned[begin - 128 * n : end - 128 * n]
                begin = end
        if n % 5 == 4:
            half = n // 5
            spot = half_rows(xt_ref, slot, half)
            for k in (2, 1, 3, 0):
                x = p.along_x(k)
                src = half_rows(at_ref, x, half)
                if k == 0:
                    moves.push(src, spot, p.at(c=core), a + 4 * half, a + 4 * half + slot, core != p.c)
                    moves.keep(src, spot, core == p.c)
                else:
                    moves.push(src, spot, p.at(x=x, c=core), a + 4 * half + k, a + 4 * half + slot)
    base = 8 * p.zh + 4 * p.c
    halo = []
    for up, bound_ref in ((True, low_ref), (False, high_ref)):
        e = moves.slots(4)
        if up:
            sends = jnp.logical_and(lax.rem(p.s, 4) == 3, p.s != 15)
            block = lax.rem(p.s + 1, 16)
        else:
            sends = jnp.logical_and(lax.rem(p.s, 4) == 0, p.s != 0)
            block = lax.rem(p.s + 15, 16)
        zh, c = lax.div(block, 8), lax.div(lax.rem(block, 8), 4)
        for k in range(4):
            x = p.along_x(k)
            src = edge_ref.at[1 if up else 0]
            target = p.at(x=x, zh=zh, c=c)
            if k == 0:
                alone = jnp.logical_and(zh == p.zh, c == p.c)
                moves.push(src, bound_ref, target, e, e, jnp.logical_and(sends, jnp.logical_not(alone)))
                moves.keep(src, bound_ref, jnp.logical_and(sends, alone))
            else:
                moves.push(src, bound_ref, target, e + k, e, sends)
        if up:
            halo.append(arrival(bound_ref, e, jnp.logical_and(base != 0, base - 1 != p.s)))
        else:
            halo.append(arrival(bound_ref, e, jnp.logical_and(base != 12, base + 4 != p.s)))

    for head in range(2):
        lanes = slice(192 * head, 192 * head + 192)
        keys, values, queries = (hw_ref[n, :, lanes].astype(F32) for n in (1, 2, 0))
        pairs = (jnp.concatenate([keys, values], axis=1), jnp.concatenate([queries, ow_ref[:, lanes].astype(F32)], axis=1))
        for column in range(2):
            for row in range(2):
                wp_ref[head, 2 * row + column] = pairs[column][48 * row : 48 * row + 48].astype(BF16)

    def quarter(zh, x, c, d):
        rows = pl.ds(pl.multiple_of(48 * lax.div(d, 2), 16), 48)
        columns = pl.ds(pl.multiple_of(384 * lax.rem(d, 2), 128), 384)
        return wf_ref.at[zh, x, c, rows, columns]

    def quarters(c, d):
        rows = pl.ds(pl.multiple_of(48 * lax.div(d, 2), 16), 48)
        columns = pl.ds(pl.multiple_of(384 * lax.rem(d, 2), 128), 384)
        return wf_ref.at[:, :, c, rows, columns]

    w = moves.slots(8)
    shard = 4 * p.zh + p.x
    own_quarter = quarter(p.zh, p.x, p.c, p.d)
    quarter_arrivals = []
    for k in range(8):
        other = lax.rem(shard + k, 8)
        zh, x = lax.div(other, 4), lax.rem(other, 4)
        src = wp_ref.at[zh, p.d]
        if k == 0:
            copy = pltpu.make_async_copy(src, own_quarter, local.at[moves.used_local])
            moves.used_local += 1
            copy.start()
            quarter_arrivals.append(copy.wait)
        else:
            moves.push(src, own_quarter, p.at(x=x, zh=zh), w + k)
            other = lax.rem(shard + 8 - k, 8)
            quarter_arrivals.append(arrival(quarter(lax.div(other, 4), lax.rem(other, 4), p.c, p.d), w + k))

    moves.arrival(fifth(other_half, p.c, p.d), first)()
    got = fifth(other_half, p.c, p.d)
    for k in (2, 1, 3):
        moves.push(got, got, p.at(d=p.along_y(k)), first + 3 + k)
    moves.push(got, got, p.sibling, first + 3)
    got = fifth(other_half, p.c, 4)
    moves.arrival(got, first + 1)()
    moves.push(got, got, p.sibling, first + 7)
    for k in (1, 3, 2):
        got = fifth(other_half, p.c, p.along_y(4 - k))
        moves.arrival(got, first + 3 + k)()
        moves.push(got, got, p.sibling, first + 7 + k)
    for wait in quarter_arrivals:
        wait()
    y = moves.slots(8)
    moves.push(quarters(p.c, p.d), quarters(p.c, p.d), p.sibling, y)
    for k in (2, 1, 3):
        moves.push(quarters(p.c, p.d), quarters(p.c, p.d), p.at(d=p.along_y(k)), y + k)

    for n in range(4):
        x, c = 2 * p.c + n // 2, n % 2
        for half in range(2):
            arrival(half_rows(xt_ref, n, half), a + 4 * half + n, jnp.logical_or(x != p.x, c != p.c))()
    for wait in halo:
        wait()
    for when, wait in moves.locals:
        under(when, wait)
    moves.locals = []
    row = lax.broadcasted_iota(jnp.int32, (16, 128), 0)
    column = lax.broadcasted_iota(jnp.int32, (16, 128), 1)
    zero_rows = jnp.zeros((16, 1280), BF16)
    ends = []
    for there, bound_ref, shift in ((base != 0, low_ref, 14), (base != 12, high_ref, 0)):
        pick = (row == column + shift).astype(BF16)
        end_ref[...] = dot(jnp.where(there, bound_ref[...], zero_rows), pick, TN)
        lower = pl.multiple_of(160 * p.x, 32)
        ends.append(jnp.concatenate([end_ref[pl.ds(lower, 160)], end_ref[pl.ds(640 + lower, 160)]], axis=0))
    low, high = ends
    even = jnp.concatenate([xt_ref[n, 0] for n in range(4)], axis=1).astype(F32)
    odd = jnp.concatenate([xt_ref[n, 1] for n in range(4)], axis=1).astype(F32)
    lane = lax.broadcasted_iota(jnp.int32, (320, 512), 1)
    both = even + odd
    x5_ref[pl.ds(640, 320), :] = both.astype(BF16)
    x5_ref[pl.ds(0, 320), :] = jnp.where(lane == 0, low[:, 0:1] + low[:, 1:2], pltpu.roll(both, 1, 1)).astype(BF16)
    x5_ref[pl.ds(1280, 320), :] = jnp.where(
        lane == 511, high[:, 0:1] + high[:, 1:2], pltpu.roll(both, 511, 1)
    ).astype(BF16)
    x5_ref[pl.ds(320, 320), :] = (even + jnp.where(lane == 0, low[:, 1:2], pltpu.roll(odd, 1, 1))).astype(BF16)
    x5_ref[pl.ds(960, 320), :] = (odd + jnp.where(lane == 511, high[:, 0:1], pltpu.roll(even, 511, 1))).astype(BF16)
    arrival(cwf_ref.at[:, 2 * p.zh + 1 - p.c], first + 2)()
    arrival(fifth(other_half, 1 - p.c, p.d), first + 3)()
    arrival(fifth(other_half, 1 - p.c, 4), first + 7)()
    for k in (1, 3, 2):
        arrival(fifth(other_half, 1 - p.c, p.along_y(4 - k)), first + 7 + k)()
    x5t_ref[...] = x5_ref[...].T
    b = moves.slots(8)
    pieces = ((0, 512), (512, 256))
    for piece, (lower, width) in enumerate(pieces):
        lanes = pl.ds(lower, width)
        conv = dot(x5t_ref[...], cwf_ref[:, :, :, lanes].reshape(1600, width), NN) * 0.5
        for slot in range(4):
            part_ref[slot, :, lanes] = conv[128 * slot : 128 * slot + 128].astype(BF16)
            x, c = 2 * p.c + slot // 2, slot % 2
            alone = jnp.logical_and(x == p.x, c == p.c)
            src, dst = part_ref.at[slot, :, lanes], rs_ref.at[p.x, :, lanes]
            moves.push(src, dst, p.at(x=x, c=c), b + 4 * piece + slot, b + 4 * piece + p.x, jnp.logical_not(alone))
            moves.keep(src, dst, alone)
    other_x5 = moves.slots(1)
    moves.push(x5_ref, x5s_ref, p.sibling, other_x5)
    for when, wait in moves.locals:
        under(when, wait)
    moves.locals = []
    g = moves.slots(8)
    for piece, (lower, width) in enumerate(pieces):
        lanes = pl.ds(lower, width)
        for x in range(4):
            arrival(rs_ref.at[x, :, lanes], b + 4 * piece + x, jnp.logical_or(p.x != x, core != p.c))()
        total = rs_ref[0, :, lanes].astype(F32)
        for x in range(1, 4):
            total = total + rs_ref[x, :, lanes].astype(F32)
        sec_ref[:, lanes] = total.astype(BF16)
        secs_ref[p.z, :, lanes] = total.astype(BF16)
        for k in (2, 1, 3):
            moves.push(sec_ref.at[:, lanes], secs_ref.at[p.z, :, lanes], p.at_z(p.along_z(k)), g + 4 * piece + k)

    for k in (1, 3, 2):
        d = p.along_y(4 - k)
        arrival(quarters(p.c, d), y + k)()
        moves.push(quarters(p.c, d), quarters(p.c, d), p.sibling, y + 3 + k)
    arrival(quarters(1 - p.c, p.d), y)()
    for k in (1, 3, 2):
        arrival(quarters(1 - p.c, p.along_y(4 - k)), y + 3 + k)()

    def kv_rows(zh):
        return wf_ref[zh, :, :, :, :640].reshape(768, 640)

    def output_rows(zh):
        return wf_ref[zh, :, :, :, 512:].reshape(768, 256)

    def channels(ref, t):
        return jnp.concatenate([ref[t], ref[2 + t]], axis=0)

    wide_lane = lax.broadcasted_iota(jnp.int32, (256, 256), 1)

    for k in (2, 1, 3):
        for piece, (lower, width) in enumerate(pieces):
            arrival(secs_ref.at[p.along_z(4 - k), :, pl.ds(lower, width)], g + 4 * piece + k)()
    cot_first = moves.slots(4)
    cot_own = pltpu.make_async_copy(cot_ref, cots_ref.at[p.z], local.at[moves.used_local])
    moves.used_local += 1
    cot_own.start()
    cot_arrivals = [cot_own.wait]
    for k in (2, 1, 3):
        moves.push(cot_ref, cots_ref.at[p.z], p.at_z(p.along_z(k)), cot_first + k)
        cot_arrivals.append(arrival(cots_ref.at[p.along_z(4 - k)], cot_first + k))
    o = moves.slots(4)
    for zh in range(2):
        left, right = secs_ref[2 * zh].astype(F32), secs_ref[2 * zh + 1].astype(F32)
        squares = jnp.sum(left * left, axis=1, keepdims=True) + jnp.sum(right * right, axis=1, keepdims=True)
        inverse = lax.rsqrt(squares * (1.0 / 1536) + EPSILON)
        inv_ref[zh] = jnp.broadcast_to(inverse, (128, 128))
        nb_ref[2 * zh] = (left * inverse).astype(BF16)
        nb_ref[2 * zh + 1] = (right * inverse).astype(BF16)
    projected = dot(channels(nb_ref, 0), kv_rows(0), NN) + dot(channels(nb_ref, 1), kv_rows(1), NN)
    kv_ref[p.c, p.x] = projected[:, :384].astype(BF16)
    query = jnp.where(wide_lane < 192, projected[:, 384:], 0.0).astype(BF16)
    q = moves.slots(8)
    mine = kv_ref.at[p.c, p.x]
    for k in (2, 1, 3):
        moves.push(mine, mine, p.at(x=p.along_x(k)), q + k)
    moves.push(mine, mine, p.sibling, q)
    for zh in range(2):
        nl_ref[zh] = nb_ref[2 * zh + p.c]
        moves.push(nb_ref.at[2 * zh + 1 - p.c], nl_ref.at[2 + zh], p.sibling, o + 2 + zh)
    for zh in range(2):
        arrival(nl_ref.at[2 + zh], o + 2 + zh)()
    nlt_ref[...] = nl_ref[...].reshape(512, 768).T
    for k in (1, 3, 2):
        spot = kv_ref.at[p.c, p.along_x(4 - k)]
        arrival(spot, q + k)()
        moves.push(spot, spot, p.sibling, q + 3 + k)
    arrival(kv_ref.at[1 - p.c, p.x], q)()
    for k in (1, 3, 2):
        arrival(kv_ref.at[1 - p.c, p.along_x(4 - k)], q + 3 + k)()

    highest = None
    for n in range(8):
        scores = dot(kv_ref[n // 4, n % 4, :, :256], query, NT) * scale
        st_ref[n] = scores
        top = jnp.max(scores, axis=0, keepdims=True)
        highest = top if highest is None else jnp.maximum(highest, top)
    sums = jnp.zeros((1, 256), F32)
    for n in range(8):
        unnormed = jnp.exp(st_ref[n] - highest)
        st_ref[n] = unnormed
        sums = sums + jnp.sum(unnormed, axis=0, keepdims=True)
    share = 1.0 / sums
    for wait in cot_arrivals:
        wait()
    for zh in range(2):
        cl_ref[zh] = cots_ref[2 * zh + p.c]
        moves.push(cots_ref.at[2 * zh + 1 - p.c], cl_ref.at[2 + zh], p.sibling, o + zh)
    grad_att = dot(channels(cots_ref, 0), output_rows(0), NN) + dot(channels(cots_ref, 1), output_rows(1), NN)
    grad_att = jnp.where(wide_lane < 64, 0.0, grad_att).astype(BF16)
    centre = jnp.zeros((1, 256), F32)
    for n in range(8):
        weights = st_ref[n] * share
        grad_prob = dot(kv_ref[n // 4, n % 4, :, 128:], grad_att, NT)
        centre = centre + jnp.sum(weights * grad_prob, axis=0, keepdims=True)
        st_ref[n] = weights
        dp_ref[n] = grad_prob
        p16_ref[n] = weights.astype(BF16)
    r = moves.slots(8)

    def key_grads(c, x):
        n = 4 * c + x
        grad_score = (st_ref[n] * (dp_ref[n] - centre)).astype(BF16)
        ds_ref[n] = grad_score
        keys = dot(grad_score, query, NN) * scale
        values = dot(p16_ref[n], grad_att, NN)
        return jnp.concatenate([keys[:, :128], keys[:, 128:] + values[:, :128], values[:, 128:]], axis=1)

    for k in (2, 1, 3, 0):
        dkv_ref[k] = key_grads(1 - p.c, p.along_x(k)).astype(BF16)
        moves.push(dkv_ref.at[k], buf_ref.at[k], p.sibling, r + k)
    for k in (2, 1, 3, 0):
        x = p.along_x(k)
        here = key_grads(p.c, x)
        arrival(buf_ref.at[k], r + k)()
        sum_ref[k] = (here + buf_ref[k].astype(F32)).astype(BF16)
        if k:
            moves.push(sum_ref.at[k], dkvs_ref.at[p.x], p.at(x=x), r + 4 + k)
    dkvs_ref[p.x] = sum_ref[0]

    def rows8(ref, first, last):
        return ref[:, :, :, first:last].reshape(2048, last - first)

    attended = dot(p16_ref[...].reshape(2048, 256), rows8(kv_ref, 128, 384), TN)
    attended = jnp.where(wide_lane < 64, 0.0, attended).astype(BF16)
    grad_query = dot(ds_ref[...].reshape(2048, 256), rows8(kv_ref, 0, 256), TN) * scale
    grad_query = jnp.where(wide_lane < 192, grad_query, 0.0).astype(BF16)
    grads_ref[0, :, :128] = grad_query[:, :128]
    grads_ref[0, :, 128:256] = grad_query[:, 128:] + attended[:, :128]
    grads_ref[0, :, 256:] = attended[:, 128:]
    h = moves.slots(12)
    moves.push(grads_ref.at[0], others_ref.at[0], p.sibling, h)
    u = moves.slots(4)
    for t in range(2):
        block = dot(attended, output_rows(t), NT).astype(BF16)
        bo_ref[t] = block[:128]
        bo_ref[2 + t] = block[128:]
    for k in (2, 1, 3):
        z = p.along_z(k)
        moves.push(bo_ref.at[z], bos_ref.at[p.z], p.at_z(z), u + k)
    bos_ref[p.z] = bo_ref[p.z]

    def share_rows(part, values):
        for n in range(8):
            for d in range(4):
                row = 96 * n + 24 * d
                hg_ref[part, d, n] = values[row : row + 24].astype(BF16)
        for k in (2, 1, 3):
            d = p.along_y(k)
            moves.push(hg_ref.at[part, d], hgs_ref.at[part, p.d], p.at(d=d), h + 4 + 4 * part + k)
        hgs_ref[part, p.d] = hg_ref[part, p.d]

    def all_bins(part):
        return jnp.concatenate([grads_ref[part], others_ref[part]], axis=0)

    for zh in range(2):
        arrival(cl_ref.at[2 + zh], o + zh)()
    arrival(others_ref.at[0], h)()
    grads = all_bins(0)
    head_part = dot(nlt_ref[...], grads[:, :256], NN)
    output_part = dot(cl_ref[...].reshape(512, 768), grads[:, 128:], TN)
    tile_lane = lax.broadcasted_iota(jnp.int32, (768, 128), 1)
    middle = jnp.where(tile_lane < 64, head_part[:, 128:], output_part[:, :128])
    share_rows(0, jnp.concatenate([head_part[:, :128], middle, output_part[:, 128:]], axis=1))

    for k in (1, 3, 2):
        arrival(dkvs_ref.at[p.along_x(4 - k)], r + 4 + k)()
    total = dkvs_ref[0].astype(F32)
    for x in range(1, 4):
        total = total + dkvs_ref[x].astype(F32)
    grad_kv = total.astype(BF16)
    grads_ref[1] = grad_kv
    moves.push(grads_ref.at[1], others_ref.at[1], p.sibling, h + 1)
    grad_proj = jnp.concatenate([grad_kv, grad_query], axis=1)
    spread = jnp.zeros((256, 1), F32)
    for t in range(2):
        block = dot(grad_proj, kv_rows(t), NT)
        spread = spread + jnp.sum(block * channels(secs_ref, t).astype(F32), axis=1, keepdims=True)
        rounded = block.astype(BF16)
        for zh in range(2):
            rows = slice(128 * zh, 128 * zh + 128)
            for c in range(2):
                norma_ref[2 * zh + t, :, 128 * c : 128 * c + 128] = rounded[rows, 384 * c : 384 * c + 128]
                normb_ref[2 * zh + t, :, 256 * c : 256 * c + 256] = rounded[rows, 384 * c + 128 : 384 * c + 384]
    spread = spread * (1.0 / 1536)
    for zh in range(2):
        spread_ref[zh] = jnp.broadcast_to(spread[128 * zh : 128 * zh + 128], (128, 128)).T[:8]
    m = moves.slots(12)
    for k in (2, 1, 3):
        z = p.along_z(k)
        moves.push(spread_ref.at[lax.div(z, 2)], spreads_ref.at[p.z], p.at_z(z), m + 8 + k)
        moves.push(norma_ref.at[z], normsa_ref.at[p.z], p.at_z(z), m + k)
    for k in (2, 1, 3):
        z = p.along_z(k)
        moves.push(normb_ref.at[z], normsb_ref.at[p.z], p.at_z(z), m + 4 + k)
    normsa_ref[p.z] = norma_ref[p.z]
    normsb_ref[p.z] = normb_ref[p.z]
    spreads_ref[p.z] = spread_ref[p.zh]
    for k in (1, 3, 2):
        arrival(normsa_ref.at[p.along_z(4 - k)], m + k)()
        arrival(spreads_ref.at[p.along_z(4 - k)], m + 8 + k)()

    mean = spreads_ref[0]
    for z in range(1, 4):
        mean = mean + spreads_ref[z]
    mean = jnp.concatenate([mean] * 16, axis=0).T[:, :1]
    inverse = inv_ref[p.zh][:, :1]
    factor = inverse * inverse * inverse * mean
    block = 2 * p.x + p.c
    j = moves.slots(24)

    def pool(norms, gp, gps, lower, width, stride, offset):
        for c in range(2):
            lanes = pl.ds(384 * c + lower, width)
            here = pl.ds(stride * c + offset, width)
            grad_normed = norms[0, :, here].astype(F32)
            for z in range(1, 4):
                grad_normed = grad_normed + norms[z, :, here].astype(F32)
            grad_section = cots_ref[p.z, :, lanes].astype(F32) + inverse * grad_normed
            grad_section = grad_section - factor * sec_ref[:, lanes].astype(F32)
            gp[c] = (0.5 * grad_section).astype(BF16)
        gps[block] = gp[p.c]

    def pool_sends(gp, gps, first):
        for k in (4, 5, 2, 3, 6, 7, 1):
            other = lax.rem(block + k, 8)
            x, c = lax.div(other, 2), lax.rem(other, 2)
            moves.push(gp.at[c], gps.at[block], p.at(x=x, c=c), first + k)

    def pool_arrivals(gps, first):
        for k in (1, 7, 6, 2, 3, 4, 5):
            arrival(gps.at[lax.rem(block + 8 - k, 8)], first + k)()

    pool(normsa_ref, gpa_ref, gpsa_ref, 0, 128, 128, 0)
    pool_sends(gpa_ref, gpsa_ref, j)
    arrival(others_ref.at[1], h + 1)()
    share_rows(1, dot(nlt_ref[...], all_bins(1), NN))
    for k in (1, 3, 2):
        arrival(normsb_ref.at[p.along_z(4 - k)], m + 4 + k)()
    pool(normsb_ref, gpb_ref, gpsb_ref, 128, 128, 256, 0)
    pool_sends(gpb_ref, gpsb_ref, j + 8)
    pool(normsb_ref, gpc_ref, gpsc_ref, 256, 128, 256, 128)
    pool_sends(gpc_ref, gpsc_ref, j + 16)
    pool_arrivals(gpsa_ref, j)

    arrival(x5s_ref, other_x5)()
    e = moves.slots(48)
    me = 8 * p.zh + 4 * p.c + p.d

    def conv_grad(gps, cg, cgs, lower, width, first):
        here = gps[pl.ds(4 * p.c, 4)].reshape(512, width)
        there = gps[pl.ds(4 - 4 * p.c, 4)].reshape(512, width)
        cgf_ref[:, lower : lower + width] = dot(x5_ref[...], here, NN) + dot(x5s_ref[...], there, NN)
        for n in range(16):
            for tap in range(5):
                cgm_ref[n % 2, pl.ds(20 * tap, 20), lower : lower + width] = cgf_ref[
                    pl.ds(320 * tap + 20 * n, 20), lower : lower + width
                ]
            cg[n] = cgm_ref[n % 2, :, lower : lower + width].astype(BF16)
        for k in (10, 14, 2, 6, 8, 12, 4, 9, 11, 13, 15, 1, 3, 5, 7):
            other = lax.rem(me + k, 16)
            zh, c, d = lax.div(other, 8), lax.rem(lax.div(other, 4), 2), lax.rem(other, 4)
            moves.push(cg.at[other], cgs.at[me], p.at(zh=zh, c=c, d=d), first + k)
        cgs[me] = cg[me]

    conv_grad(gpsa_ref, cga_ref, cgsa_ref, 0, 128, e)
    pool_arrivals(gpsb_ref, j + 8)
    conv_grad(gpsb_ref, cgb_ref, cgsb_ref, 128, 128, e + 16)
    pool_arrivals(gpsc_ref, j + 16)
    conv_grad(gpsc_ref, cgc_ref, cgsc_ref, 256, 128, e + 32)

    for k in (1, 3, 2):
        arrival(bos_ref.at[p.along_z(4 - k)], u + k)()
    total = sec_ref[...].astype(F32)
    projected_out = bos_ref[0].astype(F32)
    for z in range(1, 4):
        projected_out = projected_out + bos_ref[z].astype(F32)
    out_ref[...] = (total + projected_out).astype(BF16)

    f = moves.slots(8)
    for part in range(2):
        for k in (1, 3, 2):
            arrival(hgs_ref.at[part, p.along_y(4 - k)], h + 4 + 4 * part + k)()
        rows = hgs_ref[part, 0].astype(F32)
        for d in range(1, 4):
            rows = rows + hgs_ref[part, d].astype(F32)
        rows = rows.astype(BF16)
        lanes = pl.ds(384 - 384 * part, 384)
        for n in range(8):
            hgo_ref[n // 2, n % 2, :, lanes] = rows[n]
    for k in (2, 3, 4, 5, 6, 7, 0, 1):
        other = lax.rem(2 * p.x + k, 8)
        x, c = lax.div(other, 2), lax.rem(other, 2)
        src, dst = hgo_ref.at[x, c], hgl_ref.at[p.zh, p.x]
        if k < 2:
            alone = jnp.logical_and(jnp.logical_and(x == p.x, c == p.c), p.zh == p.c)
            moves.push(src, dst, p.at(x=x, zh=p.c, c=c), f + k, f + 4 * p.zh + p.x, jnp.logical_not(alone))
            moves.keep(src, dst, alone)
        else:
            moves.push(src, dst, p.at(x=x, zh=p.c, c=c), f + k, f + 4 * p.zh + p.x)
    for zh in range(2):
        for x in range(4):
            alone = jnp.logical_and(jnp.logical_and(x == p.x, zh == p.zh), p.zh == p.c)
            arrival(hgl_ref.at[zh, x], f + 4 * zh + x, jnp.logical_not(alone))()
    for when, wait in moves.locals:
        under(when, wait)
    moves.locals = []
    heads = []
    for zh in range(2):
        rows = hgl_ref[zh, 0].astype(F32)
        for x in range(1, 4):
            rows = rows + hgl_ref[zh, x].astype(F32)
        heads.append(rows)
    for n, first in enumerate((384, 0, 192, 576)):
        piece = jnp.concatenate([rows[:, first : first + 192] for rows in heads], axis=1)
        if n < 3:
            head_ref[n] = piece
        else:
            output_ref[...] = piece
    for cgs, lower, width, first in (
        (cgsa_ref, 0, 128, e),
        (cgsb_ref, 128, 128, e + 16),
        (cgsc_ref, 256, 128, e + 32),
    ):
        for k in range(1, 16):
            arrival(cgs.at[lax.rem(me + 16 - k, 16)], first + k)()
        for c in range(2):
            total = None
            for zh in range(2):
                for d in range(4):
                    part = cgs[8 * zh + 4 * c + d].astype(F32)
                    total = part if total is None else total + part
            lanes = slice(lower, lower + width)
            cgm_ref[c, :, lanes] = total
            for tap in range(5):
                conv_ref[tap, :, 384 * c + lower : 384 * c + lower + width] = cgm_ref[c, pl.ds(20 * tap, 20), lanes]
    moves.settle()


def main_call(section_input, cw, hw, ow, cot):
    anywhere = pl.BlockSpec(memory_space=pl.ANY)
    inside = pl.BlockSpec(memory_space=pltpu.VMEM)

    def vmem(*dims, dtype=BF16):
        return pltpu.VMEM(dims, dtype)

    scratch = [
        vmem(10, 256, 128, dtype=F32), vmem(4, 2, 320, 128), vmem(2, 16, 1280), vmem(2, 4, 48, 384),
        vmem(1280, 128, dtype=F32), vmem(4, 2, 320, 128), vmem(16, 1280), vmem(16, 1280),
        vmem(5, 4, 80, 768), vmem(2, 4, 2, 96, 768), vmem(4, 128, 768),
        vmem(1600, 512), vmem(512, 1600), vmem(1600, 512), vmem(4, 128, 768), vmem(4, 128, 768),
        vmem(128, 768), vmem(4, 128, 768), vmem(2, 128, 128, dtype=F32),
        vmem(4, 128, 768), vmem(4, 128, 768), vmem(768, 512), vmem(4, 128, 768),
        vmem(2, 4, 256, 384), vmem(8, 256, 256, dtype=F32), vmem(8, 256, 256, dtype=F32),
        vmem(8, 256, 256), vmem(8, 256, 256), vmem(4, 256, 384), vmem(4, 256, 384), vmem(4, 256, 384),
        vmem(4, 256, 384), vmem(4, 128, 768), vmem(4, 128, 768),
        vmem(2, 256, 384), vmem(2, 256, 384),
        vmem(4, 128, 256), vmem(4, 128, 512), vmem(4, 128, 256), vmem(4, 128, 512),
        vmem(2, 8, 128, dtype=F32), vmem(4, 8, 128, dtype=F32),
        vmem(2, 4, 8, 24, 384), vmem(2, 4, 8, 24, 384),
        vmem(2, 128, 128), vmem(2, 128, 128), vmem(2, 128, 128),
        vmem(8, 128, 128), vmem(8, 128, 128), vmem(8, 128, 128),
        vmem(4, 2, 24, 768), vmem(2, 4, 24, 768), vmem(1600, 384, dtype=F32), vmem(2, 104, 384, dtype=F32),
        vmem(16, 104, 128), vmem(16, 104, 128), vmem(16, 104, 128),
        vmem(16, 104, 128), vmem(16, 104, 128), vmem(16, 104, 128),
        pltpu.SemaphoreType.DMA((200,)), pltpu.SemaphoreType.DMA((200,)), pltpu.SemaphoreType.DMA((24,)),
    ]
    return pl.pallas_call(
        main_kernel,
        name="main",
        out_shape=(
            shape(128, 768),
            jax.ShapeDtypeStruct((5, 20, 768), F32),
            jax.ShapeDtypeStruct((3, 24, 384), F32),
            jax.ShapeDtypeStruct((24, 384), F32),
        ),
        in_specs=[inside, anywhere, inside, inside, anywhere],
        out_specs=(inside,) * 4,
        scratch_shapes=scratch,
        compiler_params=pltpu.CompilerParams(
            collective_id=1, has_side_effects=True, vmem_limit_bytes=60 * 1024 * 1024
        ),
    )(section_input, cw, hw, ow, cot)


def shape(*dims):
    return jax.ShapeDtypeStruct(dims, BF16)


def finish_kernel(*refs):
    for source, target in zip(refs[:4], refs[4:]):
        target[...] = source[...]


def finish(*arrays):
    inside = pl.BlockSpec(memory_space=pltpu.VMEM)
    return pl.pallas_call(
        finish_kernel,
        name="finish",
        out_shape=tuple(jax.ShapeDtypeStruct(array.shape, array.dtype) for array in arrays),
        in_specs=[inside] * 4,
        out_specs=(inside,) * 4,
    )(*arrays)


def local(section_input, conv_weight, head_weight, output_weight, cotangent):
    block_out, conv_grad, head_grad, output_grad = finish(
        *main_call(
            section_input[0], conv_weight.transpose(1, 0, 2), head_weight.transpose(1, 0, 2), output_weight, cotangent[0]
        )
    )
    return (block_out[None], conv_grad.transpose(1, 0, 2), head_grad.transpose(1, 0, 2), output_grad)


def solution(mesh):
    placed = (
        P("dp", "seq", None),
        P("seq", None, "tensor"),
        P("seq", None, "tensor"),
        P("seq", "tensor"),
        P("dp", "seq", "tensor"),
    )
    return jax.shard_map(
        local,
        mesh=mesh,
        in_specs=placed,
        out_specs=(
            P("dp", "seq", "tensor"),
            P(("seq", "dp"), None, "tensor"),
            P(("seq", "dp"), None, "tensor"),
            P(("seq", "dp"), "tensor"),
        ),
        check_vma=False,
    )
```
